32 devices in a mesh: ax: 4 (over y, x), az: 8 (over z, core).
Axes of the slice: x: 2, y: 2, z: 4, core: 2. Of those that a mesh axis runs over, the one named last changes fastest.
Arguments:
- velocity: float32 [3, 64, 512, 512], P(None, 'ax', 'az'), may hold values from -6 to 6
- viscosity: float32 [64, 512, 512], P('ax', 'az'), may hold values from 0.5 to 4
- force: float32 [3, 8192, 512], P(None, ('ax', 'az')), may hold values from -6 to 6
- area: float32 [8192], P(('ax', 'az')), may hold values from 0.5 to 2
- adjacency: int32 [8192, 4], P(('ax', 'az')), may hold values from 0 to 8191, as said below
- crossing: int32 [8192, 1], P(('ax', 'az')), may hold values from 0 to 31; in each aligned block of 256 rows (0 to 255, 256 to 511, ...) at most 16 rows name the same one
- cell: int32 [8192], P(('ax', 'az')), may hold values from 0 to 1023
Outputs:
- updated: float32 [3, 64, 512, 512], P(None, 'ax', 'az')
The draws below stay inside these ranges and needn't reach their ends.
Inputs may be any that keep to these rules, and one draw needn't show every extreme that they name: adjacency[p, k] differs from p by at most 32; the first neighbour of a panel lies exactly 32 away unless the surface ends there. `crossing`: among the panels of one device no brick is crossed by more than 16 panels, a bound that some block reaches.
All inputs are finite; a program needn't handle non-finite values.
Results may differ from the reference program's by a relative error of at most 0.000062.
Values sent between devices are 32-bit elements; how exact they have to be, the bound alone decides.
A program may use at most 128 MiB of HBM per device.

```python
import math
import jax
import jax.numpy as jnp
import numpy as np

CA = 16
CT = 64
CR = 512
PAN_DEV = 256
HALO = 32
BRICKS = 32
CAP = 16
PANELS = 8192
NA = 64
NT = 512
N_AZ = 8


def draw_adjacency(key, part):
    first_key = jax.random.fold_in(key, 11)
    rest_key = jax.random.fold_in(key, 12)
    index = jnp.arange(PANELS, dtype=jnp.int32)[:, None]
    sign = jax.random.randint(first_key, (PANELS, 1), 0, 2).astype(jnp.int32) * 2 - 1
    first = index + sign * HALO
    rest = index + jax.random.randint(rest_key, (PANELS, 3), -HALO, HALO + 1).astype(jnp.int32)
    joined = jnp.concatenate([first, rest], axis=1)
    return jnp.clip(joined, 0, PANELS - 1).astype(jnp.int32)


def plant(values, own_key, low, high):
    longest = values.shape.index(max(values.shape))
    spots = []
    for shift in (0, 1):
        where = [jax.random.randint(jax.random.fold_in(own_key, axis), (), 0, length) for axis, length in enumerate(values.shape)]
        where[longest] = (where[longest] + shift) % values.shape[longest]
        spots.append(tuple(where))
    return values.at[spots[0]].set(low).at[spots[1]].set(high)


def block_levels(stream_key, dims, shards, least, high):
    level = 1.0
    for position, shards_of in shards:
        draws = jax.random.uniform(jax.random.fold_in(jax.random.fold_in(stream_key, 6), position), (shards_of,), jnp.float32, least / len(shards), high / len(shards))
        level = level * jnp.repeat(jnp.exp(draws), dims[position] // shards_of).reshape((-1,) + (1,) * (len(dims) - 1 - position))
    return level


def routed_block(stream_key, own, number, rows, number_of, top, most, skew):
    order = jax.random.permutation(stream_key, number_of)
    crowded, common = portions_of(number_of, rows * top, most, skew, True), portions_of(number_of, rows * top, most, skew, False)
    places = jnp.arange(number_of)

    def named(sizes, offset_by):
        used = int((sizes > 0).sum())
        fixed = max(1, used // 4)
        shifted = fixed + (places - fixed + offset_by * (used - fixed)) % max(1, number_of - fixed)
        return jnp.zeros((number_of,), jnp.int32).at[order[jnp.where(places < fixed, places, shifted)]].set(jnp.asarray(sizes, jnp.int32))

    sizes = jnp.where(number % 4 == 0, named(crowded, number // 4), named(common, number - number // 4 - 1))
    mixed = jax.random.permutation(jax.random.fold_in(own, 3), number_of)
    giver, taker = mixed[0:number_of // 2 * 2:2], mixed[1:number_of // 2 * 2:2]
    slack = jnp.minimum(sizes[giver] - 1, most - sizes[taker]) // 2
    slack = jnp.where((giver == order[0]) | (taker == order[0]) | (sizes[taker] == 0), 0, jnp.maximum(slack, 0))
    shifted = jax.random.randint(jax.random.fold_in(own, 4), (number_of // 2,), 0, 1 << 20) % (slack + 1)
    sizes = sizes.at[giver].add(-shifted).at[taker].add(shifted)
    members = jnp.searchsorted(jnp.cumsum(sizes), jnp.arange(rows * top), side="right").astype(jnp.int32)
    grid = members.reshape(top, rows).T
    grid = grid[jax.random.permutation(jax.random.fold_in(own, 1), rows)]
    offset_by = jax.random.randint(jax.random.fold_in(own, 2), (rows, 1), 0, top)
    return jnp.take_along_axis(grid, (jnp.arange(top)[None, :] + offset_by) % top, axis=1)


def portions_of(count, total, limit, lean, full):
    portions = [(1 << 20) // math.isqrt(rank ** lean) + 1 for rank in range(1, count + 1)]
    largest = limit if full else min(limit, max(-(-total // count), total * portions[0] // sum(portions)))
    least = 1 if total - largest >= count - 1 else 0
    given, surplus = [largest] + [least] * (count - 1), total - largest - least * (count - 1)
    while surplus > 0:
        candidates = [i for i in range(1, count) if given[i] < largest] or [i for i in range(1, count) if given[i] < limit]
        whole, budget = sum([portions[i] for i in candidates]), surplus
        for i in candidates:
            more = min(limit - given[i], max(1, budget * portions[i] // whole), surplus)
            given[i] = given[i] + more
            surplus = surplus - more
    return np.array(given)


def noise(own_key, dims, deviation, bound, split=(), kind=jnp.bfloat16):
    values = deviation * jax.random.normal(own_key, dims, jnp.float32)
    if split:
        values = values * block_levels(own_key, dims, split, -0.22, 0.18)
    return jnp.clip(values, -bound, bound).astype(kind)


def setup_inputs(seed: int = 0) -> dict:
    arg_keys = jax.random.split(jax.random.key(seed), 8)
    velocity = noise(arg_keys[0], (3, NA, NT, CR), 1.0, 6.0, ((1, 4), (2, 8)), jnp.float32)
    viscosity = jnp.clip(jnp.exp(math.log(4.0) - 2.0794415 * jax.random.uniform(arg_keys[1], (NA, NT, CR), jnp.float32) ** block_levels(arg_keys[1], (NA, NT, CR), ((0, 4), (1, 8)), -0.2, 0.2)), 0.5, 4.0)
    force = noise(arg_keys[2], (3, PANELS, CR), 1.0, 6.0, ((1, 32),), jnp.float32)
    area = jnp.clip(jnp.exp(math.log(2.0) - 1.3862944 * jax.random.uniform(arg_keys[3], (PANELS,), jnp.float32) ** block_levels(arg_keys[3], (PANELS,), ((0, 32),), -0.2, 0.2)), 0.5, 2.0)
    adjacency = draw_adjacency(jax.random.fold_in(arg_keys[7], 71), 0)
    crossing_keys = jax.random.split(jax.random.fold_in(arg_keys[5], 1), PANELS // PAN_DEV)
    crossing_turns = jax.random.permutation(jax.random.fold_in(arg_keys[5], 3), PANELS // PAN_DEV)
    crossing = jax.vmap(lambda own, number: routed_block(jax.random.fold_in(arg_keys[5], 2), own, number, PAN_DEV, BRICKS, 1, CAP, 2))(crossing_keys, crossing_turns).reshape((PANELS, 1))
    cell = plant(jax.random.randint(arg_keys[6], (PANELS,), 0, CA * CT), jax.random.fold_in(arg_keys[6], 1), 0, (CA * CT) - 1).astype(jnp.int32)
    return {"velocity": velocity, "viscosity": viscosity, "force": force, "area": area, "adjacency": adjacency, "crossing": crossing, "cell": cell}


step_size = 0.1
coupling = 0.2


def face_term(mu, mu_other, field, field_other):
    return 0.5 * (mu + mu_other)[None] * (field_other - field)


def viscous_sum(field, mu):
    fpad = jnp.pad(field, ((0, 0), (1, 1), (0, 0), (0, 0)))
    mpad = jnp.pad(mu, ((1, 1), (0, 0), (0, 0)))
    total = face_term(mu, mpad[2:], field, fpad[:, 2:])
    total = total + face_term(mu, mpad[:-2], field, fpad[:, :-2])
    total = total + face_term(mu, jnp.roll(mu, -1, axis=1), field, jnp.roll(field, -1, axis=2))
    total = total + face_term(mu, jnp.roll(mu, 1, axis=1), field, jnp.roll(field, 1, axis=2))
    fpad = jnp.pad(field, ((0, 0), (0, 0), (0, 0), (1, 1)))
    mpad = jnp.pad(mu, ((0, 0), (0, 0), (1, 1)))
    total = total + face_term(mu, mpad[:, :, 2:], field, fpad[:, :, :, 2:])
    total = total + face_term(mu, mpad[:, :, :-2], field, fpad[:, :, :, :-2])
    return total


def reference(velocity, viscosity, force, area, adjacency, crossing, cell):
    neighbours = jnp.take(force, adjacency, axis=1)
    jump = area[None, :, None] * (force + coupling * jnp.sum(neighbours - force[:, :, None, :], axis=2))
    dest = crossing[:, 0]
    brick_ax = dest // N_AZ
    brick_az = dest % N_AZ
    row = (brick_ax * CA + cell // CT) * NT + brick_az * CT + cell % CT
    tiles = jnp.transpose(jump, (1, 0, 2)).reshape(PANELS, 3 * CR)
    deposit = jax.ops.segment_sum(tiles, row.astype(jnp.int32), num_segments=NA * NT)
    deposit = jnp.transpose(deposit.reshape(NA, NT, 3, CR), (2, 0, 1, 3))
    viscous = viscous_sum(velocity, viscosity)
    return velocity + step_size * viscous + deposit
```

```python
import functools

import jax
import jax.numpy as jnp
from jax import lax
from jax.experimental import pallas as pl
from jax.experimental.pallas import tpu as pltpu
from jax.sharding import PartitionSpec as P

HALO = 32
LANES = 128

step_size = 0.1
coupling = 0.2


def split(x):
    hi = x.astype(jnp.bfloat16)
    lo = (x - hi.astype(jnp.float32)).astype(jnp.bfloat16)
    return hi, lo


def dot(a, b):
    return jnp.dot(a, b, preferred_element_type=jnp.float32)


def wide_row(cells, cap):
    m = cells.shape[0]
    slots = m * cap
    big = jnp.floor((cells + 1.0) * (1.0 / 64.0))
    small = (cells + 1.0) - 64.0 * big
    spread = (lax.broadcasted_iota(jnp.int32, (LANES, slots), 0)
              == lax.rem(lax.broadcasted_iota(jnp.int32, (LANES, slots), 1), cap))
    spread = spread.astype(jnp.float32).astype(jnp.bfloat16)
    wide = 64.0 * dot(big.astype(jnp.bfloat16), spread) + dot(small.astype(jnp.bfloat16), spread)
    mine = (lax.broadcasted_iota(jnp.int32, (m, slots), 0)
            == lax.broadcasted_iota(jnp.int32, (m, slots), 1) // cap)
    return jnp.sum(jnp.where(mine, wide, 0.0), axis=0, keepdims=True) - 1.0


def landing_of(crow, first, count):
    here = lax.broadcasted_iota(jnp.int32, (count, crow.shape[1]), 0) + first
    return (crow.astype(jnp.int32) == here).astype(jnp.float32).astype(jnp.bfloat16)


def exchange(n_ax, n_az, cap, vel, visc, force, dest_h, cell_h, area_h, adj_h, base, got, gcell,
             dest_i, cell_i, area, adj_i,
             velx, viscx, ext, exthi, extlo, send, scell, edges, edge_in, acc,
             tiles, tcell, thi, tlo,
             load_sem, halo_send, halo_recv, tile_send, tile_recv,
             cell_send, cell_recv, own_sem, out_sem):
    n, half_n = n_ax * n_az, n_az // 2
    ax, az = lax.axis_index("ax"), lax.axis_index("az")
    me = ax * n_az + az
    half, spot = az // half_n, lax.rem(az, half_n)
    ncomp, na, nt, nr = vel.shape
    pan = force.shape[1]
    slots = n * cap
    f32, bf16 = jnp.float32, jnp.bfloat16

    def place(linear):
        return (linear // n_az, lax.rem(linear, n_az))

    def remote(src, dst, ssem, rsem, device):
        return pltpu.make_async_remote_copy(
            src_ref=src, dst_ref=dst, send_sem=ssem, recv_sem=rsem,
            device_id=device, device_id_type=pl.DeviceIdType.MESH)

    barrier = pltpu.get_barrier_semaphore()

    def greet(k, carry):
        pl.semaphore_signal(barrier, inc=1, device_id=place(lax.rem(me + k, n)),
                            device_id_type=pl.DeviceIdType.MESH)
        return carry

    lax.fori_loop(1, n, greet, 0)
    small = [pltpu.make_async_copy(src, dst, load_sem.at[3 + k]) for k, (src, dst) in enumerate(
        [(dest_h, dest_i), (cell_h, cell_i), (adj_h, adj_i), (area_h, area)])]
    loads = [
        pltpu.make_async_copy(force, ext.at[:, pl.ds(HALO, pan)], load_sem.at[0]),
        pltpu.make_async_copy(vel, velx.at[:, pl.ds(1, na)], load_sem.at[1]),
        pltpu.make_async_copy(visc, viscx.at[pl.ds(1, na)], load_sem.at[2]),
    ]
    for c in small + loads:
        c.start()

    pl.semaphore_wait(barrier, n - 1)

    up, down = place(lax.rem(me + 1, n)), place(lax.rem(me + n - 1, n))
    ax_up, ax_down = lax.rem(ax + 1, n_ax), lax.rem(ax + n_ax - 1, n_ax)
    az_up, az_down = lax.rem(az + 1, n_az), lax.rem(az + n_az - 1, n_az)

    def halo(i, src, dst, device):
        return remote(src, dst, halo_send.at[i], halo_recv.at[i], device)

    fhalo = [
        halo(0, force.at[:, pl.ds(pan - HALO, HALO)], ext.at[:, pl.ds(0, HALO)], up),
        halo(1, force.at[:, pl.ds(0, HALO)], ext.at[:, pl.ds(HALO + pan, HALO)], down),
    ]
    ahalo = [
        halo(2, vel.at[:, na - 1], velx.at[:, 0], (ax_up, az)),
        halo(3, vel.at[:, 0], velx.at[:, na + 1], (ax_down, az)),
        halo(4, visc.at[na - 1], viscx.at[0], (ax_up, az)),
        halo(5, visc.at[0], viscx.at[na + 1], (ax_down, az)),
    ]
    zhalo = [
        halo(6, edges.at[1], edge_in.at[0], (ax, az_up)),
        halo(7, edges.at[0], edge_in.at[1], (ax, az_down)),
    ]
    for c in fhalo:
        c.start()
    for c in small:
        c.wait()

    dest_row, cell_row = dest_i[...].astype(f32), cell_i[...].astype(f32)
    adj = (adj_i[...] - (me * pan - HALO)).astype(f32)
    rows = jnp.concatenate([dest_row, cell_row, adj, dest_row, dest_row], axis=0)
    cols = rows.T
    dest_col, cell_col = cols[:, 0:1], cols[:, 1:2]
    same = dest_col == dest_row
    r0 = lax.broadcasted_iota(jnp.int32, (pan, pan), 0)
    r1 = lax.broadcasted_iota(jnp.int32, (pan, pan), 1)
    rank_row = jnp.sum((same & (r0 < r1)).astype(f32), axis=0, keepdims=True)
    rank_col = jnp.sum((same & (r1 < r0)).astype(f32), axis=1, keepdims=True)
    dax = jnp.floor(dest_row * (1.0 / n_az))
    daz = dest_row - n_az * dax
    dhalf = jnp.floor(daz * (1.0 / half_n))
    turn = dax - ax.astype(f32)
    turn = jnp.where(turn < 0.0, turn + n_ax, turn)
    group = turn + jnp.where(dhalf == half.astype(f32), 0.0, float(n_ax))
    peer = group * half_n + (daz - half_n * dhalf)
    target = (peer * cap + rank_row).astype(jnp.int32)
    hits = lax.broadcasted_iota(jnp.int32, (slots, pan), 0) == target
    scale = jnp.sum(jnp.where(hits, coupling * area[...], 0.0), axis=1, keepdims=True)
    q = lax.broadcasted_iota(jnp.int32, (pan, pan + 2 * HALO), 1).astype(f32)
    p = lax.broadcasted_iota(jnp.int32, (pan, pan + 2 * HALO), 0).astype(f32)
    count = (q == p + HALO).astype(f32)
    for k in range(4):
        count = count + (q == cols[:, 2 + k:3 + k]).astype(f32)
    pick = dot(hits.astype(f32).astype(bf16), count.astype(bf16)).astype(bf16)

    loads[1].wait()
    loads[2].wait()
    for c in range(ncomp):
        edges[0, c] = velx[c, 1:na + 1, 0, :]
        edges[1, c] = velx[c, 1:na + 1, nt - 1, :]
    edges[0, ncomp] = viscx[1:na + 1, 0, :]
    edges[1, ncomp] = viscx[1:na + 1, nt - 1, :]

    for c in zhalo + ahalo:
        c.start()

    big = jnp.floor((cell_col + 1.0) * (1.0 / 64.0))
    small = (cell_col + 1.0) - 64.0 * big
    at_rank = lax.broadcasted_iota(jnp.int32, (pan, LANES), 1).astype(f32) == rank_col
    owner = lax.broadcasted_iota(jnp.int32, (n, pan), 0).astype(f32) == peer
    owner = owner.astype(f32).astype(bf16)
    cells = (64.0 * dot(owner, jnp.where(at_rank, big, 0.0).astype(bf16))
             + dot(owner, jnp.where(at_rank, small, 0.0).astype(bf16)) - 1.0)
    for d in range(n):
        scell[d] = cells[d:d + 1, :]

    def split_force(lo_row, hi_row):
        h, l = split(ext[:, lo_row:hi_row])
        exthi[:, lo_row:hi_row] = h
        extlo[:, lo_row:hi_row] = l

    loads[0].wait()
    split_force(HALO, HALO + pan)
    for c in fhalo:
        c.wait()
    split_force(0, HALO)
    split_force(HALO + pan, pan + 2 * HALO)

    def tiles_to(g, i):
        there = lax.rem(spot + i, half_n)
        side = half if g < n_ax else 1 - half
        device = (lax.rem(ax + g % n_ax, n_ax), side * half_n + there)
        src, k = g * half_n + there, g * half_n + i
        at = (g % n_ax) * half_n + spot
        tile_at, cell_at = (tiles, tcell) if g < n_ax else (got, gcell)
        return (remote(send.at[src], tile_at.at[at], tile_send.at[k], tile_recv.at[k], device),
                remote(scell.at[src], cell_at.at[at], cell_send.at[k], cell_recv.at[k], device))

    def each_tile(groups, act):
        for g in groups:
            def body(i, carry):
                for c in tiles_to(g, i):
                    act(c)
                return carry
            lax.fori_loop(1 if g == 0 else 0, half_n, body, 0)

    for part in range(2):
        r = slice(part * (slots // 2), (part + 1) * (slots // 2))
        for c in range(ncomp):
            tile = (dot(pick[r], exthi[c]) + dot(pick[r], extlo[c])) * scale[r]
            send[part * (n // 2):(part + 1) * (n // 2), :, c * nr:(c + 1) * nr] = (
                tile.reshape(n // 2, cap, nr))
        each_tile(range(part * n_ax, (part + 1) * n_ax), lambda c: c.start())
    own = [pltpu.make_async_copy(send.at[spot], tiles.at[spot], own_sem.at[0]),
           pltpu.make_async_copy(scell.at[spot], tcell.at[spot], own_sem.at[1])]
    for c in own:
        c.start()

    for c in ahalo + zhalo:
        c.wait()

    @pl.when(ax == 0)
    def _():
        velx[:, 0] = jnp.zeros((ncomp, nt, nr), f32)
        viscx[0] = jnp.zeros((nt, nr), f32)

    @pl.when(ax == n_ax - 1)
    def _():
        velx[:, na + 1] = jnp.zeros((ncomp, nt, nr), f32)
        viscx[na + 1] = jnp.zeros((nt, nr), f32)

    row_id = lax.broadcasted_iota(jnp.int32, (nt, nr), 0)
    lane_id = lax.broadcasted_iota(jnp.int32, (nt, nr), 1)

    def neighbours(x, low, high):
        left = jnp.where(row_id == 0, low, pltpu.roll(x, 1, 0))
        right = jnp.where(row_id == nt - 1, high, pltpu.roll(x, nt - 1, 0))
        inner = jnp.where(lane_id == 0, 0.0, pltpu.roll(x, 1, 1))
        outer = jnp.where(lane_id == nr - 1, 0.0, pltpu.roll(x, nr - 1, 1))
        return left, right, inner, outer

    def plane(i, carry):
        mu = viscx[i + 1]
        sides = neighbours(mu, edge_in[0, ncomp, pl.ds(i, 1), :], edge_in[1, ncomp, pl.ds(i, 1), :])
        faces = [mu + s for s in (viscx[i], viscx[i + 2]) + sides]
        for c in range(ncomp):
            f = velx[c, i + 1]
            near = neighbours(f, edge_in[0, c, pl.ds(i, 1), :], edge_in[1, c, pl.ds(i, 1), :])
            near = (velx[c, i], velx[c, i + 2]) + near
            total = faces[0] * (near[0] - f)
            for w, g in zip(faces[1:], near[1:]):
                total = total + w * (g - f)
            acc[c, i] = f + (0.5 * step_size) * total
        return carry

    lax.fori_loop(0, na, plane, 0)

    for c in own:
        c.wait()
    each_tile(range(n_ax), lambda c: c.wait())
    h, l = split(tiles[...].reshape(-1, ncomp * nr))
    thi[...] = h
    tlo[...] = l
    crow = wide_row(tcell[...].reshape(-1, LANES), cap)
    blk = max(1, 256 // nt)

    def stored(j):
        return pltpu.make_async_copy(acc.at[:, pl.ds(j * blk, blk)],
                                     base.at[:, pl.ds(j * blk, blk)], out_sem.at[j])

    for j in range(na // blk):
        landing = landing_of(crow, j * blk * nt, blk * nt)
        for c in range(ncomp):
            cs = slice(c * nr, (c + 1) * nr)
            deposit = dot(landing, thi[:, cs]) + dot(landing, tlo[:, cs])
            acc[c, j * blk:(j + 1) * blk] += deposit.reshape(blk, nt, nr)
        stored(j).start()
    for j in range(na // blk):
        stored(j).wait()
    each_tile(range(n_ax, 2 * n_ax), lambda c: c.wait())


def settle(cap, base, got, gcell, out, hi, lo, crow):
    step = pl.program_id(0)
    ncomp, blk, nt, nr = out.shape

    @pl.when(step == 0)
    def _():
        crow[...] = wide_row(gcell[...].reshape(-1, LANES), cap)
        h, l = split(got[...])
        hi[...] = h
        lo[...] = l

    landing = landing_of(crow[...], step * (blk * nt), blk * nt)
    for c in range(ncomp):
        cs = slice(c * nr, (c + 1) * nr)
        deposit = dot(landing, hi[:, cs]) + dot(landing, lo[:, cs])
        out[c] = base[c, pl.ds(step * blk, blk)] + deposit.reshape(blk, nt, nr)


def on_device(n_ax, n_az, velocity, viscosity, force, area, adjacency, crossing, cell):
    n = n_ax * n_az
    ncomp, pan, nr = force.shape
    na, nt = velocity.shape[1:3]
    cap = max(2, 2 * pan // n)
    cap = -(-cap // 8) * 8
    slots = n * cap
    late = n // 2
    soon = n - late
    f32, bf16 = jnp.float32, jnp.bfloat16
    any_ = pl.BlockSpec(memory_space=pl.ANY)
    hbm = pl.BlockSpec(memory_space=pltpu.HBM)
    vmem = pl.BlockSpec(memory_space=pltpu.VMEM)
    dma = pltpu.SemaphoreType.DMA
    i32 = jnp.int32
    inputs = (velocity, viscosity, force, crossing.reshape(1, pan), cell.reshape(1, pan),
              area.reshape(1, pan), adjacency.T)
    inputs = [pltpu.with_memory_space_constraint(x, pltpu.HBM) for x in inputs]
    base, got, gcell = pl.pallas_call(
        functools.partial(exchange, n_ax, n_az, cap),
        out_shape=(jax.ShapeDtypeStruct(velocity.shape, f32),
                   jax.ShapeDtypeStruct((late, cap, ncomp * nr), f32),
                   jax.ShapeDtypeStruct((late, 1, LANES), f32)),
        in_specs=[hbm] * 7,
        out_specs=(any_, any_, any_),
        scratch_shapes=[
            pltpu.VMEM((1, pan), i32), pltpu.VMEM((1, pan), i32),
            pltpu.VMEM((1, pan), f32), pltpu.VMEM((4, pan), i32),
            pltpu.VMEM((ncomp, na + 2, nt, nr), f32),
            pltpu.VMEM((na + 2, nt, nr), f32),
            pltpu.VMEM((ncomp, pan + 2 * HALO, nr), f32),
            pltpu.VMEM((ncomp, pan + 2 * HALO, nr), bf16),
            pltpu.VMEM((ncomp, pan + 2 * HALO, nr), bf16),
            pltpu.VMEM((n, cap, ncomp * nr), f32),
            pltpu.VMEM((n, 1, LANES), f32),
            pltpu.VMEM((2, ncomp + 1, na, nr), f32),
            pltpu.VMEM((2, ncomp + 1, na, nr), f32),
            pltpu.VMEM((ncomp, na, nt, nr), f32),
            pltpu.VMEM((soon, cap, ncomp * nr), f32),
            pltpu.VMEM((soon, 1, LANES), f32),
            pltpu.VMEM((soon * cap, ncomp * nr), bf16),
            pltpu.VMEM((soon * cap, ncomp * nr), bf16),
            dma((7,)), dma((8,)), dma((8,)), dma((n,)), dma((n,)), dma((n,)), dma((n,)),
            dma((2,)), dma((na,)),
        ],
        compiler_params=pltpu.CompilerParams(collective_id=0, has_side_effects=True,
                                             vmem_limit_bytes=40 << 20),
        name="exchange",
    )(*inputs)
    blk = max(1, 128 // nt)
    window = pl.BlockSpec((ncomp, blk, nt, nr), lambda s: (0, s, 0, 0))
    return pl.pallas_call(
        functools.partial(settle, cap),
        out_shape=jax.ShapeDtypeStruct(velocity.shape, f32),
        grid=(na // blk,),
        in_specs=[vmem,
                  pl.BlockSpec((late * cap, ncomp * nr), lambda s: (0, 0)),
                  pl.BlockSpec((late, 1, LANES), lambda s: (0, 0, 0))],
        out_specs=window,
        scratch_shapes=[pltpu.VMEM((late * cap, ncomp * nr), bf16),
                        pltpu.VMEM((late * cap, ncomp * nr), bf16),
                        pltpu.VMEM((1, late * cap), f32)],
        compiler_params=pltpu.CompilerParams(vmem_limit_bytes=24 << 20),
        name="settle",
    )(base, got.reshape(late * cap, ncomp * nr), gcell)


def solution(mesh):
    n_ax, n_az = mesh.shape["ax"], mesh.shape["az"]
    in_specs = (
        P(None, "ax", "az", None),
        P("ax", "az", None),
        P(None, ("ax", "az"), None),
        P(("ax", "az")),
        P(("ax", "az"), None),
        P(("ax", "az"), None),
        P(("ax", "az")),
    )
    return jax.shard_map(
        functools.partial(on_device, n_ax, n_az), mesh=mesh, in_specs=in_specs,
        out_specs=P(None, "ax", "az", None), check_vma=False)
```

```python
import functools

import jax
import jax.numpy as jnp
from jax import lax
from jax.experimental import pallas as pl
from jax.experimental.pallas import tpu as pltpu
from jax.sharding import PartitionSpec as P

HALO = 32
LANES = 128

step_size = 0.1
coupling = 0.2


def split(x):
    hi = x.astype(jnp.bfloat16)
    lo = (x - hi.astype(jnp.float32)).astype(jnp.bfloat16)
    return hi, lo


def dot(a, b):
    return jnp.dot(a, b, preferred_element_type=jnp.float32)


def wide_row(cells, cap):
    m = cells.shape[0]
    slots = m * cap
    big = jnp.floor((cells + 1.0) * (1.0 / 64.0))
    small = (cells + 1.0) - 64.0 * big
    spread = (lax.broadcasted_iota(jnp.int32, (LANES, slots), 0)
              == lax.rem(lax.broadcasted_iota(jnp.int32, (LANES, slots), 1), cap))
    spread = spread.astype(jnp.float32).astype(jnp.bfloat16)
    wide = 64.0 * dot(big.astype(jnp.bfloat16), spread) + dot(small.astype(jnp.bfloat16), spread)
    mine = (lax.broadcasted_iota(jnp.int32, (m, slots), 0)
            == lax.broadcasted_iota(jnp.int32, (m, slots), 1) // cap)
    return jnp.sum(jnp.where(mine, wide, 0.0), axis=0, keepdims=True) - 1.0


def landing_of(crow, first, count):
    here = lax.broadcasted_iota(jnp.int32, (count, crow.shape[1]), 0) + first
    return (crow.astype(jnp.int32) == here).astype(jnp.float32).astype(jnp.bfloat16)


def exchange(n_ax, n_az, cap, vel, visc, force, dest_h, cell_h, area_h, adj_h, base, got, gcell,
             dest_i, cell_i, area, adj_i,
             velx, viscx, ext, exthi, extlo, send, scell, edges, edge_in, acc,
             tiles, tcell, thi, tlo,
             load_sem, halo_send, halo_recv, tile_send, tile_recv,
             cell_send, cell_recv, own_sem, out_sem):
    n, half_n = n_ax * n_az, n_az // 2
    ax, az = lax.axis_index("ax"), lax.axis_index("az")
    me = ax * n_az + az
    half, spot = az // half_n, lax.rem(az, half_n)
    ncomp, na, nt, nr = vel.shape
    pan = force.shape[1]
    slots = n * cap
    f32, bf16 = jnp.float32, jnp.bfloat16

    def place(linear):
        return (linear // n_az, lax.rem(linear, n_az))

    def remote(src, dst, ssem, rsem, device):
        return pltpu.make_async_remote_copy(
            src_ref=src, dst_ref=dst, send_sem=ssem, recv_sem=rsem,
            device_id=device, device_id_type=pl.DeviceIdType.MESH)

    barrier = pltpu.get_barrier_semaphore()

    def greet(k, carry):
        pl.semaphore_signal(barrier, inc=1, device_id=place(lax.rem(me + k, n)),
                            device_id_type=pl.DeviceIdType.MESH)
        return carry

    lax.fori_loop(1, n, greet, 0)
    small = [pltpu.make_async_copy(src, dst, load_sem.at[3 + k]) for k, (src, dst) in enumerate(
        [(dest_h, dest_i), (cell_h, cell_i), (adj_h, adj_i), (area_h, area)])]
    loads = [
        pltpu.make_async_copy(force, ext.at[:, pl.ds(HALO, pan)], load_sem.at[0]),
        pltpu.make_async_copy(vel, velx.at[:, pl.ds(1, na)], load_sem.at[1]),
        pltpu.make_async_copy(visc, viscx.at[pl.ds(1, na)], load_sem.at[2]),
    ]
    for c in small + loads:
        c.start()

    pl.semaphore_wait(barrier, n - 1)

    up, down = place(lax.rem(me + 1, n)), place(lax.rem(me + n - 1, n))
    ax_up, ax_down = lax.rem(ax + 1, n_ax), lax.rem(ax + n_ax - 1, n_ax)
    az_up, az_down = lax.rem(az + 1, n_az), lax.rem(az + n_az - 1, n_az)

    def halo(i, src, dst, device):
        return remote(src, dst, halo_send.at[i], halo_recv.at[i], device)

    fhalo = [
        halo(0, force.at[:, pl.ds(pan - HALO, HALO)], ext.at[:, pl.ds(0, HALO)], up),
        halo(1, force.at[:, pl.ds(0, HALO)], ext.at[:, pl.ds(HALO + pan, HALO)], down),
    ]
    ahalo = [
        halo(2, vel.at[:, na - 1], velx.at[:, 0], (ax_up, az)),
        halo(3, vel.at[:, 0], velx.at[:, na + 1], (ax_down, az)),
        halo(4, visc.at[na - 1], viscx.at[0], (ax_up, az)),
        halo(5, visc.at[0], viscx.at[na + 1], (ax_down, az)),
    ]
    zhalo = [
        halo(6, edges.at[1], edge_in.at[0], (ax, az_up)),
        halo(7, edges.at[0], edge_in.at[1], (ax, az_down)),
    ]
    for c in fhalo:
        c.start()
    for c in small:
        c.wait()

    dest_row, cell_row = dest_i[...].astype(f32), cell_i[...].astype(f32)
    adj = (adj_i[...] - (me * pan - HALO)).astype(f32)
    rows = jnp.concatenate([dest_row, cell_row, adj, dest_row, dest_row], axis=0)
    cols = rows.T
    dest_col, cell_col = cols[:, 0:1], cols[:, 1:2]
    same = dest_col == dest_row
    r0 = lax.broadcasted_iota(jnp.int32, (pan, pan), 0)
    r1 = lax.broadcasted_iota(jnp.int32, (pan, pan), 1)
    rank_row = jnp.sum((same & (r0 < r1)).astype(f32), axis=0, keepdims=True)
    rank_col = jnp.sum((same & (r1 < r0)).astype(f32), axis=1, keepdims=True)
    dax = jnp.floor(dest_row * (1.0 / n_az))
    daz = dest_row - n_az * dax
    dhalf = jnp.floor(daz * (1.0 / half_n))
    turn = dax - ax.astype(f32)
    turn = jnp.where(turn < 0.0, turn + n_ax, turn)
    group = turn + jnp.where(dhalf == half.astype(f32), 0.0, float(n_ax))
    peer = group * half_n + (daz - half_n * dhalf)
    target = (peer * cap + rank_row).astype(jnp.int32)
    hits = lax.broadcasted_iota(jnp.int32, (slots, pan), 0) == target
    scale = jnp.sum(jnp.where(hits, coupling * area[...], 0.0), axis=1, keepdims=True)
    q = lax.broadcasted_iota(jnp.int32, (pan, pan + 2 * HALO), 1).astype(f32)
    p = lax.broadcasted_iota(jnp.int32, (pan, pan + 2 * HALO), 0).astype(f32)
    count = (q == p + HALO).astype(f32)
    for k in range(4):
        count = count + (q == cols[:, 2 + k:3 + k]).astype(f32)
    pick = dot(hits.astype(f32).astype(bf16), count.astype(bf16)).astype(bf16)

    loads[1].wait()
    loads[2].wait()
    for c in range(ncomp):
        edges[0, c] = velx[c, 1:na + 1, 0, :]
        edges[1, c] = velx[c, 1:na + 1, nt - 1, :]
    edges[0, ncomp] = viscx[1:na + 1, 0, :]
    edges[1, ncomp] = viscx[1:na + 1, nt - 1, :]

    for c in zhalo + ahalo:
        c.start()

    big = jnp.floor((cell_col + 1.0) * (1.0 / 64.0))
    small = (cell_col + 1.0) - 64.0 * big
    at_rank = lax.broadcasted_iota(jnp.int32, (pan, LANES), 1).astype(f32) == rank_col
    owner = lax.broadcasted_iota(jnp.int32, (n, pan), 0).astype(f32) == peer
    owner = owner.astype(f32).astype(bf16)
    cells = (64.0 * dot(owner, jnp.where(at_rank, big, 0.0).astype(bf16))
             + dot(owner, jnp.where(at_rank, small, 0.0).astype(bf16)) - 1.0)
    for d in range(n):
        scell[d] = cells[d:d + 1, :]

    def split_force(lo_row, hi_row):
        h, l = split(ext[:, lo_row:hi_row])
        exthi[:, lo_row:hi_row] = h
        extlo[:, lo_row:hi_row] = l

    loads[0].wait()
    split_force(HALO, HALO + pan)
    for c in fhalo:
        c.wait()
    split_force(0, HALO)
    split_force(HALO + pan, pan + 2 * HALO)

    def tiles_to(g, i):
        there = lax.rem(spot + i, half_n)
        side = half if g < n_ax else 1 - half
        device = (lax.rem(ax + g % n_ax, n_ax), side * half_n + there)
        src, k = g * half_n + there, g * half_n + i
        at = (g % n_ax) * half_n + spot
        tile_at, cell_at = (tiles, tcell) if g < n_ax else (got, gcell)
        return (remote(send.at[src], tile_at.at[at], tile_send.at[k], tile_recv.at[k], device),
                remote(scell.at[src], cell_at.at[at], cell_send.at[k], cell_recv.at[k], device))

    def each_tile(groups, act):
        for g in groups:
            def body(i, carry):
                for c in tiles_to(g, i):
                    act(c)
                return carry
            lax.fori_loop(1 if g == 0 else 0, half_n, body, 0)

    for part in range(2):
        r = slice(part * (slots // 2), (part + 1) * (slots // 2))
        for c in range(ncomp):
            tile = (dot(pick[r], exthi[c]) + dot(pick[r], extlo[c])) * scale[r]
            send[part * (n // 2):(part + 1) * (n // 2), :, c * nr:(c + 1) * nr] = (
                tile.reshape(n // 2, cap, nr))
        each_tile(range(part * n_ax, (part + 1) * n_ax), lambda c: c.start())
    own = [pltpu.make_async_copy(send.at[spot], tiles.at[spot], own_sem.at[0]),
           pltpu.make_async_copy(scell.at[spot], tcell.at[spot], own_sem.at[1])]
    for c in own:
        c.start()

    for c in ahalo + zhalo:
        c.wait()

    @pl.when(ax == 0)
    def _():
        velx[:, 0] = jnp.zeros((ncomp, nt, nr), f32)
        viscx[0] = jnp.zeros((nt, nr), f32)

    @pl.when(ax == n_ax - 1)
    def _():
        velx[:, na + 1] = jnp.zeros((ncomp, nt, nr), f32)
        viscx[na + 1] = jnp.zeros((nt, nr), f32)

    row_id = lax.broadcasted_iota(jnp.int32, (nt, nr), 0)
    lane_id = lax.broadcasted_iota(jnp.int32, (nt, nr), 1)

    def neighbours(x, low, high):
        left = jnp.where(row_id == 0, low, pltpu.roll(x, 1, 0))
        right = jnp.where(row_id == nt - 1, high, pltpu.roll(x, nt - 1, 0))
        inner = jnp.where(lane_id == 0, 0.0, pltpu.roll(x, 1, 1))
        outer = jnp.where(lane_id == nr - 1, 0.0, pltpu.roll(x, nr - 1, 1))
        return left, right, inner, outer

    def plane(i, carry):
        mu = viscx[i + 1]
        sides = neighbours(mu, edge_in[0, ncomp, pl.ds(i, 1), :], edge_in[1, ncomp, pl.ds(i, 1), :])
        faces = [mu + s for s in (viscx[i], viscx[i + 2]) + sides]
        for c in range(ncomp):
            f = velx[c, i + 1]
            near = neighbours(f, edge_in[0, c, pl.ds(i, 1), :], edge_in[1, c, pl.ds(i, 1), :])
            near = (velx[c, i], velx[c, i + 2]) + near
            total = faces[0] * (near[0] - f)
            for w, g in zip(faces[1:], near[1:]):
                total = total + w * (g - f)
            acc[c, i] = f + (0.5 * step_size) * total
        return carry

    lax.fori_loop(0, na, plane, 0)

    for c in own:
        c.wait()
    each_tile(range(n_ax), lambda c: c.wait())
    h, l = split(tiles[...].reshape(-1, ncomp * nr))
    thi[...] = h
    tlo[...] = l
    crow = wide_row(tcell[...].reshape(-1, LANES), cap)
    blk = max(1, 256 // nt)

    def stored(j):
        return pltpu.make_async_copy(acc.at[:, pl.ds(j * blk, blk)],
                                     base.at[:, pl.ds(j * blk, blk)], out_sem.at[j])

    for j in range(na // blk):
        landing = landing_of(crow, j * blk * nt, blk * nt)
        for c in range(ncomp):
            cs = slice(c * nr, (c + 1) * nr)
            deposit = dot(landing, thi[:, cs]) + dot(landing, tlo[:, cs])
            acc[c, j * blk:(j + 1) * blk] += deposit.reshape(blk, nt, nr)
        stored(j).start()
    for j in range(na // blk):
        stored(j).wait()
    each_tile(range(n_ax, 2 * n_ax), lambda c: c.wait())


def exchange_packed(n_ax, n_az, cap, keep, vel, visc, force, dest_h, cell_h, area_h, adj_h,
                    base, got, landing, flag,
                    dest_i, cell_i, area, adj_i,
                    velx, viscx, ext, exthi, extlo, send, scell, edges, edge_in, acc,
                    tiles, tcell, fcell, thi, tlo, pack, packed, smeta, rmeta, sorted_, near_at,
                    load_sem, halo_send, halo_recv, tile_send, tile_recv,
                    cell_send, cell_recv, own_sem, out_sem,
                    pack_send, pack_recv, meta_send, meta_recv, hop_send, hop_recv, hop_own):
    n, half_n = n_ax * n_az, n_az // 2
    depth, group_n = half_n // 2, 2 * n_ax
    ax, az = lax.axis_index("ax"), lax.axis_index("az")
    me = ax * n_az + az
    half, spot = az // half_n, lax.rem(az, half_n)
    zpos, core = spot // 2, lax.rem(az, 2)
    seat = ax * 2 + core
    ncomp, na, nt, nr = vel.shape
    pan = force.shape[1]
    near = (n // 2) * cap
    slots = near + depth * keep
    f32, bf16 = jnp.float32, jnp.bfloat16

    def place(linear):
        return (linear // n_az, lax.rem(linear, n_az))

    def remote(src, dst, ssem, rsem, device):
        return pltpu.make_async_remote_copy(
            src_ref=src, dst_ref=dst, send_sem=ssem, recv_sem=rsem,
            device_id=device, device_id_type=pl.DeviceIdType.MESH)

    barrier = pltpu.get_barrier_semaphore()

    def greet(k, carry):
        pl.semaphore_signal(barrier, inc=1, device_id=place(lax.rem(me + k, n)),
                            device_id_type=pl.DeviceIdType.MESH)
        return carry

    lax.fori_loop(1, n, greet, 0)
    small = [pltpu.make_async_copy(src, dst, load_sem.at[3 + k]) for k, (src, dst) in enumerate(
        [(dest_h, dest_i), (cell_h, cell_i), (adj_h, adj_i), (area_h, area)])]
    loads = [
        pltpu.make_async_copy(force, ext.at[:, pl.ds(HALO, pan)], load_sem.at[0]),
        pltpu.make_async_copy(vel, velx.at[:, pl.ds(1, na)], load_sem.at[1]),
        pltpu.make_async_copy(visc, viscx.at[pl.ds(1, na)], load_sem.at[2]),
    ]
    for c in small + loads:
        c.start()

    pl.semaphore_wait(barrier, n - 1)

    up, down = place(lax.rem(me + 1, n)), place(lax.rem(me + n - 1, n))
    ax_up, ax_down = lax.rem(ax + 1, n_ax), lax.rem(ax + n_ax - 1, n_ax)
    az_up, az_down = lax.rem(az + 1, n_az), lax.rem(az + n_az - 1, n_az)

    def halo(i, src, dst, device):
        return remote(src, dst, halo_send.at[i], halo_recv.at[i], device)

    fhalo = [
        halo(0, force.at[:, pl.ds(pan - HALO, HALO)], ext.at[:, pl.ds(0, HALO)], up),
        halo(1, force.at[:, pl.ds(0, HALO)], ext.at[:, pl.ds(HALO + pan, HALO)], down),
    ]
    ahalo = [
        halo(2, vel.at[:, na - 1], velx.at[:, 0], (ax_up, az)),
        halo(3, vel.at[:, 0], velx.at[:, na + 1], (ax_down, az)),
        halo(4, visc.at[na - 1], viscx.at[0], (ax_up, az)),
        halo(5, visc.at[0], viscx.at[na + 1], (ax_down, az)),
    ]
    zhalo = [
        halo(6, edges.at[1], edge_in.at[0], (ax, az_up)),
        halo(7, edges.at[0], edge_in.at[1], (ax, az_down)),
    ]
    for c in fhalo + ahalo:
        c.start()
    for c in small:
        c.wait()

    dest_row, cell_row = dest_i[...].astype(f32), cell_i[...].astype(f32)
    adj = (adj_i[...] - (me * pan - HALO)).astype(f32)
    rows = jnp.concatenate([dest_row, cell_row, adj, dest_row, dest_row], axis=0)
    cols = rows.T
    dest_col, cell_col = cols[:, 0:1], cols[:, 1:2]
    same = dest_col == dest_row
    r0 = lax.broadcasted_iota(jnp.int32, (pan, pan), 0)
    r1 = lax.broadcasted_iota(jnp.int32, (pan, pan), 1)
    rank_row = jnp.sum((same & (r0 < r1)).astype(f32), axis=0, keepdims=True)
    rank_col = jnp.sum((same & (r1 < r0)).astype(f32), axis=1, keepdims=True)

    def layer_of(dest):
        inner = dest - n_az * jnp.floor(dest * (1.0 / n_az))
        return jnp.floor(inner * 0.5)

    dax = jnp.floor(dest_row * (1.0 / n_az))
    daz = dest_row - n_az * dax
    dhalf = jnp.floor(daz * (1.0 / half_n))
    layer_row, layer_col = layer_of(dest_row), layer_of(dest_col)
    pos_row = jnp.sum(((layer_col == layer_row) & (r0 < r1)).astype(f32), axis=0, keepdims=True)
    turn = dax - ax.astype(f32)
    turn = jnp.where(turn < 0.0, turn + n_ax, turn)
    far = dhalf != half.astype(f32)
    group = turn + jnp.where(far, float(n_ax), 0.0)
    peer = group * half_n + (daz - half_n * dhalf)
    dz = (layer_row - depth * dhalf) - zpos.astype(f32)
    dz = jnp.where(dz < 0.0, dz + depth, dz)
    spilled = far & (pos_row >= keep)
    target = jnp.where(far, near + dz * keep + pos_row, peer * cap + rank_row)
    target = jnp.where(spilled, -1.0, target).astype(jnp.int32)
    spill = jnp.max(jnp.where(spilled, 1.0, 0.0), axis=1, keepdims=True)
    hits = lax.broadcasted_iota(jnp.int32, (slots, pan), 0) == target
    scale = jnp.sum(jnp.where(hits, coupling * area[...], 0.0), axis=1, keepdims=True)
    q = lax.broadcasted_iota(jnp.int32, (pan, pan + 2 * HALO), 1).astype(f32)
    p = lax.broadcasted_iota(jnp.int32, (pan, pan + 2 * HALO), 0).astype(f32)
    count = (q == p + HALO).astype(f32)
    for k in range(4):
        count = count + (q == cols[:, 2 + k:3 + k]).astype(f32)
    hits = hits.astype(f32).astype(bf16)
    pick = dot(hits, count.astype(bf16)).astype(bf16)
    slot = (dax * 2.0 + (daz - 2.0 * layer_row)) * cap + rank_row + 1.0
    sbig = jnp.floor(slot * (1.0 / 64.0))
    digits = jnp.concatenate([sbig, slot - 64.0 * sbig] * 4, axis=0).astype(bf16)
    for j in range(depth):
        at = near + j * keep
        found = lax.dot_general(digits, hits[at:at + keep], (((1,), (1,)), ((), ())),
                                preferred_element_type=f32)
        smeta[j] = jnp.full((1, LANES), -1.0, f32)
        smeta[j, :, 0:keep] = 64.0 * found[0:1] + found[1:2] - 1.0

    loads[1].wait()
    loads[2].wait()
    for c in range(ncomp):
        edges[0, c] = velx[c, 1:na + 1, 0, :]
        edges[1, c] = velx[c, 1:na + 1, nt - 1, :]
    edges[0, ncomp] = viscx[1:na + 1, 0, :]
    edges[1, ncomp] = viscx[1:na + 1, nt - 1, :]
    for c in zhalo:
        c.start()

    big = jnp.floor((cell_col + 1.0) * (1.0 / 64.0))
    small_digit = (cell_col + 1.0) - 64.0 * big
    at_rank = lax.broadcasted_iota(jnp.int32, (pan, LANES), 1).astype(f32) == rank_col
    owner = lax.broadcasted_iota(jnp.int32, (n, pan), 0).astype(f32) == peer
    owner = owner.astype(f32).astype(bf16)
    cells = (64.0 * dot(owner, jnp.where(at_rank, big, 0.0).astype(bf16))
             + dot(owner, jnp.where(at_rank, small_digit, 0.0).astype(bf16)) - 1.0)
    last = lax.broadcasted_iota(jnp.int32, (n, LANES), 1) == LANES - 1
    cells = jnp.where(last, spill, cells)
    for d in range(n):
        scell[d] = cells[d:d + 1, :]

    def split_force(lo_row, hi_row):
        h, l = split(ext[:, lo_row:hi_row])
        exthi[:, lo_row:hi_row] = h
        extlo[:, lo_row:hi_row] = l

    loads[0].wait()
    split_force(HALO, HALO + pan)
    for c in fhalo:
        c.wait()
    split_force(0, HALO)
    split_force(HALO + pan, pan + 2 * HALO)

    def picked(c, lo_row, hi_row):
        r = slice(lo_row, hi_row)
        return (dot(pick[r], exthi[c]) + dot(pick[r], extlo[c])) * scale[r]

    def cells_to(g, i):
        there = lax.rem(spot + i, half_n)
        side = half if g < n_ax else 1 - half
        device = (lax.rem(ax + g % n_ax, n_ax), side * half_n + there)
        src, k = g * half_n + there, g * half_n + i
        if g < n_ax:
            cell_at = tcell.at[g * half_n + spot]
        else:
            cell_at = fcell.at[lax.rem(there // 2 - zpos + depth, depth) * group_n + seat]
        return remote(scell.at[src], cell_at, cell_send.at[k], cell_recv.at[k], device)

    def tiles_to(g, i):
        there = lax.rem(spot + i, half_n)
        device = (lax.rem(ax + g, n_ax), half * half_n + there)
        src, k = g * half_n + there, g * half_n + i
        return remote(send.at[src], tiles.at[g * half_n + spot], tile_send.at[k],
                      tile_recv.at[k], device)

    def each(copy, groups, act):
        for g in groups:
            def body(i, carry):
                act(copy(g, i))
                return carry
            lax.fori_loop(1 if g == 0 else 0, half_n, body, 0)

    def along(j):
        return (ax, ((1 - half) * depth + lax.rem(zpos + j, depth)) * 2 + core)

    metas = [remote(smeta.at[j], rmeta.at[j], meta_send.at[j], meta_recv.at[j], along(j))
             for j in range(depth)]
    packs = [[remote(pack.at[c, j], packed.at[c, j], pack_send.at[c, j], pack_recv.at[c, j],
                     along(j)) for j in range(depth)] for c in range(ncomp)]

    def start_packs():
        for c in range(ncomp):
            for j in range(depth):
                at = near + j * keep
                pack[c, j] = picked(c, at, at + keep)
                packs[c][j].start()

    for c in metas:
        c.start()
    start_packs()
    each(cells_to, range(2 * n_ax), lambda c: c.start())
    for c in range(ncomp):
        send[:, :, c * nr:(c + 1) * nr] = picked(c, 0, near).reshape(n // 2, cap, nr)
    each(tiles_to, range(n_ax), lambda c: c.start())
    own = [pltpu.make_async_copy(send.at[spot], tiles.at[spot], own_sem.at[0]),
           pltpu.make_async_copy(scell.at[spot], tcell.at[spot], own_sem.at[1])]
    for c in own:
        c.start()

    for c in ahalo + zhalo:
        c.wait()

    @pl.when(ax == 0)
    def _():
        velx[:, 0] = jnp.zeros((ncomp, nt, nr), f32)
        viscx[0] = jnp.zeros((nt, nr), f32)

    @pl.when(ax == n_ax - 1)
    def _():
        velx[:, na + 1] = jnp.zeros((ncomp, nt, nr), f32)
        viscx[na + 1] = jnp.zeros((nt, nr), f32)

    row_id = lax.broadcasted_iota(jnp.int32, (nt, nr), 0)
    lane_id = lax.broadcasted_iota(jnp.int32, (nt, nr), 1)

    def neighbours(x, low, high):
        left = jnp.where(row_id == 0, low, pltpu.roll(x, 1, 0))
        right = jnp.where(row_id == nt - 1, high, pltpu.roll(x, nt - 1, 0))
        inner = jnp.where(lane_id == 0, 0.0, pltpu.roll(x, 1, 1))
        outer = jnp.where(lane_id == nr - 1, 0.0, pltpu.roll(x, nr - 1, 1))
        return left, right, inner, outer

    def plane(i, carry):
        mu = viscx[i + 1]
        sides = neighbours(mu, edge_in[0, ncomp, pl.ds(i, 1), :], edge_in[1, ncomp, pl.ds(i, 1), :])
        faces = [mu + s for s in (viscx[i], viscx[i + 2]) + sides]
        for c in range(ncomp):
            f = velx[c, i + 1]
            sides_f = neighbours(f, edge_in[0, c, pl.ds(i, 1), :], edge_in[1, c, pl.ds(i, 1), :])
            sides_f = (velx[c, i], velx[c, i + 2]) + sides_f
            total = faces[0] * (sides_f[0] - f)
            for w, g in zip(faces[1:], sides_f[1:]):
                total = total + w * (g - f)
            acc[c, i] = f + (0.5 * step_size) * total
        return carry

    lax.fori_loop(0, na, plane, 0)

    def hop(c, j, k):
        there = lax.rem(seat + k, group_n)
        device = (there // 2, (half * depth + zpos) * 2 + lax.rem(there, 2))
        return remote(sorted_.at[c, j * group_n + there], arrival(c, j),
                      hop_send.at[(c * depth + j) * group_n + k],
                      hop_recv.at[(c * depth + j) * group_n + k], device)

    def arrival(c, j):
        return got.at[c, j * group_n + seat]

    def each_hop(c, j, act):
        def body(k, carry):
            act(hop(c, j, k))
            return carry
        lax.fori_loop(1, group_n, body, 0)

    def hop_mine(c, j):
        return pltpu.make_async_copy(sorted_.at[c, j * group_n + seat], arrival(c, j),
                                     hop_own.at[c * depth + j])

    for c in metas:
        c.wait()
    sorter = [(rmeta[j, :, 0:keep].astype(jnp.int32)
               == lax.broadcasted_iota(jnp.int32, (group_n * cap, keep), 0)
               ).astype(f32).astype(bf16) for j in range(depth)]

    def forward(c):
        for j in range(depth):
            packs[c][j].wait_recv()
            h, l = split(packed[c, j])
            sorted_[c, j * group_n:(j + 1) * group_n] = (
                dot(sorter[j], h) + dot(sorter[j], l)).reshape(group_n, cap, nr)
            each_hop(c, j, lambda x: x.start())
            hop_mine(c, j).start()

    def landed(c):
        for j in range(depth):
            each_hop(c, j, lambda x: x.wait())
            hop_mine(c, j).wait()

    def add(c, where, h, l):
        for m in range(2):
            rows = slice(m * (na // 2) * nt, (m + 1) * (na // 2) * nt)
            total = dot(where[rows], h) + dot(where[rows], l)
            acc[c, m * (na // 2):(m + 1) * (na // 2)] += total.reshape(na // 2, nt, nr)

    def stored(c):
        return pltpu.make_async_copy(acc.at[c], base.at[c], out_sem.at[c])

    forward(0)

    for c in own:
        c.wait()
    each(tiles_to, range(n_ax), lambda c: c.wait())
    each(cells_to, range(n_ax), lambda c: c.wait())
    h, l = split(tiles[...].reshape(-1, ncomp * nr))
    thi[...] = h
    tlo[...] = l
    near_at[...] = landing_of(wide_row(tcell[...].reshape(-1, LANES), cap), 0, na * nt)
    for c in range(ncomp):
        add(c, near_at, thi[:, c * nr:(c + 1) * nr], tlo[:, c * nr:(c + 1) * nr])
        stored(c).start()

    for c in range(1, ncomp):
        forward(c)
    each(cells_to, range(n_ax, 2 * n_ax), lambda c: c.wait())
    landing[...] = landing_of(wide_row(fcell[...].reshape(-1, LANES), cap), 0, na * nt)
    said = jnp.maximum(tcell[...].reshape(-1, LANES), fcell[...].reshape(-1, LANES))
    said = jnp.where(last[0:n // 2], said, 0.0)
    flag[...] = jnp.broadcast_to(jnp.max(jnp.max(said, axis=0, keepdims=True), axis=1,
                                         keepdims=True), (1, LANES))
    for c in range(ncomp):
        landed(c)
        stored(c).wait()
        for j in range(depth):
            packs[c][j].wait_send()


def settle(cap, base, got, gcell, out, hi, lo, crow):
    step = pl.program_id(0)
    ncomp, blk, nt, nr = out.shape

    @pl.when(step == 0)
    def _():
        crow[...] = wide_row(gcell[...].reshape(-1, LANES), cap)
        h, l = split(got[...])
        hi[...] = h
        lo[...] = l

    landing = landing_of(crow[...], step * (blk * nt), blk * nt)
    for c in range(ncomp):
        cs = slice(c * nr, (c + 1) * nr)
        deposit = dot(landing, hi[:, cs]) + dot(landing, lo[:, cs])
        out[c] = base[c, pl.ds(step * blk, blk)] + deposit.reshape(blk, nt, nr)


def settle_packed(base, got, landing, out, total, sem):
    ncomp, na, nt, nr = base.shape
    parts = 2
    blk = na // parts
    stores = []
    for c in range(ncomp):
        hi, lo = split(got[c])
        for m in range(parts):
            rows = slice(m * blk * nt, (m + 1) * blk * nt)
            deposit = dot(landing[rows], hi) + dot(landing[rows], lo)
            planes = slice(m * blk, (m + 1) * blk)
            total[c, planes] = base[c, planes] + deposit.reshape(blk, nt, nr)
            planes = pl.ds(m * blk, blk)
            stores.append(pltpu.make_async_copy(total.at[c, planes], out.at[c, planes],
                                                sem.at[c * parts + m]))
            stores[-1].start()
    for c in stores:
        c.wait()


def direct(n_ax, n_az, cap, *inputs):
    velocity, _, force = inputs[:3]
    n = n_ax * n_az
    ncomp, pan, nr = force.shape
    na, nt = velocity.shape[1:3]
    slots = n * cap
    late = n // 2
    soon = n - late
    f32, bf16 = jnp.float32, jnp.bfloat16
    any_ = pl.BlockSpec(memory_space=pl.ANY)
    hbm = pl.BlockSpec(memory_space=pltpu.HBM)
    vmem = pl.BlockSpec(memory_space=pltpu.VMEM)
    dma = pltpu.SemaphoreType.DMA
    i32 = jnp.int32
    base, got, gcell = pl.pallas_call(
        functools.partial(exchange, n_ax, n_az, cap),
        out_shape=(jax.ShapeDtypeStruct(velocity.shape, f32),
                   jax.ShapeDtypeStruct((late, cap, ncomp * nr), f32),
                   jax.ShapeDtypeStruct((late, 1, LANES), f32)),
        in_specs=[hbm] * 7,
        out_specs=(any_, any_, any_),
        scratch_shapes=[
            pltpu.VMEM((1, pan), i32), pltpu.VMEM((1, pan), i32),
            pltpu.VMEM((1, pan), f32), pltpu.VMEM((4, pan), i32),
            pltpu.VMEM((ncomp, na + 2, nt, nr), f32),
            pltpu.VMEM((na + 2, nt, nr), f32),
            pltpu.VMEM((ncomp, pan + 2 * HALO, nr), f32),
            pltpu.VMEM((ncomp, pan + 2 * HALO, nr), bf16),
            pltpu.VMEM((ncomp, pan + 2 * HALO, nr), bf16),
            pltpu.VMEM((n, cap, ncomp * nr), f32),
            pltpu.VMEM((n, 1, LANES), f32),
            pltpu.VMEM((2, ncomp + 1, na, nr), f32),
            pltpu.VMEM((2, ncomp + 1, na, nr), f32),
            pltpu.VMEM((ncomp, na, nt, nr), f32),
            pltpu.VMEM((soon, cap, ncomp * nr), f32),
            pltpu.VMEM((soon, 1, LANES), f32),
            pltpu.VMEM((soon * cap, ncomp * nr), bf16),
            pltpu.VMEM((soon * cap, ncomp * nr), bf16),
            dma((7,)), dma((8,)), dma((8,)), dma((n,)), dma((n,)), dma((n,)), dma((n,)),
            dma((2,)), dma((na,)),
        ],
        compiler_params=pltpu.CompilerParams(collective_id=1, has_side_effects=True,
                                             vmem_limit_bytes=40 << 20),
        name="exchange",
    )(*inputs)
    blk = max(1, 128 // nt)
    window = pl.BlockSpec((ncomp, blk, nt, nr), lambda s: (0, s, 0, 0))
    return pl.pallas_call(
        functools.partial(settle, cap),
        out_shape=jax.ShapeDtypeStruct(velocity.shape, f32),
        grid=(na // blk,),
        in_specs=[vmem,
                  pl.BlockSpec((late * cap, ncomp * nr), lambda s: (0, 0)),
                  pl.BlockSpec((late, 1, LANES), lambda s: (0, 0, 0))],
        out_specs=window,
        scratch_shapes=[pltpu.VMEM((late * cap, ncomp * nr), bf16),
                        pltpu.VMEM((late * cap, ncomp * nr), bf16),
                        pltpu.VMEM((1, late * cap), f32)],
        compiler_params=pltpu.CompilerParams(vmem_limit_bytes=24 << 20),
        name="settle",
    )(base, got.reshape(late * cap, ncomp * nr), gcell)


def on_device(n_ax, n_az, velocity, viscosity, force, area, adjacency, crossing, cell):
    n, depth, group_n = n_ax * n_az, n_az // 4, 2 * n_ax
    ncomp, pan, nr = force.shape
    na, nt = velocity.shape[1:3]
    most = max(2, 2 * pan // n)
    cap = -(-most // 8) * 8
    keep = -(-(3 * min(pan, group_n * most)) // 64) * 16
    half = n // 2
    f32, bf16, i32 = jnp.float32, jnp.bfloat16, jnp.int32
    any_ = pl.BlockSpec(memory_space=pl.ANY)
    hbm = pl.BlockSpec(memory_space=pltpu.HBM)
    vmem = pl.BlockSpec(memory_space=pltpu.VMEM)
    dma = pltpu.SemaphoreType.DMA
    inputs = (velocity, viscosity, force, crossing.reshape(1, pan), cell.reshape(1, pan),
              area.reshape(1, pan), adjacency.T)
    inputs = [pltpu.with_memory_space_constraint(x, pltpu.HBM) for x in inputs]
    base, got, landing, flag = pl.pallas_call(
        functools.partial(exchange_packed, n_ax, n_az, cap, keep),
        out_shape=(jax.ShapeDtypeStruct(velocity.shape, f32),
                   jax.ShapeDtypeStruct((ncomp, half, cap, nr), f32),
                   jax.ShapeDtypeStruct((na * nt, half * cap), bf16),
                   jax.ShapeDtypeStruct((1, LANES), f32)),
        in_specs=[hbm] * 7,
        out_specs=(any_, any_, vmem, vmem),
        scratch_shapes=[
            pltpu.VMEM((1, pan), i32), pltpu.VMEM((1, pan), i32),
            pltpu.VMEM((1, pan), f32), pltpu.VMEM((4, pan), i32),
            pltpu.VMEM((ncomp, na + 2, nt, nr), f32),
            pltpu.VMEM((na + 2, nt, nr), f32),
            pltpu.VMEM((ncomp, pan + 2 * HALO, nr), f32),
            pltpu.VMEM((ncomp, pan + 2 * HALO, nr), bf16),
            pltpu.VMEM((ncomp, pan + 2 * HALO, nr), bf16),
            pltpu.VMEM((half, cap, ncomp * nr), f32),
            pltpu.VMEM((n, 1, LANES), f32),
            pltpu.VMEM((2, ncomp + 1, na, nr), f32),
            pltpu.VMEM((2, ncomp + 1, na, nr), f32),
            pltpu.VMEM((ncomp, na, nt, nr), f32),
            pltpu.VMEM((half, cap, ncomp * nr), f32),
            pltpu.VMEM((half, 1, LANES), f32),
            pltpu.VMEM((half, 1, LANES), f32),
            pltpu.VMEM((half * cap, ncomp * nr), bf16),
            pltpu.VMEM((half * cap, ncomp * nr), bf16),
            pltpu.VMEM((ncomp, depth, keep, nr), f32),
            pltpu.VMEM((ncomp, depth, keep, nr), f32),
            pltpu.VMEM((depth, 1, LANES), f32),
            pltpu.VMEM((depth, 1, LANES), f32),
            pltpu.VMEM((ncomp, half, cap, nr), f32),
            pltpu.VMEM((na * nt, half * cap), bf16),
            dma((7,)), dma((8,)), dma((8,)), dma((half,)), dma((half,)), dma((n,)), dma((n,)),
            dma((2,)), dma((na,)),
            dma((ncomp, depth)), dma((ncomp, depth)), dma((depth,)), dma((depth,)),
            dma((ncomp * half,)), dma((ncomp * half,)), dma((ncomp * depth,)),
        ],
        compiler_params=pltpu.CompilerParams(collective_id=0, has_side_effects=True,
                                             vmem_limit_bytes=44 << 20),
        name="exchange_packed",
    )(*inputs)
    def finish(base, got, landing, *inputs):
        return pl.pallas_call(
            settle_packed,
            out_shape=jax.ShapeDtypeStruct(velocity.shape, f32),
            in_specs=[vmem, vmem, vmem],
            out_specs=hbm,
            scratch_shapes=[pltpu.VMEM((ncomp, na, nt, nr), f32), dma((2 * ncomp,))],
            compiler_params=pltpu.CompilerParams(vmem_limit_bytes=52 << 20),
            name="settle_packed",
        )(base, got.reshape(ncomp, half * cap, nr), landing)

    def again(base, got, landing, *inputs):
        return direct(n_ax, n_az, cap, *inputs)

    return lax.cond(flag[0, 0] > 0.5, again, finish, base, got, landing, *inputs)


def solution(mesh):
    n_ax, n_az = mesh.shape["ax"], mesh.shape["az"]
    in_specs = (
        P(None, "ax", "az", None),
        P("ax", "az", None),
        P(None, ("ax", "az"), None),
        P(("ax", "az")),
        P(("ax", "az"), None),
        P(("ax", "az"), None),
        P(("ax", "az")),
    )
    return jax.shard_map(
        functools.partial(on_device, n_ax, n_az), mesh=mesh, in_specs=in_specs,
        out_specs=P(None, "ax", "az", None), check_vma=False)
```

```python
import functools

import jax
import jax.numpy as jnp
from jax import lax
from jax.experimental import pallas as pl
from jax.experimental.pallas import tpu as pltpu
from jax.sharding import PartitionSpec as P

HALO = 32
LANES = 128

step_size = 0.1
coupling = 0.2


def split(x):
    hi = x.astype(jnp.bfloat16)
    lo = (x - hi.astype(jnp.float32)).astype(jnp.bfloat16)
    return hi, lo


def dot(a, b):
    return jnp.dot(a, b, preferred_element_type=jnp.float32)


def wide_row(cells, cap):
    m = cells.shape[0]
    slots = m * cap
    big = jnp.floor((cells + 1.0) * (1.0 / 64.0))
    small = (cells + 1.0) - 64.0 * big
    spread = (lax.broadcasted_iota(jnp.int32, (LANES, slots), 0)
              == lax.rem(lax.broadcasted_iota(jnp.int32, (LANES, slots), 1), cap))
    spread = spread.astype(jnp.float32).astype(jnp.bfloat16)
    wide = 64.0 * dot(big.astype(jnp.bfloat16), spread) + dot(small.astype(jnp.bfloat16), spread)
    mine = (lax.broadcasted_iota(jnp.int32, (m, slots), 0)
            == lax.broadcasted_iota(jnp.int32, (m, slots), 1) // cap)
    return jnp.sum(jnp.where(mine, wide, 0.0), axis=0, keepdims=True) - 1.0


def landing_of(crow, first, count):
    here = lax.broadcasted_iota(jnp.int32, (count, crow.shape[1]), 0) + first
    return (crow.astype(jnp.int32) == here).astype(jnp.float32).astype(jnp.bfloat16)


def exchange(n_ax, n_az, cap, vel, visc, force, dest_h, cell_h, area_h, adj_h, base, got, gcell,
             dest_i, cell_i, area, adj_i,
             velx, viscx, ext, exthi, extlo, send, scell, edges, edge_in, acc,
             tiles, tcell, thi, tlo,
             load_sem, halo_send, halo_recv, tile_send, tile_recv,
             cell_send, cell_recv, own_sem, out_sem):
    n, half_n = n_ax * n_az, n_az // 2
    ax, az = lax.axis_index("ax"), lax.axis_index("az")
    me = ax * n_az + az
    half, spot = az // half_n, lax.rem(az, half_n)
    ncomp, na, nt, nr = vel.shape
    pan = force.shape[1]
    slots = n * cap
    f32, bf16 = jnp.float32, jnp.bfloat16

    def place(linear):
        return (linear // n_az, lax.rem(linear, n_az))

    def remote(src, dst, ssem, rsem, device):
        return pltpu.make_async_remote_copy(
            src_ref=src, dst_ref=dst, send_sem=ssem, recv_sem=rsem,
            device_id=device, device_id_type=pl.DeviceIdType.MESH)

    barrier = pltpu.get_barrier_semaphore()

    def greet(k, carry):
        pl.semaphore_signal(barrier, inc=1, device_id=place(lax.rem(me + k, n)),
                            device_id_type=pl.DeviceIdType.MESH)
        return carry

    lax.fori_loop(1, n, greet, 0)
    small = [pltpu.make_async_copy(src, dst, load_sem.at[3 + k]) for k, (src, dst) in enumerate(
        [(dest_h, dest_i), (cell_h, cell_i), (adj_h, adj_i), (area_h, area)])]
    loads = [
        pltpu.make_async_copy(force, ext.at[:, pl.ds(HALO, pan)], load_sem.at[0]),
        pltpu.make_async_copy(vel, velx.at[:, pl.ds(1, na)], load_sem.at[1]),
        pltpu.make_async_copy(visc, viscx.at[pl.ds(1, na)], load_sem.at[2]),
    ]
    for c in small + loads:
        c.start()

    pl.semaphore_wait(barrier, n - 1)

    up, down = place(lax.rem(me + 1, n)), place(lax.rem(me + n - 1, n))
    ax_up, ax_down = lax.rem(ax + 1, n_ax), lax.rem(ax + n_ax - 1, n_ax)
    az_up, az_down = lax.rem(az + 1, n_az), lax.rem(az + n_az - 1, n_az)

    def halo(i, src, dst, device):
        return remote(src, dst, halo_send.at[i], halo_recv.at[i], device)

    fhalo = [
        halo(0, force.at[:, pl.ds(pan - HALO, HALO)], ext.at[:, pl.ds(0, HALO)], up),
        halo(1, force.at[:, pl.ds(0, HALO)], ext.at[:, pl.ds(HALO + pan, HALO)], down),
    ]
    ahalo = [
        halo(2, vel.at[:, na - 1], velx.at[:, 0], (ax_up, az)),
        halo(3, vel.at[:, 0], velx.at[:, na + 1], (ax_down, az)),
        halo(4, visc.at[na - 1], viscx.at[0], (ax_up, az)),
        halo(5, visc.at[0], viscx.at[na + 1], (ax_down, az)),
    ]
    zhalo = [
        halo(6, edges.at[1], edge_in.at[0], (ax, az_up)),
        halo(7, edges.at[0], edge_in.at[1], (ax, az_down)),
    ]
    for c in fhalo:
        c.start()
    for c in small:
        c.wait()

    dest_row, cell_row = dest_i[...].astype(f32), cell_i[...].astype(f32)
    adj = (adj_i[...] - (me * pan - HALO)).astype(f32)
    rows = jnp.concatenate([dest_row, cell_row, adj, dest_row, dest_row], axis=0)
    cols = rows.T
    dest_col, cell_col = cols[:, 0:1], cols[:, 1:2]
    same = dest_col == dest_row
    r0 = lax.broadcasted_iota(jnp.int32, (pan, pan), 0)
    r1 = lax.broadcasted_iota(jnp.int32, (pan, pan), 1)
    rank_row = jnp.sum((same & (r0 < r1)).astype(f32), axis=0, keepdims=True)
    rank_col = jnp.sum((same & (r1 < r0)).astype(f32), axis=1, keepdims=True)
    dax = jnp.floor(dest_row * (1.0 / n_az))
    daz = dest_row - n_az * dax
    dhalf = jnp.floor(daz * (1.0 / half_n))
    turn = dax - ax.astype(f32)
    turn = jnp.where(turn < 0.0, turn + n_ax, turn)
    group = turn + jnp.where(dhalf == half.astype(f32), 0.0, float(n_ax))
    peer = group * half_n + (daz - half_n * dhalf)
    target = (peer * cap + rank_row).astype(jnp.int32)
    hits = lax.broadcasted_iota(jnp.int32, (slots, pan), 0) == target
    scale = jnp.sum(jnp.where(hits, coupling * area[...], 0.0), axis=1, keepdims=True)
    q = lax.broadcasted_iota(jnp.int32, (pan, pan + 2 * HALO), 1).astype(f32)
    p = lax.broadcasted_iota(jnp.int32, (pan, pan + 2 * HALO), 0).astype(f32)
    count = (q == p + HALO).astype(f32)
    for k in range(4):
        count = count + (q == cols[:, 2 + k:3 + k]).astype(f32)
    pick = dot(hits.astype(f32).astype(bf16), count.astype(bf16)).astype(bf16)

    loads[1].wait()
    loads[2].wait()
    for c in range(ncomp):
        edges[0, c] = velx[c, 1:na + 1, 0, :]
        edges[1, c] = velx[c, 1:na + 1, nt - 1, :]
    edges[0, ncomp] = viscx[1:na + 1, 0, :]
    edges[1, ncomp] = viscx[1:na + 1, nt - 1, :]

    for c in zhalo + ahalo:
        c.start()

    big = jnp.floor((cell_col + 1.0) * (1.0 / 64.0))
    small = (cell_col + 1.0) - 64.0 * big
    at_rank = lax.broadcasted_iota(jnp.int32, (pan, LANES), 1).astype(f32) == rank_col
    owner = lax.broadcasted_iota(jnp.int32, (n, pan), 0).astype(f32) == peer
    owner = owner.astype(f32).astype(bf16)
    cells = (64.0 * dot(owner, jnp.where(at_rank, big, 0.0).astype(bf16))
             + dot(owner, jnp.where(at_rank, small, 0.0).astype(bf16)) - 1.0)
    for d in range(n):
        scell[d] = cells[d:d + 1, :]

    def split_force(lo_row, hi_row):
        h, l = split(ext[:, lo_row:hi_row])
        exthi[:, lo_row:hi_row] = h
        extlo[:, lo_row:hi_row] = l

    loads[0].wait()
    split_force(HALO, HALO + pan)
    for c in fhalo:
        c.wait()
    split_force(0, HALO)
    split_force(HALO + pan, pan + 2 * HALO)

    def tiles_to(g, i):
        there = lax.rem(spot + i, half_n)
        side = half if g < n_ax else 1 - half
        device = (lax.rem(ax + g % n_ax, n_ax), side * half_n + there)
        src, k = g * half_n + there, g * half_n + i
        at = (g % n_ax) * half_n + spot
        tile_at, cell_at = (tiles, tcell) if g < n_ax else (got, gcell)
        return (remote(send.at[src], tile_at.at[at], tile_send.at[k], tile_recv.at[k], device),
                remote(scell.at[src], cell_at.at[at], cell_send.at[k], cell_recv.at[k], device))

    def each_tile(groups, act):
        for g in groups:
            def body(i, carry):
                for c in tiles_to(g, i):
                    act(c)
                return carry
            lax.fori_loop(1 if g == 0 else 0, half_n, body, 0)

    for part in range(2):
        r = slice(part * (slots // 2), (part + 1) * (slots // 2))
        for c in range(ncomp):
            tile = (dot(pick[r], exthi[c]) + dot(pick[r], extlo[c])) * scale[r]
            send[part * (n // 2):(part + 1) * (n // 2), :, c * nr:(c + 1) * nr] = (
                tile.reshape(n // 2, cap, nr))
        each_tile(range(part * n_ax, (part + 1) * n_ax), lambda c: c.start())
    own = [pltpu.make_async_copy(send.at[spot], tiles.at[spot], own_sem.at[0]),
           pltpu.make_async_copy(scell.at[spot], tcell.at[spot], own_sem.at[1])]
    for c in own:
        c.start()

    for c in ahalo + zhalo:
        c.wait()

    @pl.when(ax == 0)
    def _():
        velx[:, 0] = jnp.zeros((ncomp, nt, nr), f32)
        viscx[0] = jnp.zeros((nt, nr), f32)

    @pl.when(ax == n_ax - 1)
    def _():
        velx[:, na + 1] = jnp.zeros((ncomp, nt, nr), f32)
        viscx[na + 1] = jnp.zeros((nt, nr), f32)

    row_id = lax.broadcasted_iota(jnp.int32, (nt, nr), 0)
    lane_id = lax.broadcasted_iota(jnp.int32, (nt, nr), 1)

    def neighbours(x, low, high):
        left = jnp.where(row_id == 0, low, pltpu.roll(x, 1, 0))
        right = jnp.where(row_id == nt - 1, high, pltpu.roll(x, nt - 1, 0))
        inner = jnp.where(lane_id == 0, 0.0, pltpu.roll(x, 1, 1))
        outer = jnp.where(lane_id == nr - 1, 0.0, pltpu.roll(x, nr - 1, 1))
        return left, right, inner, outer

    def plane(i, carry):
        mu = viscx[i + 1]
        sides = neighbours(mu, edge_in[0, ncomp, pl.ds(i, 1), :], edge_in[1, ncomp, pl.ds(i, 1), :])
        faces = [mu + s for s in (viscx[i], viscx[i + 2]) + sides]
        for c in range(ncomp):
            f = velx[c, i + 1]
            near = neighbours(f, edge_in[0, c, pl.ds(i, 1), :], edge_in[1, c, pl.ds(i, 1), :])
            near = (velx[c, i], velx[c, i + 2]) + near
            total = faces[0] * (near[0] - f)
            for w, g in zip(faces[1:], near[1:]):
                total = total + w * (g - f)
            acc[c, i] = f + (0.5 * step_size) * total
        return carry

    lax.fori_loop(0, na, plane, 0)

    for c in own:
        c.wait()
    each_tile(range(n_ax), lambda c: c.wait())
    h, l = split(tiles[...].reshape(-1, ncomp * nr))
    thi[...] = h
    tlo[...] = l
    crow = wide_row(tcell[...].reshape(-1, LANES), cap)
    blk = max(1, 256 // nt)

    def stored(j):
        return pltpu.make_async_copy(acc.at[:, pl.ds(j * blk, blk)],
                                     base.at[:, pl.ds(j * blk, blk)], out_sem.at[j])

    for j in range(na // blk):
        landing = landing_of(crow, j * blk * nt, blk * nt)
        for c in range(ncomp):
            cs = slice(c * nr, (c + 1) * nr)
            deposit = dot(landing, thi[:, cs]) + dot(landing, tlo[:, cs])
            acc[c, j * blk:(j + 1) * blk] += deposit.reshape(blk, nt, nr)
        stored(j).start()
    for j in range(na // blk):
        stored(j).wait()
    each_tile(range(n_ax, 2 * n_ax), lambda c: c.wait())


def exchange_packed(n_ax, n_az, cap, keep, vel, visc, force, dest_h, cell_h, area_h, adj_h,
                    base, got, landing, flag,
                    dest_i, cell_i, area, adj_i,
                    velx, viscx, ext, exthi, extlo, send, scell, edges, edge_in, acc,
                    tiles, tcell, fcell, thi, tlo, pack, packed, smeta, rmeta, sorted_, near_at,
                    load_sem, halo_send, halo_recv, tile_send, tile_recv,
                    cell_send, cell_recv, own_sem, out_sem,
                    pack_send, pack_recv, meta_send, meta_recv, hop_send, hop_recv, hop_own):
    n, half_n = n_ax * n_az, n_az // 2
    depth, group_n = half_n // 2, 2 * n_ax
    ax, az = lax.axis_index("ax"), lax.axis_index("az")
    me = ax * n_az + az
    half, spot = az // half_n, lax.rem(az, half_n)
    zpos, core = spot // 2, lax.rem(az, 2)
    seat = ax * 2 + core
    ncomp, na, nt, nr = vel.shape
    pan = force.shape[1]
    near = (n // 2) * cap
    slots = near + depth * keep
    f32, bf16 = jnp.float32, jnp.bfloat16

    def place(linear):
        return (linear // n_az, lax.rem(linear, n_az))

    def remote(src, dst, ssem, rsem, device):
        return pltpu.make_async_remote_copy(
            src_ref=src, dst_ref=dst, send_sem=ssem, recv_sem=rsem,
            device_id=device, device_id_type=pl.DeviceIdType.MESH)

    barrier = pltpu.get_barrier_semaphore()

    def greet(k, carry):
        pl.semaphore_signal(barrier, inc=1, device_id=place(lax.rem(me + k, n)),
                            device_id_type=pl.DeviceIdType.MESH)
        return carry

    lax.fori_loop(1, n, greet, 0)
    small = [pltpu.make_async_copy(src, dst, load_sem.at[3 + k]) for k, (src, dst) in enumerate(
        [(dest_h, dest_i), (cell_h, cell_i), (adj_h, adj_i), (area_h, area)])]
    loads = [
        pltpu.make_async_copy(force, ext.at[:, pl.ds(HALO, pan)], load_sem.at[0]),
        pltpu.make_async_copy(vel, velx.at[:, pl.ds(1, na)], load_sem.at[1]),
        pltpu.make_async_copy(visc, viscx.at[pl.ds(1, na)], load_sem.at[2]),
    ]
    for c in small + loads:
        c.start()

    pl.semaphore_wait(barrier, n - 1)

    up, down = place(lax.rem(me + 1, n)), place(lax.rem(me + n - 1, n))
    ax_up, ax_down = lax.rem(ax + 1, n_ax), lax.rem(ax + n_ax - 1, n_ax)
    az_up, az_down = lax.rem(az + 1, n_az), lax.rem(az + n_az - 1, n_az)

    def halo(i, src, dst, device):
        return remote(src, dst, halo_send.at[i], halo_recv.at[i], device)

    fhalo = [
        halo(0, force.at[:, pl.ds(pan - HALO, HALO)], ext.at[:, pl.ds(0, HALO)], up),
        halo(1, force.at[:, pl.ds(0, HALO)], ext.at[:, pl.ds(HALO + pan, HALO)], down),
    ]
    ahalo = [
        halo(2, vel.at[:, na - 1], velx.at[:, 0], (ax_up, az)),
        halo(3, vel.at[:, 0], velx.at[:, na + 1], (ax_down, az)),
        halo(4, visc.at[na - 1], viscx.at[0], (ax_up, az)),
        halo(5, visc.at[0], viscx.at[na + 1], (ax_down, az)),
    ]
    zhalo = [
        halo(6, edges.at[1], edge_in.at[0], (ax, az_up)),
        halo(7, edges.at[0], edge_in.at[1], (ax, az_down)),
    ]
    for c in fhalo + ahalo:
        c.start()
    for c in small:
        c.wait()

    dest_row, cell_row = dest_i[...].astype(f32), cell_i[...].astype(f32)
    adj = (adj_i[...] - (me * pan - HALO)).astype(f32)
    rows = jnp.concatenate([dest_row, cell_row, adj, dest_row, dest_row], axis=0)
    cols = rows.T
    dest_col, cell_col = cols[:, 0:1], cols[:, 1:2]
    same = dest_col == dest_row
    r0 = lax.broadcasted_iota(jnp.int32, (pan, pan), 0)
    r1 = lax.broadcasted_iota(jnp.int32, (pan, pan), 1)
    rank_row = jnp.sum((same & (r0 < r1)).astype(f32), axis=0, keepdims=True)
    rank_col = jnp.sum((same & (r1 < r0)).astype(f32), axis=1, keepdims=True)

    def layer_of(dest):
        inner = dest - n_az * jnp.floor(dest * (1.0 / n_az))
        return jnp.floor(inner * 0.5)

    dax = jnp.floor(dest_row * (1.0 / n_az))
    daz = dest_row - n_az * dax
    dhalf = jnp.floor(daz * (1.0 / half_n))
    layer_row, layer_col = layer_of(dest_row), layer_of(dest_col)
    pos_row = jnp.sum(((layer_col == layer_row) & (r0 < r1)).astype(f32), axis=0, keepdims=True)
    turn = dax - ax.astype(f32)
    turn = jnp.where(turn < 0.0, turn + n_ax, turn)
    far = dhalf != half.astype(f32)
    group = turn + jnp.where(far, float(n_ax), 0.0)
    peer = group * half_n + (daz - half_n * dhalf)
    dz = (layer_row - depth * dhalf) - zpos.astype(f32)
    dz = jnp.where(dz < 0.0, dz + depth, dz)
    spilled = far & (pos_row >= keep)
    target = jnp.where(far, near + dz * keep + pos_row, peer * cap + rank_row)
    target = jnp.where(spilled, -1.0, target).astype(jnp.int32)
    spill = jnp.max(jnp.where(spilled, 1.0, 0.0), axis=1, keepdims=True)
    hits = lax.broadcasted_iota(jnp.int32, (slots, pan), 0) == target
    scale = jnp.sum(jnp.where(hits, coupling * area[...], 0.0), axis=1, keepdims=True)
    q = lax.broadcasted_iota(jnp.int32, (pan, pan + 2 * HALO), 1).astype(f32)
    p = lax.broadcasted_iota(jnp.int32, (pan, pan + 2 * HALO), 0).astype(f32)
    count = (q == p + HALO).astype(f32)
    for k in range(4):
        count = count + (q == cols[:, 2 + k:3 + k]).astype(f32)
    hits = hits.astype(f32).astype(bf16)
    pick = dot(hits, count.astype(bf16)).astype(bf16)
    slot = (dax * 2.0 + (daz - 2.0 * layer_row)) * cap + rank_row + 1.0
    sbig = jnp.floor(slot * (1.0 / 64.0))
    digits = jnp.concatenate([sbig, slot - 64.0 * sbig] * 4, axis=0).astype(bf16)
    for j in range(depth):
        at = near + j * keep
        found = lax.dot_general(digits, hits[at:at + keep], (((1,), (1,)), ((), ())),
                                preferred_element_type=f32)
        smeta[j] = jnp.full((1, LANES), -1.0, f32)
        smeta[j, :, 0:keep] = 64.0 * found[0:1] + found[1:2] - 1.0

    loads[1].wait()
    loads[2].wait()
    for c in range(ncomp):
        edges[0, c] = velx[c, 1:na + 1, 0, :]
        edges[1, c] = velx[c, 1:na + 1, nt - 1, :]
    edges[0, ncomp] = viscx[1:na + 1, 0, :]
    edges[1, ncomp] = viscx[1:na + 1, nt - 1, :]
    for c in zhalo:
        c.start()

    big = jnp.floor((cell_col + 1.0) * (1.0 / 64.0))
    small_digit = (cell_col + 1.0) - 64.0 * big
    at_rank = lax.broadcasted_iota(jnp.int32, (pan, LANES), 1).astype(f32) == rank_col
    owner = lax.broadcasted_iota(jnp.int32, (n, pan), 0).astype(f32) == peer
    owner = owner.astype(f32).astype(bf16)
    cells = (64.0 * dot(owner, jnp.where(at_rank, big, 0.0).astype(bf16))
             + dot(owner, jnp.where(at_rank, small_digit, 0.0).astype(bf16)) - 1.0)
    last = lax.broadcasted_iota(jnp.int32, (n, LANES), 1) == LANES - 1
    cells = jnp.where(last, spill, cells)
    for d in range(n):
        scell[d] = cells[d:d + 1, :]

    def split_force(lo_row, hi_row):
        h, l = split(ext[:, lo_row:hi_row])
        exthi[:, lo_row:hi_row] = h
        extlo[:, lo_row:hi_row] = l

    loads[0].wait()
    split_force(HALO, HALO + pan)
    for c in fhalo:
        c.wait()
    split_force(0, HALO)
    split_force(HALO + pan, pan + 2 * HALO)

    def picked(c, lo_row, hi_row):
        r = slice(lo_row, hi_row)
        return (dot(pick[r], exthi[c]) + dot(pick[r], extlo[c])) * scale[r]

    def cells_to(g, i):
        there = lax.rem(spot + i, half_n)
        side = half if g < n_ax else 1 - half
        device = (lax.rem(ax + g % n_ax, n_ax), side * half_n + there)
        src, k = g * half_n + there, g * half_n + i
        if g < n_ax:
            cell_at = tcell.at[g * half_n + spot]
        else:
            cell_at = fcell.at[lax.rem(there // 2 - zpos + depth, depth) * group_n + seat]
        return remote(scell.at[src], cell_at, cell_send.at[k], cell_recv.at[k], device)

    def tiles_to(g, i):
        there = lax.rem(spot + i, half_n)
        device = (lax.rem(ax + g, n_ax), half * half_n + there)
        src, k = g * half_n + there, g * half_n + i
        return remote(send.at[src], tiles.at[g * half_n + spot], tile_send.at[k],
                      tile_recv.at[k], device)

    def each(copy, groups, act):
        for g in groups:
            def body(i, carry):
                act(copy(g, i))
                return carry
            lax.fori_loop(1 if g == 0 else 0, half_n, body, 0)

    def along(j):
        return (ax, ((1 - half) * depth + lax.rem(zpos + j, depth)) * 2 + core)

    metas = [remote(smeta.at[j], rmeta.at[j], meta_send.at[j], meta_recv.at[j], along(j))
             for j in range(depth)]
    packs = [[remote(pack.at[c, j], packed.at[c, j], pack_send.at[c, j], pack_recv.at[c, j],
                     along(j)) for j in range(depth)] for c in range(ncomp)]

    def start_packs():
        for c in range(ncomp):
            for j in range(depth):
                at = near + j * keep
                pack[c, j] = picked(c, at, at + keep)
                packs[c][j].start()

    for c in metas:
        c.start()
    each(cells_to, range(2 * n_ax), lambda c: c.start())
    for c in range(ncomp):
        send[:, :, c * nr:(c + 1) * nr] = picked(c, 0, near).reshape(n // 2, cap, nr)
    each(tiles_to, range(n_ax), lambda c: c.start())
    start_packs()
    own = [pltpu.make_async_copy(send.at[spot], tiles.at[spot], own_sem.at[0]),
           pltpu.make_async_copy(scell.at[spot], tcell.at[spot], own_sem.at[1])]
    for c in own:
        c.start()

    for c in ahalo + zhalo:
        c.wait()

    @pl.when(ax == 0)
    def _():
        velx[:, 0] = jnp.zeros((ncomp, nt, nr), f32)
        viscx[0] = jnp.zeros((nt, nr), f32)

    @pl.when(ax == n_ax - 1)
    def _():
        velx[:, na + 1] = jnp.zeros((ncomp, nt, nr), f32)
        viscx[na + 1] = jnp.zeros((nt, nr), f32)

    row_id = lax.broadcasted_iota(jnp.int32, (nt, nr), 0)
    lane_id = lax.broadcasted_iota(jnp.int32, (nt, nr), 1)

    def neighbours(x, low, high):
        left = jnp.where(row_id == 0, low, pltpu.roll(x, 1, 0))
        right = jnp.where(row_id == nt - 1, high, pltpu.roll(x, nt - 1, 0))
        inner = jnp.where(lane_id == 0, 0.0, pltpu.roll(x, 1, 1))
        outer = jnp.where(lane_id == nr - 1, 0.0, pltpu.roll(x, nr - 1, 1))
        return left, right, inner, outer

    def plane(i, carry):
        mu = viscx[i + 1]
        sides = neighbours(mu, edge_in[0, ncomp, pl.ds(i, 1), :], edge_in[1, ncomp, pl.ds(i, 1), :])
        faces = [mu + s for s in (viscx[i], viscx[i + 2]) + sides]
        for c in range(ncomp):
            f = velx[c, i + 1]
            sides_f = neighbours(f, edge_in[0, c, pl.ds(i, 1), :], edge_in[1, c, pl.ds(i, 1), :])
            sides_f = (velx[c, i], velx[c, i + 2]) + sides_f
            total = faces[0] * (sides_f[0] - f)
            for w, g in zip(faces[1:], sides_f[1:]):
                total = total + w * (g - f)
            acc[c, i] = f + (0.5 * step_size) * total
        return carry

    lax.fori_loop(0, na, plane, 0)

    def hop(c, j, k):
        there = lax.rem(seat + k, group_n)
        device = (there // 2, (half * depth + zpos) * 2 + lax.rem(there, 2))
        return remote(sorted_.at[c, j * group_n + there], arrival(c, j),
                      hop_send.at[(c * depth + j) * group_n + k],
                      hop_recv.at[(c * depth + j) * group_n + k], device)

    def arrival(c, j):
        return got.at[c, j * group_n + seat]

    def each_hop(c, j, act):
        def body(k, carry):
            act(hop(c, j, k))
            return carry
        lax.fori_loop(1, group_n, body, 0)

    def hop_mine(c, j):
        return pltpu.make_async_copy(sorted_.at[c, j * group_n + seat], arrival(c, j),
                                     hop_own.at[c * depth + j])

    for c in metas:
        c.wait()
    sorter = [(rmeta[j, :, 0:keep].astype(jnp.int32)
               == lax.broadcasted_iota(jnp.int32, (group_n * cap, keep), 0)
               ).astype(f32).astype(bf16) for j in range(depth)]

    def forward(c):
        for j in range(depth):
            packs[c][j].wait_recv()
            h, l = split(packed[c, j])
            sorted_[c, j * group_n:(j + 1) * group_n] = (
                dot(sorter[j], h) + dot(sorter[j], l)).reshape(group_n, cap, nr)
            each_hop(c, j, lambda x: x.start())
            hop_mine(c, j).start()

    def landed(c):
        for j in range(depth):
            each_hop(c, j, lambda x: x.wait())
            hop_mine(c, j).wait()

    def add(c, where, h, l):
        for m in range(2):
            rows = slice(m * (na // 2) * nt, (m + 1) * (na // 2) * nt)
            total = dot(where[rows], h) + dot(where[rows], l)
            acc[c, m * (na // 2):(m + 1) * (na // 2)] += total.reshape(na // 2, nt, nr)

    def stored(c):
        return pltpu.make_async_copy(acc.at[c], base.at[c], out_sem.at[c])

    forward(0)

    for c in own:
        c.wait()
    each(tiles_to, range(n_ax), lambda c: c.wait())
    each(cells_to, range(n_ax), lambda c: c.wait())
    h, l = split(tiles[...].reshape(-1, ncomp * nr))
    thi[...] = h
    tlo[...] = l
    near_at[...] = landing_of(wide_row(tcell[...].reshape(-1, LANES), cap), 0, na * nt)
    for c in range(ncomp):
        add(c, near_at, thi[:, c * nr:(c + 1) * nr], tlo[:, c * nr:(c + 1) * nr])
        stored(c).start()

    for c in range(1, ncomp):
        forward(c)
    each(cells_to, range(n_ax, 2 * n_ax), lambda c: c.wait())
    landing[...] = landing_of(wide_row(fcell[...].reshape(-1, LANES), cap), 0, na * nt)
    said = jnp.maximum(tcell[...].reshape(-1, LANES), fcell[...].reshape(-1, LANES))
    said = jnp.where(last[0:n // 2], said, 0.0)
    flag[...] = jnp.broadcast_to(jnp.max(jnp.max(said, axis=0, keepdims=True), axis=1,
                                         keepdims=True), (1, LANES))
    for c in range(ncomp):
        landed(c)
        stored(c).wait()
        for j in range(depth):
            packs[c][j].wait_send()


def settle(cap, base, got, gcell, out, hi, lo, crow):
    step = pl.program_id(0)
    ncomp, blk, nt, nr = out.shape

    @pl.when(step == 0)
    def _():
        crow[...] = wide_row(gcell[...].reshape(-1, LANES), cap)
        h, l = split(got[...])
        hi[...] = h
        lo[...] = l

    landing = landing_of(crow[...], step * (blk * nt), blk * nt)
    for c in range(ncomp):
        cs = slice(c * nr, (c + 1) * nr)
        deposit = dot(landing, hi[:, cs]) + dot(landing, lo[:, cs])
        out[c] = base[c, pl.ds(step * blk, blk)] + deposit.reshape(blk, nt, nr)


def settle_packed(base, got, landing, out, total, sem):
    ncomp, na, nt, nr = base.shape
    parts = 2
    blk = na // parts
    stores = []
    for c in range(ncomp):
        hi, lo = split(got[c])
        for m in range(parts):
            rows = slice(m * blk * nt, (m + 1) * blk * nt)
            deposit = dot(landing[rows], hi) + dot(landing[rows], lo)
            planes = slice(m * blk, (m + 1) * blk)
            total[c, planes] = base[c, planes] + deposit.reshape(blk, nt, nr)
            planes = pl.ds(m * blk, blk)
            stores.append(pltpu.make_async_copy(total.at[c, planes], out.at[c, planes],
                                                sem.at[c * parts + m]))
            stores[-1].start()
    for c in stores:
        c.wait()


def direct(n_ax, n_az, cap, *inputs):
    velocity, _, force = inputs[:3]
    n = n_ax * n_az
    ncomp, pan, nr = force.shape
    na, nt = velocity.shape[1:3]
    slots = n * cap
    late = n // 2
    soon = n - late
    f32, bf16 = jnp.float32, jnp.bfloat16
    any_ = pl.BlockSpec(memory_space=pl.ANY)
    hbm = pl.BlockSpec(memory_space=pltpu.HBM)
    vmem = pl.BlockSpec(memory_space=pltpu.VMEM)
    dma = pltpu.SemaphoreType.DMA
    i32 = jnp.int32
    base, got, gcell = pl.pallas_call(
        functools.partial(exchange, n_ax, n_az, cap),
        out_shape=(jax.ShapeDtypeStruct(velocity.shape, f32),
                   jax.ShapeDtypeStruct((late, cap, ncomp * nr), f32),
                   jax.ShapeDtypeStruct((late, 1, LANES), f32)),
        in_specs=[hbm] * 7,
        out_specs=(any_, any_, any_),
        scratch_shapes=[
            pltpu.VMEM((1, pan), i32), pltpu.VMEM((1, pan), i32),
            pltpu.VMEM((1, pan), f32), pltpu.VMEM((4, pan), i32),
            pltpu.VMEM((ncomp, na + 2, nt, nr), f32),
            pltpu.VMEM((na + 2, nt, nr), f32),
            pltpu.VMEM((ncomp, pan + 2 * HALO, nr), f32),
            pltpu.VMEM((ncomp, pan + 2 * HALO, nr), bf16),
            pltpu.VMEM((ncomp, pan + 2 * HALO, nr), bf16),
            pltpu.VMEM((n, cap, ncomp * nr), f32),
            pltpu.VMEM((n, 1, LANES), f32),
            pltpu.VMEM((2, ncomp + 1, na, nr), f32),
            pltpu.VMEM((2, ncomp + 1, na, nr), f32),
            pltpu.VMEM((ncomp, na, nt, nr), f32),
            pltpu.VMEM((soon, cap, ncomp * nr), f32),
            pltpu.VMEM((soon, 1, LANES), f32),
            pltpu.VMEM((soon * cap, ncomp * nr), bf16),
            pltpu.VMEM((soon * cap, ncomp * nr), bf16),
            dma((7,)), dma((8,)), dma((8,)), dma((n,)), dma((n,)), dma((n,)), dma((n,)),
            dma((2,)), dma((na,)),
        ],
        compiler_params=pltpu.CompilerParams(collective_id=1, has_side_effects=True,
                                             vmem_limit_bytes=40 << 20),
        name="exchange",
    )(*inputs)
    blk = max(1, 128 // nt)
    window = pl.BlockSpec((ncomp, blk, nt, nr), lambda s: (0, s, 0, 0))
    return pl.pallas_call(
        functools.partial(settle, cap),
        out_shape=jax.ShapeDtypeStruct(velocity.shape, f32),
        grid=(na // blk,),
        in_specs=[vmem,
                  pl.BlockSpec((late * cap, ncomp * nr), lambda s: (0, 0)),
                  pl.BlockSpec((late, 1, LANES), lambda s: (0, 0, 0))],
        out_specs=window,
        scratch_shapes=[pltpu.VMEM((late * cap, ncomp * nr), bf16),
                        pltpu.VMEM((late * cap, ncomp * nr), bf16),
                        pltpu.VMEM((1, late * cap), f32)],
        compiler_params=pltpu.CompilerParams(vmem_limit_bytes=24 << 20),
        name="settle",
    )(base, got.reshape(late * cap, ncomp * nr), gcell)


def on_device(n_ax, n_az, velocity, viscosity, force, area, adjacency, crossing, cell):
    n, depth, group_n = n_ax * n_az, n_az // 4, 2 * n_ax
    ncomp, pan, nr = force.shape
    na, nt = velocity.shape[1:3]
    most = max(2, 2 * pan // n)
    cap = -(-most // 8) * 8
    keep = -(-(3 * min(pan, group_n * most)) // 64) * 16
    half = n // 2
    f32, bf16, i32 = jnp.float32, jnp.bfloat16, jnp.int32
    any_ = pl.BlockSpec(memory_space=pl.ANY)
    hbm = pl.BlockSpec(memory_space=pltpu.HBM)
    vmem = pl.BlockSpec(memory_space=pltpu.VMEM)
    dma = pltpu.SemaphoreType.DMA
    inputs = (velocity, viscosity, force, crossing.reshape(1, pan), cell.reshape(1, pan),
              area.reshape(1, pan), adjacency.T)
    inputs = [pltpu.with_memory_space_constraint(x, pltpu.HBM) for x in inputs]
    base, got, landing, flag = pl.pallas_call(
        functools.partial(exchange_packed, n_ax, n_az, cap, keep),
        out_shape=(jax.ShapeDtypeStruct(velocity.shape, f32),
                   jax.ShapeDtypeStruct((ncomp, half, cap, nr), f32),
                   jax.ShapeDtypeStruct((na * nt, half * cap), bf16),
                   jax.ShapeDtypeStruct((1, LANES), f32)),
        in_specs=[hbm] * 7,
        out_specs=(any_, any_, vmem, vmem),
        scratch_shapes=[
            pltpu.VMEM((1, pan), i32), pltpu.VMEM((1, pan), i32),
            pltpu.VMEM((1, pan), f32), pltpu.VMEM((4, pan), i32),
            pltpu.VMEM((ncomp, na + 2, nt, nr), f32),
            pltpu.VMEM((na + 2, nt, nr), f32),
            pltpu.VMEM((ncomp, pan + 2 * HALO, nr), f32),
            pltpu.VMEM((ncomp, pan + 2 * HALO, nr), bf16),
            pltpu.VMEM((ncomp, pan + 2 * HALO, nr), bf16),
            pltpu.VMEM((half, cap, ncomp * nr), f32),
            pltpu.VMEM((n, 1, LANES), f32),
            pltpu.VMEM((2, ncomp + 1, na, nr), f32),
            pltpu.VMEM((2, ncomp + 1, na, nr), f32),
            pltpu.VMEM((ncomp, na, nt, nr), f32),
            pltpu.VMEM((half, cap, ncomp * nr), f32),
            pltpu.VMEM((half, 1, LANES), f32),
            pltpu.VMEM((half, 1, LANES), f32),
            pltpu.VMEM((half * cap, ncomp * nr), bf16),
            pltpu.VMEM((half * cap, ncomp * nr), bf16),
            pltpu.VMEM((ncomp, depth, keep, nr), f32),
            pltpu.VMEM((ncomp, depth, keep, nr), f32),
            pltpu.VMEM((depth, 1, LANES), f32),
            pltpu.VMEM((depth, 1, LANES), f32),
            pltpu.VMEM((ncomp, half, cap, nr), f32),
            pltpu.VMEM((na * nt, half * cap), bf16),
            dma((7,)), dma((8,)), dma((8,)), dma((half,)), dma((half,)), dma((n,)), dma((n,)),
            dma((2,)), dma((na,)),
            dma((ncomp, depth)), dma((ncomp, depth)), dma((depth,)), dma((depth,)),
            dma((ncomp * half,)), dma((ncomp * half,)), dma((ncomp * depth,)),
        ],
        compiler_params=pltpu.CompilerParams(collective_id=0, has_side_effects=True,
                                             vmem_limit_bytes=44 << 20),
        name="exchange_packed",
    )(*inputs)
    def finish(base, got, landing, *inputs):
        return pl.pallas_call(
            settle_packed,
            out_shape=jax.ShapeDtypeStruct(velocity.shape, f32),
            in_specs=[vmem, vmem, vmem],
            out_specs=hbm,
            scratch_shapes=[pltpu.VMEM((ncomp, na, nt, nr), f32), dma((2 * ncomp,))],
            compiler_params=pltpu.CompilerParams(vmem_limit_bytes=52 << 20),
            name="settle_packed",
        )(base, got.reshape(ncomp, half * cap, nr), landing)

    def again(base, got, landing, *inputs):
        return direct(n_ax, n_az, cap, *inputs)

    return lax.cond(flag[0, 0] > 0.5, again, finish, base, got, landing, *inputs)


def solution(mesh):
    n_ax, n_az = mesh.shape["ax"], mesh.shape["az"]
    in_specs = (
        P(None, "ax", "az", None),
        P("ax", "az", None),
        P(None, ("ax", "az"), None),
        P(("ax", "az")),
        P(("ax", "az"), None),
        P(("ax", "az"), None),
        P(("ax", "az")),
    )
    return jax.shard_map(
        functools.partial(on_device, n_ax, n_az), mesh=mesh, in_specs=in_specs,
        out_specs=P(None, "ax", "az", None), check_vma=False)
```

```python
import functools

import jax
import jax.numpy as jnp
from jax import lax
from jax.experimental import pallas as pl
from jax.experimental.pallas import tpu as pltpu
from jax.sharding import PartitionSpec as P

HALO = 32
LANES = 128

step_size = 0.1
coupling = 0.2


def split(x):
    hi = x.astype(jnp.bfloat16)
    lo = (x - hi.astype(jnp.float32)).astype(jnp.bfloat16)
    return hi, lo


def dot(a, b):
    return jnp.dot(a, b, preferred_element_type=jnp.float32)


def wide_row(cells, cap):
    m = cells.shape[0]
    slots = m * cap
    big = jnp.floor((cells + 1.0) * (1.0 / 64.0))
    small = (cells + 1.0) - 64.0 * big
    spread = (lax.broadcasted_iota(jnp.int32, (LANES, slots), 0)
              == lax.rem(lax.broadcasted_iota(jnp.int32, (LANES, slots), 1), cap))
    spread = spread.astype(jnp.float32).astype(jnp.bfloat16)
    wide = 64.0 * dot(big.astype(jnp.bfloat16), spread) + dot(small.astype(jnp.bfloat16), spread)
    mine = (lax.broadcasted_iota(jnp.int32, (m, slots), 0)
            == lax.broadcasted_iota(jnp.int32, (m, slots), 1) // cap)
    return jnp.sum(jnp.where(mine, wide, 0.0), axis=0, keepdims=True) - 1.0


def landing_of(crow, first, count):
    here = lax.broadcasted_iota(jnp.int32, (count, crow.shape[1]), 0) + first
    return (crow.astype(jnp.int32) == here).astype(jnp.float32).astype(jnp.bfloat16)


def exchange(n_ax, n_az, cap, vel, visc, force, dest_h, cell_h, area_h, adj_h, base, got, gcell,
             dest_i, cell_i, area, adj_i,
             velx, viscx, ext, exthi, extlo, send, scell, edges, edge_in, acc,
             tiles, tcell, thi, tlo,
             load_sem, halo_send, halo_recv, tile_send, tile_recv,
             cell_send, cell_recv, own_sem, out_sem):
    n, half_n = n_ax * n_az, n_az // 2
    ax, az = lax.axis_index("ax"), lax.axis_index("az")
    me = ax * n_az + az
    half, spot = az // half_n, lax.rem(az, half_n)
    ncomp, na, nt, nr = vel.shape
    pan = force.shape[1]
    slots = n * cap
    f32, bf16 = jnp.float32, jnp.bfloat16

    def place(linear):
        return (linear // n_az, lax.rem(linear, n_az))

    def remote(src, dst, ssem, rsem, device):
        return pltpu.make_async_remote_copy(
            src_ref=src, dst_ref=dst, send_sem=ssem, recv_sem=rsem,
            device_id=device, device_id_type=pl.DeviceIdType.MESH)

    barrier = pltpu.get_barrier_semaphore()

    def greet(k, carry):
        pl.semaphore_signal(barrier, inc=1, device_id=place(lax.rem(me + k, n)),
                            device_id_type=pl.DeviceIdType.MESH)
        return carry

    lax.fori_loop(1, n, greet, 0)
    small = [pltpu.make_async_copy(src, dst, load_sem.at[3 + k]) for k, (src, dst) in enumerate(
        [(dest_h, dest_i), (cell_h, cell_i), (adj_h, adj_i), (area_h, area)])]
    loads = [
        pltpu.make_async_copy(force, ext.at[:, pl.ds(HALO, pan)], load_sem.at[0]),
        pltpu.make_async_copy(vel, velx.at[:, pl.ds(1, na)], load_sem.at[1]),
        pltpu.make_async_copy(visc, viscx.at[pl.ds(1, na)], load_sem.at[2]),
    ]
    for c in small + loads:
        c.start()

    pl.semaphore_wait(barrier, n - 1)

    up, down = place(lax.rem(me + 1, n)), place(lax.rem(me + n - 1, n))
    ax_up, ax_down = lax.rem(ax + 1, n_ax), lax.rem(ax + n_ax - 1, n_ax)
    az_up, az_down = lax.rem(az + 1, n_az), lax.rem(az + n_az - 1, n_az)

    def halo(i, src, dst, device):
        return remote(src, dst, halo_send.at[i], halo_recv.at[i], device)

    fhalo = [
        halo(0, force.at[:, pl.ds(pan - HALO, HALO)], ext.at[:, pl.ds(0, HALO)], up),
        halo(1, force.at[:, pl.ds(0, HALO)], ext.at[:, pl.ds(HALO + pan, HALO)], down),
    ]
    ahalo = [
        halo(2, vel.at[:, na - 1], velx.at[:, 0], (ax_up, az)),
        halo(3, vel.at[:, 0], velx.at[:, na + 1], (ax_down, az)),
        halo(4, visc.at[na - 1], viscx.at[0], (ax_up, az)),
        halo(5, visc.at[0], viscx.at[na + 1], (ax_down, az)),
    ]
    zhalo = [
        halo(6, edges.at[1], edge_in.at[0], (ax, az_up)),
        halo(7, edges.at[0], edge_in.at[1], (ax, az_down)),
    ]
    for c in fhalo:
        c.start()
    for c in small:
        c.wait()

    dest_row, cell_row = dest_i[...].astype(f32), cell_i[...].astype(f32)
    adj = (adj_i[...] - (me * pan - HALO)).astype(f32)
    rows = jnp.concatenate([dest_row, cell_row, adj, dest_row, dest_row], axis=0)
    cols = rows.T
    dest_col, cell_col = cols[:, 0:1], cols[:, 1:2]
    same = dest_col == dest_row
    r0 = lax.broadcasted_iota(jnp.int32, (pan, pan), 0)
    r1 = lax.broadcasted_iota(jnp.int32, (pan, pan), 1)
    rank_row = jnp.sum((same & (r0 < r1)).astype(f32), axis=0, keepdims=True)
    rank_col = jnp.sum((same & (r1 < r0)).astype(f32), axis=1, keepdims=True)
    dax = jnp.floor(dest_row * (1.0 / n_az))
    daz = dest_row - n_az * dax
    dhalf = jnp.floor(daz * (1.0 / half_n))
    turn = dax - ax.astype(f32)
    turn = jnp.where(turn < 0.0, turn + n_ax, turn)
    group = turn + jnp.where(dhalf == half.astype(f32), 0.0, float(n_ax))
    peer = group * half_n + (daz - half_n * dhalf)
    target = (peer * cap + rank_row).astype(jnp.int32)
    hits = lax.broadcasted_iota(jnp.int32, (slots, pan), 0) == target
    scale = jnp.sum(jnp.where(hits, coupling * area[...], 0.0), axis=1, keepdims=True)
    q = lax.broadcasted_iota(jnp.int32, (pan, pan + 2 * HALO), 1).astype(f32)
    p = lax.broadcasted_iota(jnp.int32, (pan, pan + 2 * HALO), 0).astype(f32)
    count = (q == p + HALO).astype(f32)
    for k in range(4):
        count = count + (q == cols[:, 2 + k:3 + k]).astype(f32)
    pick = dot(hits.astype(f32).astype(bf16), count.astype(bf16)).astype(bf16)

    loads[1].wait()
    loads[2].wait()
    for c in range(ncomp):
        edges[0, c] = velx[c, 1:na + 1, 0, :]
        edges[1, c] = velx[c, 1:na + 1, nt - 1, :]
    edges[0, ncomp] = viscx[1:na + 1, 0, :]
    edges[1, ncomp] = viscx[1:na + 1, nt - 1, :]

    for c in zhalo + ahalo:
        c.start()

    big = jnp.floor((cell_col + 1.0) * (1.0 / 64.0))
    small = (cell_col + 1.0) - 64.0 * big
    at_rank = lax.broadcasted_iota(jnp.int32, (pan, LANES), 1).astype(f32) == rank_col
    owner = lax.broadcasted_iota(jnp.int32, (n, pan), 0).astype(f32) == peer
    owner = owner.astype(f32).astype(bf16)
    cells = (64.0 * dot(owner, jnp.where(at_rank, big, 0.0).astype(bf16))
             + dot(owner, jnp.where(at_rank, small, 0.0).astype(bf16)) - 1.0)
    for d in range(n):
        scell[d] = cells[d:d + 1, :]

    def split_force(lo_row, hi_row):
        h, l = split(ext[:, lo_row:hi_row])
        exthi[:, lo_row:hi_row] = h
        extlo[:, lo_row:hi_row] = l

    loads[0].wait()
    split_force(HALO, HALO + pan)
    for c in fhalo:
        c.wait()
    split_force(0, HALO)
    split_force(HALO + pan, pan + 2 * HALO)

    def tiles_to(g, i):
        there = lax.rem(spot + i, half_n)
        side = half if g < n_ax else 1 - half
        device = (lax.rem(ax + g % n_ax, n_ax), side * half_n + there)
        src, k = g * half_n + there, g * half_n + i
        at = (g % n_ax) * half_n + spot
        tile_at, cell_at = (tiles, tcell) if g < n_ax else (got, gcell)
        return (remote(send.at[src], tile_at.at[at], tile_send.at[k], tile_recv.at[k], device),
                remote(scell.at[src], cell_at.at[at], cell_send.at[k], cell_recv.at[k], device))

    def each_tile(groups, act):
        for g in groups:
            def body(i, carry):
                for c in tiles_to(g, i):
                    act(c)
                return carry
            lax.fori_loop(1 if g == 0 else 0, half_n, body, 0)

    for part in range(2):
        r = slice(part * (slots // 2), (part + 1) * (slots // 2))
        for c in range(ncomp):
            tile = (dot(pick[r], exthi[c]) + dot(pick[r], extlo[c])) * scale[r]
            send[part * (n // 2):(part + 1) * (n // 2), :, c * nr:(c + 1) * nr] = (
                tile.reshape(n // 2, cap, nr))
        each_tile(range(part * n_ax, (part + 1) * n_ax), lambda c: c.start())
    own = [pltpu.make_async_copy(send.at[spot], tiles.at[spot], own_sem.at[0]),
           pltpu.make_async_copy(scell.at[spot], tcell.at[spot], own_sem.at[1])]
    for c in own:
        c.start()

    for c in ahalo + zhalo:
        c.wait()

    @pl.when(ax == 0)
    def _():
        velx[:, 0] = jnp.zeros((ncomp, nt, nr), f32)
        viscx[0] = jnp.zeros((nt, nr), f32)

    @pl.when(ax == n_ax - 1)
    def _():
        velx[:, na + 1] = jnp.zeros((ncomp, nt, nr), f32)
        viscx[na + 1] = jnp.zeros((nt, nr), f32)

    row_id = lax.broadcasted_iota(jnp.int32, (nt, nr), 0)
    lane_id = lax.broadcasted_iota(jnp.int32, (nt, nr), 1)

    def neighbours(x, low, high):
        left = jnp.where(row_id == 0, low, pltpu.roll(x, 1, 0))
        right = jnp.where(row_id == nt - 1, high, pltpu.roll(x, nt - 1, 0))
        inner = jnp.where(lane_id == 0, 0.0, pltpu.roll(x, 1, 1))
        outer = jnp.where(lane_id == nr - 1, 0.0, pltpu.roll(x, nr - 1, 1))
        return left, right, inner, outer

    def plane(i, carry):
        mu = viscx[i + 1]
        sides = neighbours(mu, edge_in[0, ncomp, pl.ds(i, 1), :], edge_in[1, ncomp, pl.ds(i, 1), :])
        faces = [mu + s for s in (viscx[i], viscx[i + 2]) + sides]
        for c in range(ncomp):
            f = velx[c, i + 1]
            near = neighbours(f, edge_in[0, c, pl.ds(i, 1), :], edge_in[1, c, pl.ds(i, 1), :])
            near = (velx[c, i], velx[c, i + 2]) + near
            total = faces[0] * (near[0] - f)
            for w, g in zip(faces[1:], near[1:]):
                total = total + w * (g - f)
            acc[c, i] = f + (0.5 * step_size) * total
        return carry

    lax.fori_loop(0, na, plane, 0)

    for c in own:
        c.wait()
    each_tile(range(n_ax), lambda c: c.wait())
    h, l = split(tiles[...].reshape(-1, ncomp * nr))
    thi[...] = h
    tlo[...] = l
    crow = wide_row(tcell[...].reshape(-1, LANES), cap)
    blk = max(1, 256 // nt)

    def stored(j):
        return pltpu.make_async_copy(acc.at[:, pl.ds(j * blk, blk)],
                                     base.at[:, pl.ds(j * blk, blk)], out_sem.at[j])

    for j in range(na // blk):
        landing = landing_of(crow, j * blk * nt, blk * nt)
        for c in range(ncomp):
            cs = slice(c * nr, (c + 1) * nr)
            deposit = dot(landing, thi[:, cs]) + dot(landing, tlo[:, cs])
            acc[c, j * blk:(j + 1) * blk] += deposit.reshape(blk, nt, nr)
        stored(j).start()
    for j in range(na // blk):
        stored(j).wait()
    each_tile(range(n_ax, 2 * n_ax), lambda c: c.wait())


def exchange_packed(n_ax, n_az, cap, keep, extra, vel, visc, force, dest_h, cell_h, area_h, adj_h,
                    base, got, landing, flag,
                    dest_i, cell_i, area, adj_i,
                    velx, viscx, ext, exthi, extlo, send, scell, edges, edge_in, acc,
                    tiles, tcell, fcell, thi, tlo, pack, share, packed, smeta, rmeta, sorted_, near_at, relay,
                    load_sem, halo_send, halo_recv, tile_send, tile_recv,
                    cell_send, cell_recv, own_sem, out_sem,
                    pack_send, pack_recv, meta_send, meta_recv, hop_send, hop_recv, hop_own,
                    share_send, share_recv, pass_send):
    n, half_n = n_ax * n_az, n_az // 2
    depth, group_n = half_n // 2, 2 * n_ax
    ax, az = lax.axis_index("ax"), lax.axis_index("az")
    me = ax * n_az + az
    half, spot = az // half_n, lax.rem(az, half_n)
    zpos, core = spot // 2, lax.rem(az, 2)
    seat = ax * 2 + core
    ncomp, na, nt, nr = vel.shape
    pan = force.shape[1]
    near = (n // 2) * cap
    slots = near + depth * keep + extra
    both = keep + extra
    detour = n_ax == 4
    f32, bf16 = jnp.float32, jnp.bfloat16

    def place(linear):
        return (linear // n_az, lax.rem(linear, n_az))

    def remote(src, dst, ssem, rsem, device):
        return pltpu.make_async_remote_copy(
            src_ref=src, dst_ref=dst, send_sem=ssem, recv_sem=rsem,
            device_id=device, device_id_type=pl.DeviceIdType.MESH)

    barrier = pltpu.get_barrier_semaphore()

    def greet(k, carry):
        pl.semaphore_signal(barrier, inc=1, device_id=place(lax.rem(me + k, n)),
                            device_id_type=pl.DeviceIdType.MESH)
        return carry

    lax.fori_loop(1, n, greet, 0)
    small = [pltpu.make_async_copy(src, dst, load_sem.at[3 + k]) for k, (src, dst) in enumerate(
        [(dest_h, dest_i), (cell_h, cell_i), (adj_h, adj_i), (area_h, area)])]
    loads = [
        pltpu.make_async_copy(force, ext.at[:, pl.ds(HALO, pan)], load_sem.at[0]),
        pltpu.make_async_copy(vel, velx.at[:, pl.ds(1, na)], load_sem.at[1]),
        pltpu.make_async_copy(visc, viscx.at[pl.ds(1, na)], load_sem.at[2]),
    ]
    for c in small + loads:
        c.start()

    for c in small:
        c.wait()

    dest_row, cell_row = dest_i[...].astype(f32), cell_i[...].astype(f32)
    adj = (adj_i[...] - (me * pan - HALO)).astype(f32)
    rows = jnp.concatenate([dest_row, cell_row, adj, dest_row, dest_row], axis=0)
    cols = rows.T
    dest_col, cell_col = cols[:, 0:1], cols[:, 1:2]
    same = dest_col == dest_row
    r0 = lax.broadcasted_iota(jnp.int32, (pan, pan), 0)
    r1 = lax.broadcasted_iota(jnp.int32, (pan, pan), 1)
    rank_row = jnp.sum((same & (r0 < r1)).astype(f32), axis=0, keepdims=True)
    rank_col = jnp.sum((same & (r1 < r0)).astype(f32), axis=1, keepdims=True)

    pl.semaphore_wait(barrier, n - 1)

    up, down = place(lax.rem(me + 1, n)), place(lax.rem(me + n - 1, n))
    ax_up, ax_down = lax.rem(ax + 1, n_ax), lax.rem(ax + n_ax - 1, n_ax)
    az_up, az_down = lax.rem(az + 1, n_az), lax.rem(az + n_az - 1, n_az)

    def halo(i, src, dst, device):
        return remote(src, dst, halo_send.at[i], halo_recv.at[i], device)

    fhalo = [
        halo(0, force.at[:, pl.ds(pan - HALO, HALO)], ext.at[:, pl.ds(0, HALO)], up),
        halo(1, force.at[:, pl.ds(0, HALO)], ext.at[:, pl.ds(HALO + pan, HALO)], down),
    ]
    top, bottom, below, above = na - 1, 0, 0, na + 1
    ahalo = [
        halo(2, vel.at[:, top], velx.at[:, below], (ax_up, az)),
        halo(3, vel.at[:, bottom], velx.at[:, above], (ax_down, az)),
        halo(4, visc.at[top], viscx.at[below], (ax_up, az)),
        halo(5, visc.at[bottom], viscx.at[above], (ax_down, az)),
    ]
    first, final = pl.ds(0, ncomp - 1), ncomp - 1

    def halves(src, dst, to, via):
        i = 2 if dst == below else 3
        return [halo(i, vel.at[first, src], velx.at[first, dst], (to, az)),
                halo(8, vel.at[final, src], relay.at[0], (via, az)),
                halo(9, visc.at[src], relay.at[1], (via, az))]

    def passed(dst, to):
        return [halo(10, relay.at[0], velx.at[final, dst], (to, az)),
                halo(11, relay.at[1], viscx.at[dst], (to, az))]

    even = lax.rem(ax, 2) == 0

    def start_ahalo():
        if not detour:
            for c in ahalo:
                c.start()
            return

        @pl.when(even)
        def _():
            ahalo[0].start()
            ahalo[2].start()

        @pl.when(jnp.logical_not(even))
        def _():
            ahalo[1].start()
            ahalo[3].start()

        @pl.when(ax == 1)
        def _():
            for c in halves(top, below, 2, 3):
                c.start()

        @pl.when(ax == 2)
        def _():
            for c in halves(bottom, above, 1, 0):
                c.start()

    def pass_on():
        if not detour:
            return

        @pl.when(ax == 3)
        def _():
            for c in halves(top, below, 2, 3)[1:]:
                c.wait_recv()
            for c in passed(below, 2):
                c.start()

        @pl.when(ax == 0)
        def _():
            for c in halves(bottom, above, 1, 0)[1:]:
                c.wait_recv()
            for c in passed(above, 1):
                c.start()

    def wait_ahalo():
        if not detour:
            for c in ahalo:
                c.wait()
            return

        @pl.when(even)
        def _():
            for c in (ahalo[0], ahalo[2]):
                c.wait_send()
            for c in (ahalo[1], ahalo[3]):
                c.wait_recv()

        @pl.when(jnp.logical_not(even))
        def _():
            for c in (ahalo[1], ahalo[3]):
                c.wait_send()
            for c in (ahalo[0], ahalo[2]):
                c.wait_recv()

        @pl.when(ax == 1)
        def _():
            for c in halves(top, below, 2, 3):
                c.wait_send()
            halves(bottom, above, 1, 0)[0].wait_recv()
            for c in passed(above, 1):
                c.wait_recv()

        @pl.when(ax == 2)
        def _():
            for c in halves(bottom, above, 1, 0):
                c.wait_send()
            halves(top, below, 2, 3)[0].wait_recv()
            for c in passed(below, 2):
                c.wait_recv()

        @pl.when(ax == 3)
        def _():
            for c in passed(below, 2):
                c.wait_send()

        @pl.when(ax == 0)
        def _():
            for c in passed(above, 1):
                c.wait_send()

    zhalo = [
        halo(6, edges.at[1], edge_in.at[0], (ax, az_up)),
        halo(7, edges.at[0], edge_in.at[1], (ax, az_down)),
    ]
    for c in fhalo:
        c.start()
    start_ahalo()
    def layer_of(dest):
        inner = dest - n_az * jnp.floor(dest * (1.0 / n_az))
        return jnp.floor(inner * 0.5)

    dax = jnp.floor(dest_row * (1.0 / n_az))
    daz = dest_row - n_az * dax
    dhalf = jnp.floor(daz * (1.0 / half_n))
    layer_row, layer_col = layer_of(dest_row), layer_of(dest_col)
    pos_row = jnp.sum(((layer_col == layer_row) & (r0 < r1)).astype(f32), axis=0, keepdims=True)
    turn = dax - ax.astype(f32)
    turn = jnp.where(turn < 0.0, turn + n_ax, turn)
    far = dhalf != half.astype(f32)
    group = turn + jnp.where(far, float(n_ax), 0.0)
    peer = group * half_n + (daz - half_n * dhalf)
    dz = (layer_row - depth * dhalf) - zpos.astype(f32)
    dz = jnp.where(dz < 0.0, dz + depth, dz)
    pos_col = jnp.sum(((layer_col == layer_row) & (r1 < r0)).astype(f32), axis=1, keepdims=True)
    far_col = jnp.floor(layer_col * (1.0 / depth)) != half.astype(f32)
    over_col = far_col & (pos_col >= keep)
    order = jnp.sum((over_col & (r0 < r1)).astype(f32), axis=0, keepdims=True)
    over = far & (pos_row >= keep)
    spilled = over & (order >= extra)
    target = jnp.where(far, near + dz * keep + pos_row, peer * cap + rank_row)
    target = jnp.where(over, near + depth * keep + order, target)
    target = jnp.where(spilled, -1.0, target).astype(jnp.int32)
    spill = jnp.max(jnp.where(spilled, 1.0, 0.0), axis=1, keepdims=True)
    hits = lax.broadcasted_iota(jnp.int32, (slots, pan), 0) == target
    scale = jnp.sum(jnp.where(hits, coupling * area[...], 0.0), axis=1, keepdims=True)
    q = lax.broadcasted_iota(jnp.int32, (pan, pan + 2 * HALO), 1).astype(f32)
    p = lax.broadcasted_iota(jnp.int32, (pan, pan + 2 * HALO), 0).astype(f32)
    count = (q == p + HALO).astype(f32)
    for k in range(4):
        count = count + (q == cols[:, 2 + k:3 + k]).astype(f32)
    hits = hits.astype(f32).astype(bf16)
    pick = dot(hits, count.astype(bf16)).astype(bf16)
    slot = (dax * 2.0 + (daz - 2.0 * layer_row)) * cap + rank_row + 1.0
    sbig = jnp.floor(slot * (1.0 / 64.0))
    digits = jnp.concatenate([sbig, slot - 64.0 * sbig] * 4, axis=0)
    for j in range(depth):
        at = near + j * keep
        holds = jnp.concatenate([hits[at:at + keep], hits[near + depth * keep:]], axis=0)
        found = lax.dot_general(jnp.where(dz == j, digits, 0.0).astype(bf16), holds,
                                (((1,), (1,)), ((), ())), preferred_element_type=f32)
        smeta[j] = jnp.full(smeta.shape[1:], -1.0, f32)
        smeta[j, :, 0:both] = 64.0 * found[0:1] + found[1:2] - 1.0

    loads[1].wait()
    loads[2].wait()
    for c in range(ncomp):
        edges[0, c] = velx[c, 1:na + 1, 0, :]
        edges[1, c] = velx[c, 1:na + 1, nt - 1, :]
    edges[0, ncomp] = viscx[1:na + 1, 0, :]
    edges[1, ncomp] = viscx[1:na + 1, nt - 1, :]
    for c in zhalo:
        c.start()

    big = jnp.floor((cell_col + 1.0) * (1.0 / 64.0))
    small_digit = (cell_col + 1.0) - 64.0 * big
    at_rank = lax.broadcasted_iota(jnp.int32, (pan, LANES), 1).astype(f32) == rank_col
    owner = lax.broadcasted_iota(jnp.int32, (n, pan), 0).astype(f32) == peer
    owner = owner.astype(f32).astype(bf16)
    cells = (64.0 * dot(owner, jnp.where(at_rank, big, 0.0).astype(bf16))
             + dot(owner, jnp.where(at_rank, small_digit, 0.0).astype(bf16)) - 1.0)
    last = lax.broadcasted_iota(jnp.int32, (n, LANES), 1) == LANES - 1
    cells = jnp.where(last, spill, cells)
    for d in range(n):
        scell[d] = cells[d:d + 1, :]

    def split_force(lo_row, hi_row):
        h, l = split(ext[:, lo_row:hi_row])
        exthi[:, lo_row:hi_row] = h
        extlo[:, lo_row:hi_row] = l

    loads[0].wait()
    split_force(HALO, HALO + pan)
    for c in fhalo:
        c.wait()
    split_force(0, HALO)
    split_force(HALO + pan, pan + 2 * HALO)

    def picked(c, lo_row, hi_row):
        r = slice(lo_row, hi_row)
        return (dot(pick[r], exthi[c]) + dot(pick[r], extlo[c])) * scale[r]

    def cells_to(g, i):
        there = lax.rem(spot + i, half_n)
        side = half if g < n_ax else 1 - half
        device = (lax.rem(ax + g % n_ax, n_ax), side * half_n + there)
        src, k = g * half_n + there, g * half_n + i
        if g < n_ax:
            cell_at = tcell.at[g * half_n + spot]
        else:
            cell_at = fcell.at[lax.rem(there // 2 - zpos + depth, depth) * group_n + seat]
        return remote(scell.at[src], cell_at, cell_send.at[k], cell_recv.at[k], device)

    def tiles_to(g, i):
        there = lax.rem(spot + i, half_n)
        device = (lax.rem(ax + g, n_ax), half * half_n + there)
        src, k = g * half_n + there, g * half_n + i
        return remote(send.at[src], tiles.at[g * half_n + spot], tile_send.at[k],
                      tile_recv.at[k], device)

    def each(copy, groups, act):
        for g in groups:
            def body(i, carry):
                act(copy(g, i))
                return carry
            lax.fori_loop(1 if g == 0 else 0, half_n, body, 0)

    def along(j):
        return (ax, ((1 - half) * depth + lax.rem(zpos + j, depth)) * 2 + core)

    metas = [remote(smeta.at[j], rmeta.at[j], meta_send.at[j], meta_recv.at[j], along(j))
             for j in range(depth)]
    packs = [[remote(pack.at[c, j], packed.at[c, j, pl.ds(0, keep)], pack_send.at[c, j], pack_recv.at[c, j],
                     along(j)) for j in range(depth)] for c in range(ncomp)]

    def entry(side):
        return jnp.where(side == 1, 0, depth - 1)

    at_gate = lax.rem(entry(1 - half) - zpos + depth, depth)
    shares = [remote(share.at[c], packed.at[c, at_gate, pl.ds(keep, extra)], share_send.at[c],
                     share_recv.at[c, at_gate], along(at_gate)) for c in range(ncomp)]
    gate = zpos == entry(half)

    def spread(c, j, d):
        there = lax.rem(zpos + d, depth)
        k = (j + d) % depth
        return remote(packed.at[c, j, pl.ds(keep, extra)], packed.at[c, k, pl.ds(keep, extra)],
                      pass_send.at[c, j, d], share_recv.at[c, k],
                      (ax, (half * depth + there) * 2 + core))

    def shared_in(c, j):
        return remote(share.at[c], packed.at[c, j, pl.ds(keep, extra)], share_send.at[c],
                      share_recv.at[c, j], along(j))

    def spread_shares(c):
        @pl.when(gate)
        def _():
            for j in range(depth):
                shared_in(c, j).wait_recv()
                for d in range(1, depth):
                    spread(c, j, d).start()

    def start_packs():
        for c in range(ncomp):
            share[c] = picked(c, near + depth * keep, slots)
            shares[c].start()
        for c in range(ncomp):
            for j in range(depth):
                at = near + j * keep
                pack[c, j] = picked(c, at, at + keep)
                packs[c][j].start()

    for c in metas:
        c.start()
    each(cells_to, range(2 * n_ax), lambda c: c.start())
    for c in range(ncomp):
        send[:, :, c * nr:(c + 1) * nr] = picked(c, 0, near).reshape(n // 2, cap, nr)
    each(tiles_to, range(n_ax), lambda c: c.start())
    start_packs()
    own = [pltpu.make_async_copy(send.at[spot], tiles.at[spot], own_sem.at[0]),
           pltpu.make_async_copy(scell.at[spot], tcell.at[spot], own_sem.at[1])]
    for c in own:
        c.start()

    pass_on()
    for c in zhalo:
        c.wait()

    row_id = lax.broadcasted_iota(jnp.int32, (nt, nr), 0)
    lane_id = lax.broadcasted_iota(jnp.int32, (nt, nr), 1)

    def neighbours(x, low, high):
        left = jnp.where(row_id == 0, low, pltpu.roll(x, 1, 0))
        right = jnp.where(row_id == nt - 1, high, pltpu.roll(x, nt - 1, 0))
        inner = jnp.where(lane_id == 0, 0.0, pltpu.roll(x, 1, 1))
        outer = jnp.where(lane_id == nr - 1, 0.0, pltpu.roll(x, nr - 1, 1))
        return left, right, inner, outer

    def plane(i, carry):
        mu = viscx[i + 1]
        sides = neighbours(mu, edge_in[0, ncomp, pl.ds(i, 1), :], edge_in[1, ncomp, pl.ds(i, 1), :])
        faces = [mu + s for s in (viscx[i], viscx[i + 2]) + sides]
        for c in range(ncomp):
            f = velx[c, i + 1]
            sides_f = neighbours(f, edge_in[0, c, pl.ds(i, 1), :], edge_in[1, c, pl.ds(i, 1), :])
            sides_f = (velx[c, i], velx[c, i + 2]) + sides_f
            total = faces[0] * (sides_f[0] - f)
            for w, g in zip(faces[1:], sides_f[1:]):
                total = total + w * (g - f)
            acc[c, i] = f + (0.5 * step_size) * total
        return carry

    lax.fori_loop(1, na - 1, plane, 0)
    for c in range(ncomp):
        spread_shares(c)

    def hop(c, j, k):
        there = lax.rem(seat + k, group_n)
        device = (there // 2, (half * depth + zpos) * 2 + lax.rem(there, 2))
        return remote(sorted_.at[c, j * group_n + there], arrival(c, j),
                      hop_send.at[(c * depth + j) * group_n + k],
                      hop_recv.at[(c * depth + j) * group_n + k], device)

    def arrival(c, j):
        return got.at[c, j * group_n + seat]

    def each_hop(c, j, act):
        def body(k, carry):
            act(hop(c, j, k))
            return carry
        lax.fori_loop(1, group_n, body, 0)

    def hop_mine(c, j):
        return pltpu.make_async_copy(sorted_.at[c, j * group_n + seat], arrival(c, j),
                                     hop_own.at[c * depth + j])

    for c in metas:
        c.wait()
    sorter = [(rmeta[j, :, 0:both].astype(jnp.int32)
               == lax.broadcasted_iota(jnp.int32, (group_n * cap, both), 0)
               ).astype(f32).astype(bf16) for j in range(depth)]

    def forward(c):
        for j in range(depth):
            packs[c][j].wait_recv()

            @pl.when(jnp.logical_not(gate))
            def _():
                shared_in(c, j).wait_recv()

            h, l = split(packed[c, j])
            sorted_[c, j * group_n:(j + 1) * group_n] = (
                dot(sorter[j], h) + dot(sorter[j], l)).reshape(group_n, cap, nr)
            each_hop(c, j, lambda x: x.start())
            hop_mine(c, j).start()

    def landed(c):
        for j in range(depth):
            each_hop(c, j, lambda x: x.wait())
            hop_mine(c, j).wait()

    def add(c, where, h, l):
        for m in range(2):
            rows = slice(m * (na // 2) * nt, (m + 1) * (na // 2) * nt)
            total = dot(where[rows], h) + dot(where[rows], l)
            acc[c, m * (na // 2):(m + 1) * (na // 2)] += total.reshape(na // 2, nt, nr)

    def stored(c):
        return pltpu.make_async_copy(acc.at[c], base.at[c], out_sem.at[c])

    forward(0)

    wait_ahalo()

    @pl.when(ax == 0)
    def _():
        velx[:, 0] = jnp.zeros((ncomp, nt, nr), f32)
        viscx[0] = jnp.zeros((nt, nr), f32)

    @pl.when(ax == n_ax - 1)
    def _():
        velx[:, na + 1] = jnp.zeros((ncomp, nt, nr), f32)
        viscx[na + 1] = jnp.zeros((nt, nr), f32)

    lax.fori_loop(0, 2, lambda i, carry: plane(i * (na - 1), carry), 0)

    for c in own:
        c.wait()
    each(tiles_to, range(n_ax), lambda c: c.wait())
    each(cells_to, range(n_ax), lambda c: c.wait())
    h, l = split(tiles[...].reshape(-1, ncomp * nr))
    thi[...] = h
    tlo[...] = l
    near_at[...] = landing_of(wide_row(tcell[...].reshape(-1, LANES), cap), 0, na * nt)
    for c in range(ncomp):
        add(c, near_at, thi[:, c * nr:(c + 1) * nr], tlo[:, c * nr:(c + 1) * nr])
        stored(c).start()

    for c in range(1, ncomp):
        forward(c)
    each(cells_to, range(n_ax, 2 * n_ax), lambda c: c.wait())
    landing[...] = landing_of(wide_row(fcell[...].reshape(-1, LANES), cap), 0, na * nt)
    said = jnp.maximum(tcell[...].reshape(-1, LANES), fcell[...].reshape(-1, LANES))
    said = jnp.where(last[0:n // 2], said, 0.0)
    flag[...] = jnp.broadcast_to(jnp.max(jnp.max(said, axis=0, keepdims=True), axis=1,
                                         keepdims=True), (1, LANES))
    for c in range(ncomp):
        landed(c)
        stored(c).wait()
        shares[c].wait_send()
        for j in range(depth):
            packs[c][j].wait_send()

        @pl.when(gate)
        def _():
            for j in range(depth):
                for d in range(1, depth):
                    spread(c, j, d).wait_send()


def settle(cap, base, got, gcell, out, hi, lo, crow):
    step = pl.program_id(0)
    ncomp, blk, nt, nr = out.shape

    @pl.when(step == 0)
    def _():
        crow[...] = wide_row(gcell[...].reshape(-1, LANES), cap)
        h, l = split(got[...])
        hi[...] = h
        lo[...] = l

    landing = landing_of(crow[...], step * (blk * nt), blk * nt)
    for c in range(ncomp):
        cs = slice(c * nr, (c + 1) * nr)
        deposit = dot(landing, hi[:, cs]) + dot(landing, lo[:, cs])
        out[c] = base[c, pl.ds(step * blk, blk)] + deposit.reshape(blk, nt, nr)


def settle_packed(base, got, landing, out, total, sem):
    ncomp, na, nt, nr = base.shape
    parts = 2
    blk = na // parts
    stores = []
    for c in range(ncomp):
        hi, lo = split(got[c])
        for m in range(parts):
            rows = slice(m * blk * nt, (m + 1) * blk * nt)
            deposit = dot(landing[rows], hi) + dot(landing[rows], lo)
            planes = slice(m * blk, (m + 1) * blk)
            total[c, planes] = base[c, planes] + deposit.reshape(blk, nt, nr)
            planes = pl.ds(m * blk, blk)
            stores.append(pltpu.make_async_copy(total.at[c, planes], out.at[c, planes],
                                                sem.at[c * parts + m]))
            stores[-1].start()
    for c in stores:
        c.wait()


def direct(n_ax, n_az, cap, *inputs):
    velocity, _, force = inputs[:3]
    n = n_ax * n_az
    ncomp, pan, nr = force.shape
    na, nt = velocity.shape[1:3]
    slots = n * cap
    late = n // 2
    soon = n - late
    f32, bf16 = jnp.float32, jnp.bfloat16
    any_ = pl.BlockSpec(memory_space=pl.ANY)
    hbm = pl.BlockSpec(memory_space=pltpu.HBM)
    vmem = pl.BlockSpec(memory_space=pltpu.VMEM)
    dma = pltpu.SemaphoreType.DMA
    i32 = jnp.int32
    base, got, gcell = pl.pallas_call(
        functools.partial(exchange, n_ax, n_az, cap),
        out_shape=(jax.ShapeDtypeStruct(velocity.shape, f32),
                   jax.ShapeDtypeStruct((late, cap, ncomp * nr), f32),
                   jax.ShapeDtypeStruct((late, 1, LANES), f32)),
        in_specs=[hbm] * 7,
        out_specs=(any_, any_, any_),
        scratch_shapes=[
            pltpu.VMEM((1, pan), i32), pltpu.VMEM((1, pan), i32),
            pltpu.VMEM((1, pan), f32), pltpu.VMEM((4, pan), i32),
            pltpu.VMEM((ncomp, na + 2, nt, nr), f32),
            pltpu.VMEM((na + 2, nt, nr), f32),
            pltpu.VMEM((ncomp, pan + 2 * HALO, nr), f32),
            pltpu.VMEM((ncomp, pan + 2 * HALO, nr), bf16),
            pltpu.VMEM((ncomp, pan + 2 * HALO, nr), bf16),
            pltpu.VMEM((n, cap, ncomp * nr), f32),
            pltpu.VMEM((n, 1, LANES), f32),
            pltpu.VMEM((2, ncomp + 1, na, nr), f32),
            pltpu.VMEM((2, ncomp + 1, na, nr), f32),
            pltpu.VMEM((ncomp, na, nt, nr), f32),
            pltpu.VMEM((soon, cap, ncomp * nr), f32),
            pltpu.VMEM((soon, 1, LANES), f32),
            pltpu.VMEM((soon * cap, ncomp * nr), bf16),
            pltpu.VMEM((soon * cap, ncomp * nr), bf16),
            dma((7,)), dma((8,)), dma((8,)), dma((n,)), dma((n,)), dma((n,)), dma((n,)),
            dma((2,)), dma((na,)),
        ],
        compiler_params=pltpu.CompilerParams(collective_id=1, has_side_effects=True,
                                             vmem_limit_bytes=40 << 20),
        name="exchange",
    )(*inputs)
    blk = max(1, 128 // nt)
    window = pl.BlockSpec((ncomp, blk, nt, nr), lambda s: (0, s, 0, 0))
    return pl.pallas_call(
        functools.partial(settle, cap),
        out_shape=jax.ShapeDtypeStruct(velocity.shape, f32),
        grid=(na // blk,),
        in_specs=[vmem,
                  pl.BlockSpec((late * cap, ncomp * nr), lambda s: (0, 0)),
                  pl.BlockSpec((late, 1, LANES), lambda s: (0, 0, 0))],
        out_specs=window,
        scratch_shapes=[pltpu.VMEM((late * cap, ncomp * nr), bf16),
                        pltpu.VMEM((late * cap, ncomp * nr), bf16),
                        pltpu.VMEM((1, late * cap), f32)],
        compiler_params=pltpu.CompilerParams(vmem_limit_bytes=24 << 20),
        name="settle",
    )(base, got.reshape(late * cap, ncomp * nr), gcell)


def on_device(n_ax, n_az, velocity, viscosity, force, area, adjacency, crossing, cell):
    n, depth, group_n = n_ax * n_az, n_az // 4, 2 * n_ax
    ncomp, pan, nr = force.shape
    na, nt = velocity.shape[1:3]
    most = max(2, 2 * pan // n)
    cap = -(-most // 8) * 8
    bound = min(pan, group_n * most)
    keep = -(-5 * bound // 128) * 16
    extra = -(-bound // 128) * 16
    meta_lanes = -(-(keep + extra) // LANES) * LANES
    half = n // 2
    f32, bf16, i32 = jnp.float32, jnp.bfloat16, jnp.int32
    any_ = pl.BlockSpec(memory_space=pl.ANY)
    hbm = pl.BlockSpec(memory_space=pltpu.HBM)
    vmem = pl.BlockSpec(memory_space=pltpu.VMEM)
    dma = pltpu.SemaphoreType.DMA
    inputs = (velocity, viscosity, force, crossing.reshape(1, pan), cell.reshape(1, pan),
              area.reshape(1, pan), adjacency.T)
    inputs = [pltpu.with_memory_space_constraint(x, pltpu.HBM) for x in inputs]
    base, got, landing, flag = pl.pallas_call(
        functools.partial(exchange_packed, n_ax, n_az, cap, keep, extra),
        out_shape=(jax.ShapeDtypeStruct(velocity.shape, f32),
                   jax.ShapeDtypeStruct((ncomp, half, cap, nr), f32),
                   jax.ShapeDtypeStruct((na * nt, half * cap), bf16),
                   jax.ShapeDtypeStruct((1, LANES), f32)),
        in_specs=[hbm] * 7,
        out_specs=(any_, any_, vmem, vmem),
        scratch_shapes=[
            pltpu.VMEM((1, pan), i32), pltpu.VMEM((1, pan), i32),
            pltpu.VMEM((1, pan), f32), pltpu.VMEM((4, pan), i32),
            pltpu.VMEM((ncomp, na + 2, nt, nr), f32),
            pltpu.VMEM((na + 2, nt, nr), f32),
            pltpu.VMEM((ncomp, pan + 2 * HALO, nr), f32),
            pltpu.VMEM((ncomp, pan + 2 * HALO, nr), bf16),
            pltpu.VMEM((ncomp, pan + 2 * HALO, nr), bf16),
            pltpu.VMEM((half, cap, ncomp * nr), f32),
            pltpu.VMEM((n, 1, LANES), f32),
            pltpu.VMEM((2, ncomp + 1, na, nr), f32),
            pltpu.VMEM((2, ncomp + 1, na, nr), f32),
            pltpu.VMEM((ncomp, na, nt, nr), f32),
            pltpu.VMEM((half, cap, ncomp * nr), f32),
            pltpu.VMEM((half, 1, LANES), f32),
            pltpu.VMEM((half, 1, LANES), f32),
            pltpu.VMEM((half * cap, ncomp * nr), bf16),
            pltpu.VMEM((half * cap, ncomp * nr), bf16),
            pltpu.VMEM((ncomp, depth, keep, nr), f32),
            pltpu.VMEM((ncomp, extra, nr), f32),
            pltpu.VMEM((ncomp, depth, keep + extra, nr), f32),
            pltpu.VMEM((depth, 1, meta_lanes), f32),
            pltpu.VMEM((depth, 1, meta_lanes), f32),
            pltpu.VMEM((ncomp, half, cap, nr), f32),
            pltpu.VMEM((na * nt, half * cap), bf16),
            pltpu.VMEM((2, nt, nr), f32),
            dma((7,)), dma((12,)), dma((12,)), dma((half,)), dma((half,)), dma((n,)), dma((n,)),
            dma((2,)), dma((na,)),
            dma((ncomp, depth)), dma((ncomp, depth)), dma((depth,)), dma((depth,)),
            dma((ncomp * half,)), dma((ncomp * half,)), dma((ncomp * depth,)),
            dma((ncomp,)), dma((ncomp, depth)), dma((ncomp, depth, depth)),
        ],
        compiler_params=pltpu.CompilerParams(collective_id=0, has_side_effects=True,
                                             vmem_limit_bytes=44 << 20),
        name="exchange_packed",
    )(*inputs)
    def finish(base, got, landing, *inputs):
        return pl.pallas_call(
            settle_packed,
            out_shape=jax.ShapeDtypeStruct(velocity.shape, f32),
            in_specs=[vmem, vmem, vmem],
            out_specs=hbm,
            scratch_shapes=[pltpu.VMEM((ncomp, na, nt, nr), f32), dma((2 * ncomp,))],
            compiler_params=pltpu.CompilerParams(vmem_limit_bytes=52 << 20),
            name="settle_packed",
        )(base, got.reshape(ncomp, half * cap, nr), landing)

    def again(base, got, landing, *inputs):
        return direct(n_ax, n_az, cap, *inputs)

    return lax.cond(flag[0, 0] > 0.5, again, finish, base, got, landing, *inputs)


def solution(mesh):
    n_ax, n_az = mesh.shape["ax"], mesh.shape["az"]
    in_specs = (
        P(None, "ax", "az", None),
        P("ax", "az", None),
        P(None, ("ax", "az"), None),
        P(("ax", "az")),
        P(("ax", "az"), None),
        P(("ax", "az"), None),
        P(("ax", "az")),
    )
    return jax.shard_map(
        functools.partial(on_device, n_ax, n_az), mesh=mesh, in_specs=in_specs,
        out_specs=P(None, "ax", "az", None), check_vma=False)
```

```python
import functools

import jax
import jax.numpy as jnp
from jax import lax
from jax.experimental import pallas as pl
from jax.experimental.pallas import tpu as pltpu
from jax.sharding import PartitionSpec as P

HALO = 32
LANES = 128

step_size = 0.1
coupling = 0.2


def split(x):
    hi = x.astype(jnp.bfloat16)
    lo = (x - hi.astype(jnp.float32)).astype(jnp.bfloat16)
    return hi, lo


def dot(a, b):
    return jnp.dot(a, b, preferred_element_type=jnp.float32)


def wide_row(cells, cap):
    m = cells.shape[0]
    slots = m * cap
    big = jnp.floor((cells + 1.0) * (1.0 / 64.0))
    small = (cells + 1.0) - 64.0 * big
    spread = (lax.broadcasted_iota(jnp.int32, (LANES, slots), 0)
              == lax.rem(lax.broadcasted_iota(jnp.int32, (LANES, slots), 1), cap))
    spread = spread.astype(jnp.float32).astype(jnp.bfloat16)
    wide = 64.0 * dot(big.astype(jnp.bfloat16), spread) + dot(small.astype(jnp.bfloat16), spread)
    mine = (lax.broadcasted_iota(jnp.int32, (m, slots), 0)
            == lax.broadcasted_iota(jnp.int32, (m, slots), 1) // cap)
    return jnp.sum(jnp.where(mine, wide, 0.0), axis=0, keepdims=True) - 1.0


def landing_of(crow, first, count):
    here = lax.broadcasted_iota(jnp.int32, (count, crow.shape[1]), 0) + first
    return (crow.astype(jnp.int32) == here).astype(jnp.float32).astype(jnp.bfloat16)


def exchange(n_ax, n_az, cap, vel, visc, force, dest_h, cell_h, area_h, adj_h, base, got, gcell,
             dest_i, cell_i, area, adj_i,
             velx, viscx, ext, exthi, extlo, send, scell, edges, edge_in, acc,
             tiles, tcell, thi, tlo,
             load_sem, halo_send, halo_recv, tile_send, tile_recv,
             cell_send, cell_recv, own_sem, out_sem):
    n, half_n = n_ax * n_az, n_az // 2
    ax, az = lax.axis_index("ax"), lax.axis_index("az")
    me = ax * n_az + az
    half, spot = az // half_n, lax.rem(az, half_n)
    ncomp, na, nt, nr = vel.shape
    pan = force.shape[1]
    slots = n * cap
    f32, bf16 = jnp.float32, jnp.bfloat16

    def place(linear):
        return (linear // n_az, lax.rem(linear, n_az))

    def remote(src, dst, ssem, rsem, device):
        return pltpu.make_async_remote_copy(
            src_ref=src, dst_ref=dst, send_sem=ssem, recv_sem=rsem,
            device_id=device, device_id_type=pl.DeviceIdType.MESH)

    barrier = pltpu.get_barrier_semaphore()

    def greet(k, carry):
        pl.semaphore_signal(barrier, inc=1, device_id=place(lax.rem(me + k, n)),
                            device_id_type=pl.DeviceIdType.MESH)
        return carry

    lax.fori_loop(1, n, greet, 0)
    small = [pltpu.make_async_copy(src, dst, load_sem.at[3 + k]) for k, (src, dst) in enumerate(
        [(dest_h, dest_i), (cell_h, cell_i), (adj_h, adj_i), (area_h, area)])]
    loads = [
        pltpu.make_async_copy(force, ext.at[:, pl.ds(HALO, pan)], load_sem.at[0]),
        pltpu.make_async_copy(vel, velx.at[:, pl.ds(1, na)], load_sem.at[1]),
        pltpu.make_async_copy(visc, viscx.at[pl.ds(1, na)], load_sem.at[2]),
    ]
    for c in small + loads:
        c.start()

    pl.semaphore_wait(barrier, n - 1)

    up, down = place(lax.rem(me + 1, n)), place(lax.rem(me + n - 1, n))
    ax_up, ax_down = lax.rem(ax + 1, n_ax), lax.rem(ax + n_ax - 1, n_ax)
    az_up, az_down = lax.rem(az + 1, n_az), lax.rem(az + n_az - 1, n_az)

    def halo(i, src, dst, device):
        return remote(src, dst, halo_send.at[i], halo_recv.at[i], device)

    fhalo = [
        halo(0, force.at[:, pl.ds(pan - HALO, HALO)], ext.at[:, pl.ds(0, HALO)], up),
        halo(1, force.at[:, pl.ds(0, HALO)], ext.at[:, pl.ds(HALO + pan, HALO)], down),
    ]
    ahalo = [
        halo(2, vel.at[:, na - 1], velx.at[:, 0], (ax_up, az)),
        halo(3, vel.at[:, 0], velx.at[:, na + 1], (ax_down, az)),
        halo(4, visc.at[na - 1], viscx.at[0], (ax_up, az)),
        halo(5, visc.at[0], viscx.at[na + 1], (ax_down, az)),
    ]
    zhalo = [
        halo(6, edges.at[1], edge_in.at[0], (ax, az_up)),
        halo(7, edges.at[0], edge_in.at[1], (ax, az_down)),
    ]
    for c in fhalo:
        c.start()
    for c in small:
        c.wait()

    dest_row, cell_row = dest_i[...].astype(f32), cell_i[...].astype(f32)
    adj = (adj_i[...] - (me * pan - HALO)).astype(f32)
    rows = jnp.concatenate([dest_row, cell_row, adj, dest_row, dest_row], axis=0)
    cols = rows.T
    dest_col, cell_col = cols[:, 0:1], cols[:, 1:2]
    same = dest_col == dest_row
    r0 = lax.broadcasted_iota(jnp.int32, (pan, pan), 0)
    r1 = lax.broadcasted_iota(jnp.int32, (pan, pan), 1)
    rank_row = jnp.sum((same & (r0 < r1)).astype(f32), axis=0, keepdims=True)
    rank_col = jnp.sum((same & (r1 < r0)).astype(f32), axis=1, keepdims=True)
    dax = jnp.floor(dest_row * (1.0 / n_az))
    daz = dest_row - n_az * dax
    dhalf = jnp.floor(daz * (1.0 / half_n))
    turn = dax - ax.astype(f32)
    turn = jnp.where(turn < 0.0, turn + n_ax, turn)
    group = turn + jnp.where(dhalf == half.astype(f32), 0.0, float(n_ax))
    peer = group * half_n + (daz - half_n * dhalf)
    target = (peer * cap + rank_row).astype(jnp.int32)
    hits = lax.broadcasted_iota(jnp.int32, (slots, pan), 0) == target
    scale = jnp.sum(jnp.where(hits, coupling * area[...], 0.0), axis=1, keepdims=True)
    q = lax.broadcasted_iota(jnp.int32, (pan, pan + 2 * HALO), 1).astype(f32)
    p = lax.broadcasted_iota(jnp.int32, (pan, pan + 2 * HALO), 0).astype(f32)
    count = (q == p + HALO).astype(f32)
    for k in range(4):
        count = count + (q == cols[:, 2 + k:3 + k]).astype(f32)
    pick = dot(hits.astype(f32).astype(bf16), count.astype(bf16)).astype(bf16)

    loads[1].wait()
    loads[2].wait()
    for c in range(ncomp):
        edges[0, c] = velx[c, 1:na + 1, 0, :]
        edges[1, c] = velx[c, 1:na + 1, nt - 1, :]
    edges[0, ncomp] = viscx[1:na + 1, 0, :]
    edges[1, ncomp] = viscx[1:na + 1, nt - 1, :]

    for c in zhalo + ahalo:
        c.start()

    big = jnp.floor((cell_col + 1.0) * (1.0 / 64.0))
    small = (cell_col + 1.0) - 64.0 * big
    at_rank = lax.broadcasted_iota(jnp.int32, (pan, LANES), 1).astype(f32) == rank_col
    owner = lax.broadcasted_iota(jnp.int32, (n, pan), 0).astype(f32) == peer
    owner = owner.astype(f32).astype(bf16)
    cells = (64.0 * dot(owner, jnp.where(at_rank, big, 0.0).astype(bf16))
             + dot(owner, jnp.where(at_rank, small, 0.0).astype(bf16)) - 1.0)
    for d in range(n):
        scell[d] = cells[d:d + 1, :]

    def split_force(lo_row, hi_row):
        h, l = split(ext[:, lo_row:hi_row])
        exthi[:, lo_row:hi_row] = h
        extlo[:, lo_row:hi_row] = l

    loads[0].wait()
    split_force(HALO, HALO + pan)
    for c in fhalo:
        c.wait()
    split_force(0, HALO)
    split_force(HALO + pan, pan + 2 * HALO)

    def tiles_to(g, i):
        there = lax.rem(spot + i, half_n)
        side = half if g < n_ax else 1 - half
        device = (lax.rem(ax + g % n_ax, n_ax), side * half_n + there)
        src, k = g * half_n + there, g * half_n + i
        at = (g % n_ax) * half_n + spot
        tile_at, cell_at = (tiles, tcell) if g < n_ax else (got, gcell)
        return (remote(send.at[src], tile_at.at[at], tile_send.at[k], tile_recv.at[k], device),
                remote(scell.at[src], cell_at.at[at], cell_send.at[k], cell_recv.at[k], device))

    def each_tile(groups, act):
        for g in groups:
            def body(i, carry):
                for c in tiles_to(g, i):
                    act(c)
                return carry
            lax.fori_loop(1 if g == 0 else 0, half_n, body, 0)

    for part in range(2):
        r = slice(part * (slots // 2), (part + 1) * (slots // 2))
        for c in range(ncomp):
            tile = (dot(pick[r], exthi[c]) + dot(pick[r], extlo[c])) * scale[r]
            send[part * (n // 2):(part + 1) * (n // 2), :, c * nr:(c + 1) * nr] = (
                tile.reshape(n // 2, cap, nr))
        each_tile(range(part * n_ax, (part + 1) * n_ax), lambda c: c.start())
    own = [pltpu.make_async_copy(send.at[spot], tiles.at[spot], own_sem.at[0]),
           pltpu.make_async_copy(scell.at[spot], tcell.at[spot], own_sem.at[1])]
    for c in own:
        c.start()

    for c in ahalo + zhalo:
        c.wait()

    @pl.when(ax == 0)
    def _():
        velx[:, 0] = jnp.zeros((ncomp, nt, nr), f32)
        viscx[0] = jnp.zeros((nt, nr), f32)

    @pl.when(ax == n_ax - 1)
    def _():
        velx[:, na + 1] = jnp.zeros((ncomp, nt, nr), f32)
        viscx[na + 1] = jnp.zeros((nt, nr), f32)

    row_id = lax.broadcasted_iota(jnp.int32, (nt, nr), 0)
    lane_id = lax.broadcasted_iota(jnp.int32, (nt, nr), 1)

    def neighbours(x, low, high):
        left = jnp.where(row_id == 0, low, pltpu.roll(x, 1, 0))
        right = jnp.where(row_id == nt - 1, high, pltpu.roll(x, nt - 1, 0))
        inner = jnp.where(lane_id == 0, 0.0, pltpu.roll(x, 1, 1))
        outer = jnp.where(lane_id == nr - 1, 0.0, pltpu.roll(x, nr - 1, 1))
        return left, right, inner, outer

    def plane(i, carry):
        mu = viscx[i + 1]
        sides = neighbours(mu, edge_in[0, ncomp, pl.ds(i, 1), :], edge_in[1, ncomp, pl.ds(i, 1), :])
        faces = [mu + s for s in (viscx[i], viscx[i + 2]) + sides]
        for c in range(ncomp):
            f = velx[c, i + 1]
            near = neighbours(f, edge_in[0, c, pl.ds(i, 1), :], edge_in[1, c, pl.ds(i, 1), :])
            near = (velx[c, i], velx[c, i + 2]) + near
            total = faces[0] * (near[0] - f)
            for w, g in zip(faces[1:], near[1:]):
                total = total + w * (g - f)
            acc[c, i] = f + (0.5 * step_size) * total
        return carry

    lax.fori_loop(0, na, plane, 0)

    for c in own:
        c.wait()
    each_tile(range(n_ax), lambda c: c.wait())
    h, l = split(tiles[...].reshape(-1, ncomp * nr))
    thi[...] = h
    tlo[...] = l
    crow = wide_row(tcell[...].reshape(-1, LANES), cap)
    blk = max(1, 256 // nt)

    def stored(j):
        return pltpu.make_async_copy(acc.at[:, pl.ds(j * blk, blk)],
                                     base.at[:, pl.ds(j * blk, blk)], out_sem.at[j])

    for j in range(na // blk):
        landing = landing_of(crow, j * blk * nt, blk * nt)
        for c in range(ncomp):
            cs = slice(c * nr, (c + 1) * nr)
            deposit = dot(landing, thi[:, cs]) + dot(landing, tlo[:, cs])
            acc[c, j * blk:(j + 1) * blk] += deposit.reshape(blk, nt, nr)
        stored(j).start()
    for j in range(na // blk):
        stored(j).wait()
    each_tile(range(n_ax, 2 * n_ax), lambda c: c.wait())


def exchange_packed(n_ax, n_az, cap, keep, extra, vel, visc, force, dest_h, cell_h, area_h, adj_h,
                    base, got, landing, flag,
                    dest_i, cell_i, area, adj_i,
                    velx, viscx, ext, exthi, extlo, send, scell, edges, edge_in, acc,
                    tiles, tcell, fcell, thi, tlo, pack, share, packed, smeta, rmeta, sorted_, near_at, relay,
                    load_sem, halo_send, halo_recv, tile_send, tile_recv,
                    cell_send, cell_recv, own_sem, out_sem,
                    pack_send, pack_recv, meta_send, meta_recv, hop_send, hop_recv, hop_own,
                    share_send, share_recv, pass_send):
    n, half_n = n_ax * n_az, n_az // 2
    depth, group_n = half_n // 2, 2 * n_ax
    ax, az = lax.axis_index("ax"), lax.axis_index("az")
    me = ax * n_az + az
    half, spot = az // half_n, lax.rem(az, half_n)
    zpos, core = spot // 2, lax.rem(az, 2)
    seat = ax * 2 + core
    ncomp, na, nt, nr = vel.shape
    pan = force.shape[1]
    near = (n // 2) * cap
    slots = near + depth * keep + extra
    both = keep + extra
    detour = n_ax == 4
    f32, bf16 = jnp.float32, jnp.bfloat16

    def place(linear):
        return (linear // n_az, lax.rem(linear, n_az))

    def remote(src, dst, ssem, rsem, device):
        return pltpu.make_async_remote_copy(
            src_ref=src, dst_ref=dst, send_sem=ssem, recv_sem=rsem,
            device_id=device, device_id_type=pl.DeviceIdType.MESH)

    barrier = pltpu.get_barrier_semaphore()

    def greet(k, carry):
        pl.semaphore_signal(barrier, inc=1, device_id=place(lax.rem(me + k, n)),
                            device_id_type=pl.DeviceIdType.MESH)
        return carry

    lax.fori_loop(1, n, greet, 0)
    small = [pltpu.make_async_copy(src, dst, load_sem.at[3 + k]) for k, (src, dst) in enumerate(
        [(dest_h, dest_i), (cell_h, cell_i), (adj_h, adj_i), (area_h, area)])]
    loads = [
        pltpu.make_async_copy(force, ext.at[:, pl.ds(HALO, pan)], load_sem.at[0]),
        pltpu.make_async_copy(vel, velx.at[:, pl.ds(1, na)], load_sem.at[1]),
        pltpu.make_async_copy(visc, viscx.at[pl.ds(1, na)], load_sem.at[2]),
    ]
    for c in small + loads:
        c.start()

    for c in small:
        c.wait()

    dest_row, cell_row = dest_i[...].astype(f32), cell_i[...].astype(f32)
    adj = (adj_i[...] - (me * pan - HALO)).astype(f32)
    rows = jnp.concatenate([dest_row, cell_row, adj, dest_row, dest_row], axis=0)
    cols = rows.T
    dest_col, cell_col = cols[:, 0:1], cols[:, 1:2]
    same = dest_col == dest_row
    r0 = lax.broadcasted_iota(jnp.int32, (pan, pan), 0)
    r1 = lax.broadcasted_iota(jnp.int32, (pan, pan), 1)
    rank_row = jnp.sum((same & (r0 < r1)).astype(f32), axis=0, keepdims=True)
    rank_col = jnp.sum((same & (r1 < r0)).astype(f32), axis=1, keepdims=True)

    pl.semaphore_wait(barrier, n - 1)

    up, down = place(lax.rem(me + 1, n)), place(lax.rem(me + n - 1, n))
    ax_up, ax_down = lax.rem(ax + 1, n_ax), lax.rem(ax + n_ax - 1, n_ax)
    az_up, az_down = lax.rem(az + 1, n_az), lax.rem(az + n_az - 1, n_az)

    def halo(i, src, dst, device):
        return remote(src, dst, halo_send.at[i], halo_recv.at[i], device)

    fhalo = [
        halo(0, force.at[:, pl.ds(pan - HALO, HALO)], ext.at[:, pl.ds(0, HALO)], up),
        halo(1, force.at[:, pl.ds(0, HALO)], ext.at[:, pl.ds(HALO + pan, HALO)], down),
    ]
    top, bottom, below, above = na - 1, 0, 0, na + 1
    ahalo = [
        halo(2, vel.at[:, top], velx.at[:, below], (ax_up, az)),
        halo(3, vel.at[:, bottom], velx.at[:, above], (ax_down, az)),
        halo(4, visc.at[top], viscx.at[below], (ax_up, az)),
        halo(5, visc.at[bottom], viscx.at[above], (ax_down, az)),
    ]
    first, final = pl.ds(0, ncomp - 1), ncomp - 1

    def halves(src, dst, to, via):
        i = 2 if dst == below else 3
        return [halo(i, vel.at[first, src], velx.at[first, dst], (to, az)),
                halo(8, vel.at[final, src], relay.at[0], (via, az)),
                halo(9, visc.at[src], relay.at[1], (via, az))]

    def passed(dst, to):
        return [halo(10, relay.at[0], velx.at[final, dst], (to, az)),
                halo(11, relay.at[1], viscx.at[dst], (to, az))]

    even = lax.rem(ax, 2) == 0

    def start_ahalo():
        if not detour:
            for c in ahalo:
                c.start()
            return

        @pl.when(even)
        def _():
            ahalo[0].start()
            ahalo[2].start()

        @pl.when(jnp.logical_not(even))
        def _():
            ahalo[1].start()
            ahalo[3].start()

        @pl.when(ax == 1)
        def _():
            for c in halves(top, below, 2, 3):
                c.start()

        @pl.when(ax == 2)
        def _():
            for c in halves(bottom, above, 1, 0):
                c.start()

    def pass_on():
        if not detour:
            return

        @pl.when(ax == 3)
        def _():
            for c in halves(top, below, 2, 3)[1:]:
                c.wait_recv()
            for c in passed(below, 2):
                c.start()

        @pl.when(ax == 0)
        def _():
            for c in halves(bottom, above, 1, 0)[1:]:
                c.wait_recv()
            for c in passed(above, 1):
                c.start()

    def wait_ahalo():
        if not detour:
            for c in ahalo:
                c.wait()
            return

        @pl.when(even)
        def _():
            for c in (ahalo[0], ahalo[2]):
                c.wait_send()
            for c in (ahalo[1], ahalo[3]):
                c.wait_recv()

        @pl.when(jnp.logical_not(even))
        def _():
            for c in (ahalo[1], ahalo[3]):
                c.wait_send()
            for c in (ahalo[0], ahalo[2]):
                c.wait_recv()

        @pl.when(ax == 1)
        def _():
            for c in halves(top, below, 2, 3):
                c.wait_send()
            halves(bottom, above, 1, 0)[0].wait_recv()
            for c in passed(above, 1):
                c.wait_recv()

        @pl.when(ax == 2)
        def _():
            for c in halves(bottom, above, 1, 0):
                c.wait_send()
            halves(top, below, 2, 3)[0].wait_recv()
            for c in passed(below, 2):
                c.wait_recv()

        @pl.when(ax == 3)
        def _():
            for c in passed(below, 2):
                c.wait_send()

        @pl.when(ax == 0)
        def _():
            for c in passed(above, 1):
                c.wait_send()

    zhalo = [
        halo(6, edges.at[1], edge_in.at[0], (ax, az_up)),
        halo(7, edges.at[0], edge_in.at[1], (ax, az_down)),
    ]
    @pl.when(me < n - 1)
    def _():
        fhalo[0].start()

    @pl.when(me > 0)
    def _():
        fhalo[1].start()

    start_ahalo()
    def layer_of(dest):
        inner = dest - n_az * jnp.floor(dest * (1.0 / n_az))
        return jnp.floor(inner * 0.5)

    dax = jnp.floor(dest_row * (1.0 / n_az))
    daz = dest_row - n_az * dax
    dhalf = jnp.floor(daz * (1.0 / half_n))
    layer_row, layer_col = layer_of(dest_row), layer_of(dest_col)
    pos_row = jnp.sum(((layer_col == layer_row) & (r0 < r1)).astype(f32), axis=0, keepdims=True)
    turn = dax - ax.astype(f32)
    turn = jnp.where(turn < 0.0, turn + n_ax, turn)
    far = dhalf != half.astype(f32)
    group = turn + jnp.where(far, float(n_ax), 0.0)
    peer = group * half_n + (daz - half_n * dhalf)
    dz = (layer_row - depth * dhalf) - zpos.astype(f32)
    dz = jnp.where(dz < 0.0, dz + depth, dz)
    pos_col = jnp.sum(((layer_col == layer_row) & (r1 < r0)).astype(f32), axis=1, keepdims=True)
    far_col = jnp.floor(layer_col * (1.0 / depth)) != half.astype(f32)
    over_col = far_col & (pos_col >= keep)
    order = jnp.sum((over_col & (r0 < r1)).astype(f32), axis=0, keepdims=True)
    over = far & (pos_row >= keep)
    spilled = over & (order >= extra)
    target = jnp.where(far, near + dz * keep + pos_row, peer * cap + rank_row)
    target = jnp.where(over, near + depth * keep + order, target)
    target = jnp.where(spilled, -1.0, target).astype(jnp.int32)
    spill = jnp.max(jnp.where(spilled, 1.0, 0.0), axis=1, keepdims=True)
    hits = lax.broadcasted_iota(jnp.int32, (slots, pan), 0) == target
    scale = jnp.sum(jnp.where(hits, coupling * area[...], 0.0), axis=1, keepdims=True)
    q = lax.broadcasted_iota(jnp.int32, (pan, pan + 2 * HALO), 1).astype(f32)
    p = lax.broadcasted_iota(jnp.int32, (pan, pan + 2 * HALO), 0).astype(f32)
    count = (q == p + HALO).astype(f32)
    for k in range(4):
        count = count + (q == cols[:, 2 + k:3 + k]).astype(f32)
    hits = hits.astype(f32).astype(bf16)
    pick = dot(hits, count.astype(bf16)).astype(bf16)
    slot = (dax * 2.0 + (daz - 2.0 * layer_row)) * cap + rank_row + 1.0
    sbig = jnp.floor(slot * (1.0 / 64.0))
    digits = jnp.concatenate([sbig, slot - 64.0 * sbig] * 4, axis=0)
    for j in range(depth):
        at = near + j * keep
        holds = jnp.concatenate([hits[at:at + keep], hits[near + depth * keep:]], axis=0)
        found = lax.dot_general(jnp.where(dz == j, digits, 0.0).astype(bf16), holds,
                                (((1,), (1,)), ((), ())), preferred_element_type=f32)
        smeta[j] = jnp.full(smeta.shape[1:], -1.0, f32)
        smeta[j, :, 0:both] = 64.0 * found[0:1] + found[1:2] - 1.0

    loads[1].wait()
    loads[2].wait()
    for c in range(ncomp):
        edges[0, c] = velx[c, 1:na + 1, 0, :]
        edges[1, c] = velx[c, 1:na + 1, nt - 1, :]
    edges[0, ncomp] = viscx[1:na + 1, 0, :]
    edges[1, ncomp] = viscx[1:na + 1, nt - 1, :]
    for c in zhalo:
        c.start()

    big = jnp.floor((cell_col + 1.0) * (1.0 / 64.0))
    small_digit = (cell_col + 1.0) - 64.0 * big
    at_rank = lax.broadcasted_iota(jnp.int32, (pan, LANES), 1).astype(f32) == rank_col
    owner = lax.broadcasted_iota(jnp.int32, (n, pan), 0).astype(f32) == peer
    owner = owner.astype(f32).astype(bf16)
    cells = (64.0 * dot(owner, jnp.where(at_rank, big, 0.0).astype(bf16))
             + dot(owner, jnp.where(at_rank, small_digit, 0.0).astype(bf16)) - 1.0)
    last = lax.broadcasted_iota(jnp.int32, (n, LANES), 1) == LANES - 1
    cells = jnp.where(last, spill, cells)
    for d in range(n):
        scell[d] = cells[d:d + 1, :]

    def cells_to(g, i):
        there = lax.rem(spot + i, half_n)
        side = half if g < n_ax else 1 - half
        device = (lax.rem(ax + g % n_ax, n_ax), side * half_n + there)
        src, k = g * half_n + there, g * half_n + i
        if g < n_ax:
            cell_at = tcell.at[g * half_n + spot]
        else:
            cell_at = fcell.at[lax.rem(there // 2 - zpos + depth, depth) * group_n + seat]
        return remote(scell.at[src], cell_at, cell_send.at[k], cell_recv.at[k], device)

    def each(copy, groups, act):
        for g in groups:
            def body(i, carry):
                act(copy(g, i))
                return carry
            lax.fori_loop(1 if g == 0 else 0, half_n, body, 0)

    def along(j):
        return (ax, ((1 - half) * depth + lax.rem(zpos + j, depth)) * 2 + core)

    metas = [remote(smeta.at[j], rmeta.at[j], meta_send.at[j], meta_recv.at[j], along(j))
             for j in range(depth)]
    for c in metas:
        c.start()
    each(cells_to, range(2 * n_ax), lambda c: c.start())

    def split_force(lo_row, hi_row):
        h, l = split(ext[:, lo_row:hi_row])
        exthi[:, lo_row:hi_row] = h
        extlo[:, lo_row:hi_row] = l

    loads[0].wait()
    split_force(HALO, HALO + pan)

    @pl.when(me < n - 1)
    def _():
        fhalo[0].wait_send()
        fhalo[1].wait_recv()

    @pl.when(me > 0)
    def _():
        fhalo[1].wait_send()
        fhalo[0].wait_recv()

    @pl.when(me == 0)
    def _():
        ext[:, 0:HALO] = jnp.zeros((ncomp, HALO, nr), f32)

    @pl.when(me == n - 1)
    def _():
        ext[:, HALO + pan:] = jnp.zeros((ncomp, HALO, nr), f32)

    split_force(0, HALO)
    split_force(HALO + pan, pan + 2 * HALO)

    def picked(c, lo_row, hi_row):
        r = slice(lo_row, hi_row)
        return (dot(pick[r], exthi[c]) + dot(pick[r], extlo[c])) * scale[r]

    def tiles_to(g, i):
        there = lax.rem(spot + i, half_n)
        device = (lax.rem(ax + g, n_ax), half * half_n + there)
        src, k = g * half_n + there, g * half_n + i
        return remote(send.at[src], tiles.at[g * half_n + spot], tile_send.at[k],
                      tile_recv.at[k], device)

    packs = [[remote(pack.at[c, j], packed.at[c, j, pl.ds(0, keep)], pack_send.at[c, j], pack_recv.at[c, j],
                     along(j)) for j in range(depth)] for c in range(ncomp)]

    def entry(side):
        return jnp.where(side == 1, 0, depth - 1)

    at_gate = lax.rem(entry(1 - half) - zpos + depth, depth)
    shares = [remote(share.at[c], packed.at[c, at_gate, pl.ds(keep, extra)], share_send.at[c],
                     share_recv.at[c, at_gate], along(at_gate)) for c in range(ncomp)]
    gate = zpos == entry(half)

    def spread(c, j, d):
        there = lax.rem(zpos + d, depth)
        k = (j + d) % depth
        return remote(packed.at[c, j, pl.ds(keep, extra)], packed.at[c, k, pl.ds(keep, extra)],
                      pass_send.at[c, j, d], share_recv.at[c, k],
                      (ax, (half * depth + there) * 2 + core))

    def shared_in(c, j):
        return remote(share.at[c], packed.at[c, j, pl.ds(keep, extra)], share_send.at[c],
                      share_recv.at[c, j], along(j))

    def spread_shares(c):
        @pl.when(gate)
        def _():
            for j in range(depth):
                shared_in(c, j).wait_recv()
                for d in range(1, depth):
                    spread(c, j, d).start()

    def start_packs():
        for c in range(ncomp):
            share[c] = picked(c, near + depth * keep, slots)
            shares[c].start()
        for c in range(ncomp):
            for j in range(depth):
                at = near + j * keep
                pack[c, j] = picked(c, at, at + keep)
                packs[c][j].start()

    for c in range(ncomp):
        send[:, :, c * nr:(c + 1) * nr] = picked(c, 0, near).reshape(n // 2, cap, nr)
    each(tiles_to, range(n_ax), lambda c: c.start())
    start_packs()
    own = [pltpu.make_async_copy(send.at[spot], tiles.at[spot], own_sem.at[0]),
           pltpu.make_async_copy(scell.at[spot], tcell.at[spot], own_sem.at[1])]
    for c in own:
        c.start()

    pass_on()
    for c in zhalo:
        c.wait()

    row_id = lax.broadcasted_iota(jnp.int32, (nt, nr), 0)
    lane_id = lax.broadcasted_iota(jnp.int32, (nt, nr), 1)

    def neighbours(x, low, high):
        left = jnp.where(row_id == 0, low, pltpu.roll(x, 1, 0))
        right = jnp.where(row_id == nt - 1, high, pltpu.roll(x, nt - 1, 0))
        inner = jnp.where(lane_id == 0, 0.0, pltpu.roll(x, 1, 1))
        outer = jnp.where(lane_id == nr - 1, 0.0, pltpu.roll(x, nr - 1, 1))
        return left, right, inner, outer

    def plane(i, carry):
        mu = viscx[i + 1]
        sides = neighbours(mu, edge_in[0, ncomp, pl.ds(i, 1), :], edge_in[1, ncomp, pl.ds(i, 1), :])
        faces = [mu + s for s in (viscx[i], viscx[i + 2]) + sides]
        for c in range(ncomp):
            f = velx[c, i + 1]
            sides_f = neighbours(f, edge_in[0, c, pl.ds(i, 1), :], edge_in[1, c, pl.ds(i, 1), :])
            sides_f = (velx[c, i], velx[c, i + 2]) + sides_f
            total = faces[0] * (sides_f[0] - f)
            for w, g in zip(faces[1:], sides_f[1:]):
                total = total + w * (g - f)
            acc[c, i] = f + (0.5 * step_size) * total
        return carry

    lax.fori_loop(1, na - 1, plane, 0)
    for c in range(ncomp):
        spread_shares(c)

    def hop(c, j, k):
        there = lax.rem(seat + k, group_n)
        device = (there // 2, (half * depth + zpos) * 2 + lax.rem(there, 2))
        return remote(sorted_.at[c, j * group_n + there], arrival(c, j),
                      hop_send.at[(c * depth + j) * group_n + k],
                      hop_recv.at[(c * depth + j) * group_n + k], device)

    def arrival(c, j):
        return got.at[c, j * group_n + seat]

    def each_hop(c, j, act):
        def body(k, carry):
            act(hop(c, j, k))
            return carry
        lax.fori_loop(1, group_n, body, 0)

    def hop_mine(c, j):
        return pltpu.make_async_copy(sorted_.at[c, j * group_n + seat], arrival(c, j),
                                     hop_own.at[c * depth + j])

    for c in metas:
        c.wait()
    sorter = [(rmeta[j, :, 0:both].astype(jnp.int32)
               == lax.broadcasted_iota(jnp.int32, (group_n * cap, both), 0)
               ).astype(f32).astype(bf16) for j in range(depth)]

    def forward(c):
        for j in range(depth):
            packs[c][j].wait_recv()

            @pl.when(jnp.logical_not(gate))
            def _():
                shared_in(c, j).wait_recv()

            h, l = split(packed[c, j])
            sorted_[c, j * group_n:(j + 1) * group_n] = (
                dot(sorter[j], h) + dot(sorter[j], l)).reshape(group_n, cap, nr)
            each_hop(c, j, lambda x: x.start())
            hop_mine(c, j).start()

    def landed(c):
        for j in range(depth):
            each_hop(c, j, lambda x: x.wait())
            hop_mine(c, j).wait()

    def add(c, where, h, l):
        for m in range(2):
            rows = slice(m * (na // 2) * nt, (m + 1) * (na // 2) * nt)
            total = dot(where[rows], h) + dot(where[rows], l)
            acc[c, m * (na // 2):(m + 1) * (na // 2)] += total.reshape(na // 2, nt, nr)

    def stored(c):
        return pltpu.make_async_copy(acc.at[c], base.at[c], out_sem.at[c])

    forward(0)
    forward(1)

    wait_ahalo()

    @pl.when(ax == 0)
    def _():
        velx[:, 0] = jnp.zeros((ncomp, nt, nr), f32)
        viscx[0] = jnp.zeros((nt, nr), f32)

    @pl.when(ax == n_ax - 1)
    def _():
        velx[:, na + 1] = jnp.zeros((ncomp, nt, nr), f32)
        viscx[na + 1] = jnp.zeros((nt, nr), f32)

    lax.fori_loop(0, 2, lambda i, carry: plane(i * (na - 1), carry), 0)

    for c in own:
        c.wait()
    each(tiles_to, range(n_ax), lambda c: c.wait())
    each(cells_to, range(n_ax), lambda c: c.wait())
    h, l = split(tiles[...].reshape(-1, ncomp * nr))
    thi[...] = h
    tlo[...] = l
    near_at[...] = landing_of(wide_row(tcell[...].reshape(-1, LANES), cap), 0, na * nt)
    for c in range(ncomp):
        add(c, near_at, thi[:, c * nr:(c + 1) * nr], tlo[:, c * nr:(c + 1) * nr])
        stored(c).start()

    for c in range(2, ncomp):
        forward(c)
    each(cells_to, range(n_ax, 2 * n_ax), lambda c: c.wait())
    landing[...] = landing_of(wide_row(fcell[...].reshape(-1, LANES), cap), 0, na * nt)
    said = jnp.maximum(tcell[...].reshape(-1, LANES), fcell[...].reshape(-1, LANES))
    said = jnp.where(last[0:n // 2], said, 0.0)
    flag[...] = jnp.broadcast_to(jnp.max(jnp.max(said, axis=0, keepdims=True), axis=1,
                                         keepdims=True), (1, LANES))
    for c in range(ncomp):
        landed(c)
        stored(c).wait()
        shares[c].wait_send()
        for j in range(depth):
            packs[c][j].wait_send()

        @pl.when(gate)
        def _():
            for j in range(depth):
                for d in range(1, depth):
                    spread(c, j, d).wait_send()


def settle(cap, base, got, gcell, out, hi, lo, crow):
    step = pl.program_id(0)
    ncomp, blk, nt, nr = out.shape

    @pl.when(step == 0)
    def _():
        crow[...] = wide_row(gcell[...].reshape(-1, LANES), cap)
        h, l = split(got[...])
        hi[...] = h
        lo[...] = l

    landing = landing_of(crow[...], step * (blk * nt), blk * nt)
    for c in range(ncomp):
        cs = slice(c * nr, (c + 1) * nr)
        deposit = dot(landing, hi[:, cs]) + dot(landing, lo[:, cs])
        out[c] = base[c, pl.ds(step * blk, blk)] + deposit.reshape(blk, nt, nr)


def settle_packed(base, got, landing, out, total, sem):
    ncomp, na, nt, nr = base.shape
    parts = 4
    blk = na // parts
    stores = []
    for c in range(ncomp):
        hi, lo = split(got[c])
        for m in range(parts):
            rows = slice(m * blk * nt, (m + 1) * blk * nt)
            deposit = dot(landing[rows], hi) + dot(landing[rows], lo)
            planes = slice(m * blk, (m + 1) * blk)
            total[c, planes] = base[c, planes] + deposit.reshape(blk, nt, nr)
            planes = pl.ds(m * blk, blk)
            stores.append(pltpu.make_async_copy(total.at[c, planes], out.at[c, planes],
                                                sem.at[c * parts + m]))
            stores[-1].start()
    for c in stores:
        c.wait()


def direct(n_ax, n_az, cap, *inputs):
    velocity, _, force = inputs[:3]
    n = n_ax * n_az
    ncomp, pan, nr = force.shape
    na, nt = velocity.shape[1:3]
    slots = n * cap
    late = n // 2
    soon = n - late
    f32, bf16 = jnp.float32, jnp.bfloat16
    any_ = pl.BlockSpec(memory_space=pl.ANY)
    hbm = pl.BlockSpec(memory_space=pltpu.HBM)
    vmem = pl.BlockSpec(memory_space=pltpu.VMEM)
    dma = pltpu.SemaphoreType.DMA
    i32 = jnp.int32
    base, got, gcell = pl.pallas_call(
        functools.partial(exchange, n_ax, n_az, cap),
        out_shape=(jax.ShapeDtypeStruct(velocity.shape, f32),
                   jax.ShapeDtypeStruct((late, cap, ncomp * nr), f32),
                   jax.ShapeDtypeStruct((late, 1, LANES), f32)),
        in_specs=[hbm] * 7,
        out_specs=(any_, any_, any_),
        scratch_shapes=[
            pltpu.VMEM((1, pan), i32), pltpu.VMEM((1, pan), i32),
            pltpu.VMEM((1, pan), f32), pltpu.VMEM((4, pan), i32),
            pltpu.VMEM((ncomp, na + 2, nt, nr), f32),
            pltpu.VMEM((na + 2, nt, nr), f32),
            pltpu.VMEM((ncomp, pan + 2 * HALO, nr), f32),
            pltpu.VMEM((ncomp, pan + 2 * HALO, nr), bf16),
            pltpu.VMEM((ncomp, pan + 2 * HALO, nr), bf16),
            pltpu.VMEM((n, cap, ncomp * nr), f32),
            pltpu.VMEM((n, 1, LANES), f32),
            pltpu.VMEM((2, ncomp + 1, na, nr), f32),
            pltpu.VMEM((2, ncomp + 1, na, nr), f32),
            pltpu.VMEM((ncomp, na, nt, nr), f32),
            pltpu.VMEM((soon, cap, ncomp * nr), f32),
            pltpu.VMEM((soon, 1, LANES), f32),
            pltpu.VMEM((soon * cap, ncomp * nr), bf16),
            pltpu.VMEM((soon * cap, ncomp * nr), bf16),
            dma((7,)), dma((8,)), dma((8,)), dma((n,)), dma((n,)), dma((n,)), dma((n,)),
            dma((2,)), dma((na,)),
        ],
        compiler_params=pltpu.CompilerParams(collective_id=1, has_side_effects=True,
                                             vmem_limit_bytes=40 << 20),
        name="exchange",
    )(*inputs)
    blk = max(1, 128 // nt)
    window = pl.BlockSpec((ncomp, blk, nt, nr), lambda s: (0, s, 0, 0))
    return pl.pallas_call(
        functools.partial(settle, cap),
        out_shape=jax.ShapeDtypeStruct(velocity.shape, f32),
        grid=(na // blk,),
        in_specs=[vmem,
                  pl.BlockSpec((late * cap, ncomp * nr), lambda s: (0, 0)),
                  pl.BlockSpec((late, 1, LANES), lambda s: (0, 0, 0))],
        out_specs=window,
        scratch_shapes=[pltpu.VMEM((late * cap, ncomp * nr), bf16),
                        pltpu.VMEM((late * cap, ncomp * nr), bf16),
                        pltpu.VMEM((1, late * cap), f32)],
        compiler_params=pltpu.CompilerParams(vmem_limit_bytes=24 << 20),
        name="settle",
    )(base, got.reshape(late * cap, ncomp * nr), gcell)


def on_device(n_ax, n_az, velocity, viscosity, force, area, adjacency, crossing, cell):
    n, depth, group_n = n_ax * n_az, n_az // 4, 2 * n_ax
    ncomp, pan, nr = force.shape
    na, nt = velocity.shape[1:3]
    most = max(2, 2 * pan // n)
    cap = -(-most // 8) * 8
    bound = min(pan, group_n * most)
    keep = -(-5 * bound // 128) * 16
    extra = -(-bound // 128) * 16
    meta_lanes = -(-(keep + extra) // LANES) * LANES
    half = n // 2
    f32, bf16, i32 = jnp.float32, jnp.bfloat16, jnp.int32
    any_ = pl.BlockSpec(memory_space=pl.ANY)
    hbm = pl.BlockSpec(memory_space=pltpu.HBM)
    vmem = pl.BlockSpec(memory_space=pltpu.VMEM)
    dma = pltpu.SemaphoreType.DMA
    inputs = (velocity, viscosity, force, crossing.reshape(1, pan), cell.reshape(1, pan),
              area.reshape(1, pan), adjacency.T)
    inputs = [pltpu.with_memory_space_constraint(x, pltpu.HBM) for x in inputs]
    base, got, landing, flag = pl.pallas_call(
        functools.partial(exchange_packed, n_ax, n_az, cap, keep, extra),
        out_shape=(jax.ShapeDtypeStruct(velocity.shape, f32),
                   jax.ShapeDtypeStruct((ncomp, half, cap, nr), f32),
                   jax.ShapeDtypeStruct((na * nt, half * cap), bf16),
                   jax.ShapeDtypeStruct((1, LANES), f32)),
        in_specs=[hbm] * 7,
        out_specs=(any_, any_, vmem, vmem),
        scratch_shapes=[
            pltpu.VMEM((1, pan), i32), pltpu.VMEM((1, pan), i32),
            pltpu.VMEM((1, pan), f32), pltpu.VMEM((4, pan), i32),
            pltpu.VMEM((ncomp, na + 2, nt, nr), f32),
            pltpu.VMEM((na + 2, nt, nr), f32),
            pltpu.VMEM((ncomp, pan + 2 * HALO, nr), f32),
            pltpu.VMEM((ncomp, pan + 2 * HALO, nr), bf16),
            pltpu.VMEM((ncomp, pan + 2 * HALO, nr), bf16),
            pltpu.VMEM((half, cap, ncomp * nr), f32),
            pltpu.VMEM((n, 1, LANES), f32),
            pltpu.VMEM((2, ncomp + 1, na, nr), f32),
            pltpu.VMEM((2, ncomp + 1, na, nr), f32),
            pltpu.VMEM((ncomp, na, nt, nr), f32),
            pltpu.VMEM((half, cap, ncomp * nr), f32),
            pltpu.VMEM((half, 1, LANES), f32),
            pltpu.VMEM((half, 1, LANES), f32),
            pltpu.VMEM((half * cap, ncomp * nr), bf16),
            pltpu.VMEM((half * cap, ncomp * nr), bf16),
            pltpu.VMEM((ncomp, depth, keep, nr), f32),
            pltpu.VMEM((ncomp, extra, nr), f32),
            pltpu.VMEM((ncomp, depth, keep + extra, nr), f32),
            pltpu.VMEM((depth, 1, meta_lanes), f32),
            pltpu.VMEM((depth, 1, meta_lanes), f32),
            pltpu.VMEM((ncomp, half, cap, nr), f32),
            pltpu.VMEM((na * nt, half * cap), bf16),
            pltpu.VMEM((2, nt, nr), f32),
            dma((7,)), dma((12,)), dma((12,)), dma((half,)), dma((half,)), dma((n,)), dma((n,)),
            dma((2,)), dma((na,)),
            dma((ncomp, depth)), dma((ncomp, depth)), dma((depth,)), dma((depth,)),
            dma((ncomp * half,)), dma((ncomp * half,)), dma((ncomp * depth,)),
            dma((ncomp,)), dma((ncomp, depth)), dma((ncomp, depth, depth)),
        ],
        compiler_params=pltpu.CompilerParams(collective_id=0, has_side_effects=True,
                                             vmem_limit_bytes=44 << 20),
        name="exchange_packed",
    )(*inputs)
    def finish(base, got, landing, *inputs):
        return pl.pallas_call(
            settle_packed,
            out_shape=jax.ShapeDtypeStruct(velocity.shape, f32),
            in_specs=[vmem, vmem, vmem],
            out_specs=hbm,
            scratch_shapes=[pltpu.VMEM((ncomp, na, nt, nr), f32), dma((4 * ncomp,))],
            compiler_params=pltpu.CompilerParams(vmem_limit_bytes=52 << 20),
            name="settle_packed",
        )(base, got.reshape(ncomp, half * cap, nr), landing)

    def again(base, got, landing, *inputs):
        return direct(n_ax, n_az, cap, *inputs)

    return lax.cond(flag[0, 0] > 0.5, again, finish, base, got, landing, *inputs)


def solution(mesh):
    n_ax, n_az = mesh.shape["ax"], mesh.shape["az"]
    in_specs = (
        P(None, "ax", "az", None),
        P("ax", "az", None),
        P(None, ("ax", "az"), None),
        P(("ax", "az")),
        P(("ax", "az"), None),
        P(("ax", "az"), None),
        P(("ax", "az")),
    )
    return jax.shard_map(
        functools.partial(on_device, n_ax, n_az), mesh=mesh, in_specs=in_specs,
        out_specs=P(None, "ax", "az", None), check_vma=False)
```

```python
import functools

import jax
import jax.numpy as jnp
from jax import lax
from jax.experimental import pallas as pl
from jax.experimental.pallas import tpu as pltpu
from jax.sharding import PartitionSpec as P

HALO = 32
LANES = 128

step_size = 0.1
coupling = 0.2


def split(x):
    hi = x.astype(jnp.bfloat16)
    lo = (x - hi.astype(jnp.float32)).astype(jnp.bfloat16)
    return hi, lo


def dot(a, b):
    return jnp.dot(a, b, preferred_element_type=jnp.float32)


def wide_row(cells, cap):
    m = cells.shape[0]
    slots = m * cap
    big = jnp.floor((cells + 1.0) * (1.0 / 64.0))
    small = (cells + 1.0) - 64.0 * big
    spread = (lax.broadcasted_iota(jnp.int32, (LANES, slots), 0)
              == lax.rem(lax.broadcasted_iota(jnp.int32, (LANES, slots), 1), cap))
    spread = spread.astype(jnp.float32).astype(jnp.bfloat16)
    wide = 64.0 * dot(big.astype(jnp.bfloat16), spread) + dot(small.astype(jnp.bfloat16), spread)
    mine = (lax.broadcasted_iota(jnp.int32, (m, slots), 0)
            == lax.broadcasted_iota(jnp.int32, (m, slots), 1) // cap)
    return jnp.sum(jnp.where(mine, wide, 0.0), axis=0, keepdims=True) - 1.0


def landing_of(crow, first, count):
    here = lax.broadcasted_iota(jnp.int32, (count, crow.shape[1]), 0) + first
    return (crow.astype(jnp.int32) == here).astype(jnp.float32).astype(jnp.bfloat16)


def exchange(n_ax, n_az, cap, vel, visc, force, dest_h, cell_h, area_h, adj_h, base, got, gcell,
             dest_i, cell_i, area, adj_i,
             velx, viscx, ext, exthi, extlo, send, scell, edges, edge_in, acc,
             tiles, tcell, thi, tlo,
             load_sem, halo_send, halo_recv, tile_send, tile_recv,
             cell_send, cell_recv, own_sem, out_sem):
    n, half_n = n_ax * n_az, n_az // 2
    ax, az = lax.axis_index("ax"), lax.axis_index("az")
    me = ax * n_az + az
    half, spot = az // half_n, lax.rem(az, half_n)
    ncomp, na, nt, nr = vel.shape
    pan = force.shape[1]
    slots = n * cap
    f32, bf16 = jnp.float32, jnp.bfloat16

    def place(linear):
        return (linear // n_az, lax.rem(linear, n_az))

    def remote(src, dst, ssem, rsem, device):
        return pltpu.make_async_remote_copy(
            src_ref=src, dst_ref=dst, send_sem=ssem, recv_sem=rsem,
            device_id=device, device_id_type=pl.DeviceIdType.MESH)

    barrier = pltpu.get_barrier_semaphore()

    def greet(k, carry):
        pl.semaphore_signal(barrier, inc=1, device_id=place(lax.rem(me + k, n)),
                            device_id_type=pl.DeviceIdType.MESH)
        return carry

    lax.fori_loop(1, n, greet, 0)
    small = [pltpu.make_async_copy(src, dst, load_sem.at[3 + k]) for k, (src, dst) in enumerate(
        [(dest_h, dest_i), (cell_h, cell_i), (adj_h, adj_i), (area_h, area)])]
    loads = [
        pltpu.make_async_copy(force, ext.at[:, pl.ds(HALO, pan)], load_sem.at[0]),
        pltpu.make_async_copy(vel, velx.at[:, pl.ds(1, na)], load_sem.at[1]),
        pltpu.make_async_copy(visc, viscx.at[pl.ds(1, na)], load_sem.at[2]),
    ]
    for c in small + loads:
        c.start()

    pl.semaphore_wait(barrier, n - 1)

    up, down = place(lax.rem(me + 1, n)), place(lax.rem(me + n - 1, n))
    ax_up, ax_down = lax.rem(ax + 1, n_ax), lax.rem(ax + n_ax - 1, n_ax)
    az_up, az_down = lax.rem(az + 1, n_az), lax.rem(az + n_az - 1, n_az)

    def halo(i, src, dst, device):
        return remote(src, dst, halo_send.at[i], halo_recv.at[i], device)

    fhalo = [
        halo(0, force.at[:, pl.ds(pan - HALO, HALO)], ext.at[:, pl.ds(0, HALO)], up),
        halo(1, force.at[:, pl.ds(0, HALO)], ext.at[:, pl.ds(HALO + pan, HALO)], down),
    ]
    ahalo = [
        halo(2, vel.at[:, na - 1], velx.at[:, 0], (ax_up, az)),
        halo(3, vel.at[:, 0], velx.at[:, na + 1], (ax_down, az)),
        halo(4, visc.at[na - 1], viscx.at[0], (ax_up, az)),
        halo(5, visc.at[0], viscx.at[na + 1], (ax_down, az)),
    ]
    zhalo = [
        halo(6, edges.at[1], edge_in.at[0], (ax, az_up)),
        halo(7, edges.at[0], edge_in.at[1], (ax, az_down)),
    ]
    for c in fhalo:
        c.start()
    for c in small:
        c.wait()

    dest_row, cell_row = dest_i[...].astype(f32), cell_i[...].astype(f32)
    adj = (adj_i[...] - (me * pan - HALO)).astype(f32)
    rows = jnp.concatenate([dest_row, cell_row, adj, dest_row, dest_row], axis=0)
    cols = rows.T
    dest_col, cell_col = cols[:, 0:1], cols[:, 1:2]
    same = dest_col == dest_row
    r0 = lax.broadcasted_iota(jnp.int32, (pan, pan), 0)
    r1 = lax.broadcasted_iota(jnp.int32, (pan, pan), 1)
    rank_row = jnp.sum((same & (r0 < r1)).astype(f32), axis=0, keepdims=True)
    rank_col = jnp.sum((same & (r1 < r0)).astype(f32), axis=1, keepdims=True)
    dax = jnp.floor(dest_row * (1.0 / n_az))
    daz = dest_row - n_az * dax
    dhalf = jnp.floor(daz * (1.0 / half_n))
    turn = dax - ax.astype(f32)
    turn = jnp.where(turn < 0.0, turn + n_ax, turn)
    group = turn + jnp.where(dhalf == half.astype(f32), 0.0, float(n_ax))
    peer = group * half_n + (daz - half_n * dhalf)
    target = (peer * cap + rank_row).astype(jnp.int32)
    hits = lax.broadcasted_iota(jnp.int32, (slots, pan), 0) == target
    scale = jnp.sum(jnp.where(hits, coupling * area[...], 0.0), axis=1, keepdims=True)
    q = lax.broadcasted_iota(jnp.int32, (pan, pan + 2 * HALO), 1).astype(f32)
    p = lax.broadcasted_iota(jnp.int32, (pan, pan + 2 * HALO), 0).astype(f32)
    count = (q == p + HALO).astype(f32)
    for k in range(4):
        count = count + (q == cols[:, 2 + k:3 + k]).astype(f32)
    pick = dot(hits.astype(f32).astype(bf16), count.astype(bf16)).astype(bf16)

    loads[1].wait()
    loads[2].wait()
    for c in range(ncomp):
        edges[0, c] = velx[c, 1:na + 1, 0, :]
        edges[1, c] = velx[c, 1:na + 1, nt - 1, :]
    edges[0, ncomp] = viscx[1:na + 1, 0, :]
    edges[1, ncomp] = viscx[1:na + 1, nt - 1, :]

    for c in zhalo + ahalo:
        c.start()

    big = jnp.floor((cell_col + 1.0) * (1.0 / 64.0))
    small = (cell_col + 1.0) - 64.0 * big
    at_rank = lax.broadcasted_iota(jnp.int32, (pan, LANES), 1).astype(f32) == rank_col
    owner = lax.broadcasted_iota(jnp.int32, (n, pan), 0).astype(f32) == peer
    owner = owner.astype(f32).astype(bf16)
    cells = (64.0 * dot(owner, jnp.where(at_rank, big, 0.0).astype(bf16))
             + dot(owner, jnp.where(at_rank, small, 0.0).astype(bf16)) - 1.0)
    for d in range(n):
        scell[d] = cells[d:d + 1, :]

    def split_force(lo_row, hi_row):
        h, l = split(ext[:, lo_row:hi_row])
        exthi[:, lo_row:hi_row] = h
        extlo[:, lo_row:hi_row] = l

    loads[0].wait()
    split_force(HALO, HALO + pan)
    for c in fhalo:
        c.wait()
    split_force(0, HALO)
    split_force(HALO + pan, pan + 2 * HALO)

    def tiles_to(g, i):
        there = lax.rem(spot + i, half_n)
        side = half if g < n_ax else 1 - half
        device = (lax.rem(ax + g % n_ax, n_ax), side * half_n + there)
        src, k = g * half_n + there, g * half_n + i
        at = (g % n_ax) * half_n + spot
        tile_at, cell_at = (tiles, tcell) if g < n_ax else (got, gcell)
        return (remote(send.at[src], tile_at.at[at], tile_send.at[k], tile_recv.at[k], device),
                remote(scell.at[src], cell_at.at[at], cell_send.at[k], cell_recv.at[k], device))

    def each_tile(groups, act):
        for g in groups:
            def body(i, carry):
                for c in tiles_to(g, i):
                    act(c)
                return carry
            lax.fori_loop(1 if g == 0 else 0, half_n, body, 0)

    for part in range(2):
        r = slice(part * (slots // 2), (part + 1) * (slots // 2))
        for c in range(ncomp):
            tile = (dot(pick[r], exthi[c]) + dot(pick[r], extlo[c])) * scale[r]
            send[part * (n // 2):(part + 1) * (n // 2), :, c * nr:(c + 1) * nr] = (
                tile.reshape(n // 2, cap, nr))
        each_tile(range(part * n_ax, (part + 1) * n_ax), lambda c: c.start())
    own = [pltpu.make_async_copy(send.at[spot], tiles.at[spot], own_sem.at[0]),
           pltpu.make_async_copy(scell.at[spot], tcell.at[spot], own_sem.at[1])]
    for c in own:
        c.start()

    for c in ahalo + zhalo:
        c.wait()

    @pl.when(ax == 0)
    def _():
        velx[:, 0] = jnp.zeros((ncomp, nt, nr), f32)
        viscx[0] = jnp.zeros((nt, nr), f32)

    @pl.when(ax == n_ax - 1)
    def _():
        velx[:, na + 1] = jnp.zeros((ncomp, nt, nr), f32)
        viscx[na + 1] = jnp.zeros((nt, nr), f32)

    row_id = lax.broadcasted_iota(jnp.int32, (nt, nr), 0)
    lane_id = lax.broadcasted_iota(jnp.int32, (nt, nr), 1)

    def neighbours(x, low, high):
        left = jnp.where(row_id == 0, low, pltpu.roll(x, 1, 0))
        right = jnp.where(row_id == nt - 1, high, pltpu.roll(x, nt - 1, 0))
        inner = jnp.where(lane_id == 0, 0.0, pltpu.roll(x, 1, 1))
        outer = jnp.where(lane_id == nr - 1, 0.0, pltpu.roll(x, nr - 1, 1))
        return left, right, inner, outer

    def plane(i, carry):
        mu = viscx[i + 1]
        sides = neighbours(mu, edge_in[0, ncomp, pl.ds(i, 1), :], edge_in[1, ncomp, pl.ds(i, 1), :])
        faces = [mu + s for s in (viscx[i], viscx[i + 2]) + sides]
        for c in range(ncomp):
            f = velx[c, i + 1]
            near = neighbours(f, edge_in[0, c, pl.ds(i, 1), :], edge_in[1, c, pl.ds(i, 1), :])
            near = (velx[c, i], velx[c, i + 2]) + near
            total = faces[0] * (near[0] - f)
            for w, g in zip(faces[1:], near[1:]):
                total = total + w * (g - f)
            acc[c, i] = f + (0.5 * step_size) * total
        return carry

    lax.fori_loop(0, na, plane, 0)

    for c in own:
        c.wait()
    each_tile(range(n_ax), lambda c: c.wait())
    h, l = split(tiles[...].reshape(-1, ncomp * nr))
    thi[...] = h
    tlo[...] = l
    crow = wide_row(tcell[...].reshape(-1, LANES), cap)
    blk = max(1, 256 // nt)

    def stored(j):
        return pltpu.make_async_copy(acc.at[:, pl.ds(j * blk, blk)],
                                     base.at[:, pl.ds(j * blk, blk)], out_sem.at[j])

    for j in range(na // blk):
        landing = landing_of(crow, j * blk * nt, blk * nt)
        for c in range(ncomp):
            cs = slice(c * nr, (c + 1) * nr)
            deposit = dot(landing, thi[:, cs]) + dot(landing, tlo[:, cs])
            acc[c, j * blk:(j + 1) * blk] += deposit.reshape(blk, nt, nr)
        stored(j).start()
    for j in range(na // blk):
        stored(j).wait()
    each_tile(range(n_ax, 2 * n_ax), lambda c: c.wait())


def exchange_packed(n_ax, n_az, cap, keep, extra, vel, visc, force, dest_h, cell_h, area_h, adj_h,
                    base, got, landing, flag,
                    dest_i, cell_i, area, adj_i,
                    velx, viscx, ext, exthi, extlo, send, scell, edges, edge_in, acc,
                    tiles, tcell, fcell, thi, tlo, pack, share, packed, smeta, rmeta, sorted_, near_at, relay,
                    load_sem, halo_send, halo_recv, tile_send, tile_recv,
                    cell_send, cell_recv, own_sem, out_sem,
                    pack_send, pack_recv, meta_send, meta_recv, hop_send, hop_recv, hop_own,
                    share_send, share_recv, pass_send):
    n, half_n = n_ax * n_az, n_az // 2
    depth, group_n = half_n // 2, 2 * n_ax
    ax, az = lax.axis_index("ax"), lax.axis_index("az")
    me = ax * n_az + az
    half, spot = az // half_n, lax.rem(az, half_n)
    zpos, core = spot // 2, lax.rem(az, 2)
    seat = ax * 2 + core
    ncomp, na, nt, nr = vel.shape
    pan = force.shape[1]
    near = (n // 2) * cap
    slots = near + depth * keep + extra
    both = keep + extra
    detour = n_ax == 4
    f32, bf16 = jnp.float32, jnp.bfloat16

    def place(linear):
        return (linear // n_az, lax.rem(linear, n_az))

    def remote(src, dst, ssem, rsem, device):
        return pltpu.make_async_remote_copy(
            src_ref=src, dst_ref=dst, send_sem=ssem, recv_sem=rsem,
            device_id=device, device_id_type=pl.DeviceIdType.MESH)

    barrier = pltpu.get_barrier_semaphore()

    def greet(k, carry):
        pl.semaphore_signal(barrier, inc=1, device_id=place(lax.rem(me + k, n)),
                            device_id_type=pl.DeviceIdType.MESH)
        return carry

    lax.fori_loop(1, n, greet, 0)
    small = [pltpu.make_async_copy(src, dst, load_sem.at[3 + k]) for k, (src, dst) in enumerate(
        [(dest_h, dest_i), (cell_h, cell_i), (adj_h, adj_i), (area_h, area)])]
    loads = [
        pltpu.make_async_copy(force, ext.at[:, pl.ds(HALO, pan)], load_sem.at[0]),
        pltpu.make_async_copy(vel, velx.at[:, pl.ds(1, na)], load_sem.at[1]),
        pltpu.make_async_copy(visc, viscx.at[pl.ds(1, na)], load_sem.at[2]),
    ]
    for c in small + loads:
        c.start()

    for c in small:
        c.wait()

    dest_row, cell_row = dest_i[...].astype(f32), cell_i[...].astype(f32)
    adj = (adj_i[...] - (me * pan - HALO)).astype(f32)
    rows = jnp.concatenate([dest_row, cell_row, adj, dest_row, dest_row], axis=0)
    cols = rows.T
    dest_col, cell_col = cols[:, 0:1], cols[:, 1:2]
    same = dest_col == dest_row
    r0 = lax.broadcasted_iota(jnp.int32, (pan, pan), 0)
    r1 = lax.broadcasted_iota(jnp.int32, (pan, pan), 1)
    rank_row = jnp.sum((same & (r0 < r1)).astype(f32), axis=0, keepdims=True)
    rank_col = jnp.sum((same & (r1 < r0)).astype(f32), axis=1, keepdims=True)

    pl.semaphore_wait(barrier, n - 1)

    up, down = place(lax.rem(me + 1, n)), place(lax.rem(me + n - 1, n))
    ax_up, ax_down = lax.rem(ax + 1, n_ax), lax.rem(ax + n_ax - 1, n_ax)
    az_up, az_down = lax.rem(az + 1, n_az), lax.rem(az + n_az - 1, n_az)

    def halo(i, src, dst, device):
        return remote(src, dst, halo_send.at[i], halo_recv.at[i], device)

    fhalo = [
        halo(0, force.at[:, pl.ds(pan - HALO, HALO)], ext.at[:, pl.ds(0, HALO)], up),
        halo(1, force.at[:, pl.ds(0, HALO)], ext.at[:, pl.ds(HALO + pan, HALO)], down),
    ]
    top, bottom, below, above = na - 1, 0, 0, na + 1
    ahalo = [
        halo(2, vel.at[:, top], velx.at[:, below], (ax_up, az)),
        halo(3, vel.at[:, bottom], velx.at[:, above], (ax_down, az)),
        halo(4, visc.at[top], viscx.at[below], (ax_up, az)),
        halo(5, visc.at[bottom], viscx.at[above], (ax_down, az)),
    ]
    first, final = pl.ds(0, ncomp - 1), ncomp - 1

    def halves(src, dst, to, via):
        i = 2 if dst == below else 3
        return [halo(i, vel.at[first, src], velx.at[first, dst], (to, az)),
                halo(8, vel.at[final, src], relay.at[0], (via, az)),
                halo(9, visc.at[src], relay.at[1], (via, az))]

    def passed(dst, to):
        return [halo(10, relay.at[0], velx.at[final, dst], (to, az)),
                halo(11, relay.at[1], viscx.at[dst], (to, az))]

    even = lax.rem(ax, 2) == 0

    def start_ahalo():
        if not detour:
            for c in ahalo:
                c.start()
            return

        @pl.when(even)
        def _():
            ahalo[0].start()
            ahalo[2].start()

        @pl.when(jnp.logical_not(even))
        def _():
            ahalo[1].start()
            ahalo[3].start()

        @pl.when(ax == 1)
        def _():
            for c in halves(top, below, 2, 3):
                c.start()

        @pl.when(ax == 2)
        def _():
            for c in halves(bottom, above, 1, 0):
                c.start()

    def pass_on():
        if not detour:
            return

        @pl.when(ax == 3)
        def _():
            for c in halves(top, below, 2, 3)[1:]:
                c.wait_recv()
            for c in passed(below, 2):
                c.start()

        @pl.when(ax == 0)
        def _():
            for c in halves(bottom, above, 1, 0)[1:]:
                c.wait_recv()
            for c in passed(above, 1):
                c.start()

    def wait_ahalo():
        if not detour:
            for c in ahalo:
                c.wait()
            return

        @pl.when(even)
        def _():
            for c in (ahalo[0], ahalo[2]):
                c.wait_send()
            for c in (ahalo[1], ahalo[3]):
                c.wait_recv()

        @pl.when(jnp.logical_not(even))
        def _():
            for c in (ahalo[1], ahalo[3]):
                c.wait_send()
            for c in (ahalo[0], ahalo[2]):
                c.wait_recv()

        @pl.when(ax == 1)
        def _():
            for c in halves(top, below, 2, 3):
                c.wait_send()
            halves(bottom, above, 1, 0)[0].wait_recv()
            for c in passed(above, 1):
                c.wait_recv()

        @pl.when(ax == 2)
        def _():
            for c in halves(bottom, above, 1, 0):
                c.wait_send()
            halves(top, below, 2, 3)[0].wait_recv()
            for c in passed(below, 2):
                c.wait_recv()

        @pl.when(ax == 3)
        def _():
            for c in passed(below, 2):
                c.wait_send()

        @pl.when(ax == 0)
        def _():
            for c in passed(above, 1):
                c.wait_send()

    zhalo = [
        halo(6, edges.at[1], edge_in.at[0], (ax, az_up)),
        halo(7, edges.at[0], edge_in.at[1], (ax, az_down)),
    ]
    @pl.when(me < n - 1)
    def _():
        fhalo[0].start()

    @pl.when(me > 0)
    def _():
        fhalo[1].start()

    start_ahalo()
    def layer_of(dest):
        inner = dest - n_az * jnp.floor(dest * (1.0 / n_az))
        return jnp.floor(inner * 0.5)

    dax = jnp.floor(dest_row * (1.0 / n_az))
    daz = dest_row - n_az * dax
    dhalf = jnp.floor(daz * (1.0 / half_n))
    layer_row, layer_col = layer_of(dest_row), layer_of(dest_col)
    pos_row = jnp.sum(((layer_col == layer_row) & (r0 < r1)).astype(f32), axis=0, keepdims=True)
    turn = dax - ax.astype(f32)
    turn = jnp.where(turn < 0.0, turn + n_ax, turn)
    far = dhalf != half.astype(f32)
    group = turn + jnp.where(far, float(n_ax), 0.0)
    peer = group * half_n + (daz - half_n * dhalf)
    dz = (layer_row - depth * dhalf) - zpos.astype(f32)
    dz = jnp.where(dz < 0.0, dz + depth, dz)
    pos_col = jnp.sum(((layer_col == layer_row) & (r1 < r0)).astype(f32), axis=1, keepdims=True)
    far_col = jnp.floor(layer_col * (1.0 / depth)) != half.astype(f32)
    over_col = far_col & (pos_col >= keep)
    order = jnp.sum((over_col & (r0 < r1)).astype(f32), axis=0, keepdims=True)
    over = far & (pos_row >= keep)
    spilled = over & (order >= extra)
    target = jnp.where(far, near + dz * keep + pos_row, peer * cap + rank_row)
    target = jnp.where(over, near + depth * keep + order, target)
    target = jnp.where(spilled, -1.0, target).astype(jnp.int32)
    spill = jnp.max(jnp.where(spilled, 1.0, 0.0), axis=1, keepdims=True)
    loads[1].wait()
    loads[2].wait()
    for c in range(ncomp):
        edges[0, c] = velx[c, 1:na + 1, 0, :]
        edges[1, c] = velx[c, 1:na + 1, nt - 1, :]
    edges[0, ncomp] = viscx[1:na + 1, 0, :]
    edges[1, ncomp] = viscx[1:na + 1, nt - 1, :]
    for c in zhalo:
        c.start()

    hits = lax.broadcasted_iota(jnp.int32, (slots, pan), 0) == target
    scale = jnp.sum(jnp.where(hits, coupling * area[...], 0.0), axis=1, keepdims=True)
    q = lax.broadcasted_iota(jnp.int32, (pan, pan + 2 * HALO), 1).astype(f32)
    p = lax.broadcasted_iota(jnp.int32, (pan, pan + 2 * HALO), 0).astype(f32)
    count = (q == p + HALO).astype(f32)
    for k in range(4):
        count = count + (q == cols[:, 2 + k:3 + k]).astype(f32)
    hits = hits.astype(f32).astype(bf16)
    pick = dot(hits, count.astype(bf16)).astype(bf16)
    slot = (dax * 2.0 + (daz - 2.0 * layer_row)) * cap + rank_row + 1.0
    sbig = jnp.floor(slot * (1.0 / 64.0))
    digits = jnp.concatenate([sbig, slot - 64.0 * sbig] * 4, axis=0)
    for j in range(depth):
        at = near + j * keep
        holds = jnp.concatenate([hits[at:at + keep], hits[near + depth * keep:]], axis=0)
        found = lax.dot_general(jnp.where(dz == j, digits, 0.0).astype(bf16), holds,
                                (((1,), (1,)), ((), ())), preferred_element_type=f32)
        smeta[j] = jnp.full(smeta.shape[1:], -1.0, f32)
        smeta[j, :, 0:both] = 64.0 * found[0:1] + found[1:2] - 1.0

    big = jnp.floor((cell_col + 1.0) * (1.0 / 64.0))
    small_digit = (cell_col + 1.0) - 64.0 * big
    at_rank = lax.broadcasted_iota(jnp.int32, (pan, LANES), 1).astype(f32) == rank_col
    owner = lax.broadcasted_iota(jnp.int32, (n, pan), 0).astype(f32) == peer
    owner = owner.astype(f32).astype(bf16)
    cells = (64.0 * dot(owner, jnp.where(at_rank, big, 0.0).astype(bf16))
             + dot(owner, jnp.where(at_rank, small_digit, 0.0).astype(bf16)) - 1.0)
    last = lax.broadcasted_iota(jnp.int32, (n, LANES), 1) == LANES - 1
    cells = jnp.where(last, spill, cells)
    for d in range(n):
        scell[d] = cells[d:d + 1, :]

    def cells_to(g, i):
        there = lax.rem(spot + i, half_n)
        side = half if g < n_ax else 1 - half
        device = (lax.rem(ax + g % n_ax, n_ax), side * half_n + there)
        src, k = g * half_n + there, g * half_n + i
        if g < n_ax:
            cell_at = tcell.at[g * half_n + spot]
        else:
            cell_at = fcell.at[lax.rem(there // 2 - zpos + depth, depth) * group_n + seat]
        return remote(scell.at[src], cell_at, cell_send.at[k], cell_recv.at[k], device)

    def each(copy, groups, act):
        for g in groups:
            def body(i, carry):
                act(copy(g, i))
                return carry
            lax.fori_loop(1 if g == 0 else 0, half_n, body, 0)

    def along(j):
        return (ax, ((1 - half) * depth + lax.rem(zpos + j, depth)) * 2 + core)

    metas = [remote(smeta.at[j], rmeta.at[j], meta_send.at[j], meta_recv.at[j], along(j))
             for j in range(depth)]
    for c in metas:
        c.start()
    each(cells_to, range(2 * n_ax), lambda c: c.start())

    def split_force(lo_row, hi_row):
        h, l = split(ext[:, lo_row:hi_row])
        exthi[:, lo_row:hi_row] = h
        extlo[:, lo_row:hi_row] = l

    loads[0].wait()
    split_force(HALO, HALO + pan)

    @pl.when(me < n - 1)
    def _():
        fhalo[0].wait_send()
        fhalo[1].wait_recv()

    @pl.when(me > 0)
    def _():
        fhalo[1].wait_send()
        fhalo[0].wait_recv()

    @pl.when(me == 0)
    def _():
        ext[:, 0:HALO] = jnp.zeros((ncomp, HALO, nr), f32)

    @pl.when(me == n - 1)
    def _():
        ext[:, HALO + pan:] = jnp.zeros((ncomp, HALO, nr), f32)

    split_force(0, HALO)
    split_force(HALO + pan, pan + 2 * HALO)

    def picked(c, lo_row, hi_row):
        r = slice(lo_row, hi_row)
        return (dot(pick[r], exthi[c]) + dot(pick[r], extlo[c])) * scale[r]

    def tiles_to(g, i):
        there = lax.rem(spot + i, half_n)
        device = (lax.rem(ax + g, n_ax), half * half_n + there)
        src, k = g * half_n + there, g * half_n + i
        return remote(send.at[src], tiles.at[g * half_n + spot], tile_send.at[k],
                      tile_recv.at[k], device)

    packs = [[remote(pack.at[c, j], packed.at[c, j, pl.ds(0, keep)], pack_send.at[c, j], pack_recv.at[c, j],
                     along(j)) for j in range(depth)] for c in range(ncomp)]

    def entry(side):
        return jnp.where(side == 1, 0, depth - 1)

    at_gate = lax.rem(entry(1 - half) - zpos + depth, depth)
    shares = [remote(share.at[c], packed.at[c, at_gate, pl.ds(keep, extra)], share_send.at[c],
                     share_recv.at[c, at_gate], along(at_gate)) for c in range(ncomp)]
    gate = zpos == entry(half)

    def spread(c, j, d):
        there = lax.rem(zpos + d, depth)
        k = (j + d) % depth
        return remote(packed.at[c, j, pl.ds(keep, extra)], packed.at[c, k, pl.ds(keep, extra)],
                      pass_send.at[c, j, d], share_recv.at[c, k],
                      (ax, (half * depth + there) * 2 + core))

    def shared_in(c, j):
        return remote(share.at[c], packed.at[c, j, pl.ds(keep, extra)], share_send.at[c],
                      share_recv.at[c, j], along(j))

    def spread_shares(c):
        @pl.when(gate)
        def _():
            for j in range(depth):
                shared_in(c, j).wait_recv()
                for d in range(1, depth):
                    spread(c, j, d).start()

    def start_packs():
        for c in range(ncomp):
            share[c] = picked(c, near + depth * keep, slots)
            shares[c].start()
        for c in range(ncomp):
            for j in range(depth):
                at = near + j * keep
                pack[c, j] = picked(c, at, at + keep)
                packs[c][j].start()

    for c in range(ncomp):
        send[:, :, c * nr:(c + 1) * nr] = picked(c, 0, near).reshape(n // 2, cap, nr)
    each(tiles_to, range(n_ax), lambda c: c.start())
    start_packs()
    own = [pltpu.make_async_copy(send.at[spot], tiles.at[spot], own_sem.at[0]),
           pltpu.make_async_copy(scell.at[spot], tcell.at[spot], own_sem.at[1])]
    for c in own:
        c.start()

    pass_on()
    for c in zhalo:
        c.wait()

    row_id = lax.broadcasted_iota(jnp.int32, (nt, nr), 0)
    lane_id = lax.broadcasted_iota(jnp.int32, (nt, nr), 1)

    def neighbours(x, low, high):
        left = jnp.where(row_id == 0, low, pltpu.roll(x, 1, 0))
        right = jnp.where(row_id == nt - 1, high, pltpu.roll(x, nt - 1, 0))
        inner = jnp.where(lane_id == 0, 0.0, pltpu.roll(x, 1, 1))
        outer = jnp.where(lane_id == nr - 1, 0.0, pltpu.roll(x, nr - 1, 1))
        return left, right, inner, outer

    def plane(i, carry):
        mu = viscx[i + 1]
        sides = neighbours(mu, edge_in[0, ncomp, pl.ds(i, 1), :], edge_in[1, ncomp, pl.ds(i, 1), :])
        faces = [mu + s for s in (viscx[i], viscx[i + 2]) + sides]
        for c in range(ncomp):
            f = velx[c, i + 1]
            sides_f = neighbours(f, edge_in[0, c, pl.ds(i, 1), :], edge_in[1, c, pl.ds(i, 1), :])
            sides_f = (velx[c, i], velx[c, i + 2]) + sides_f
            total = faces[0] * (sides_f[0] - f)
            for w, g in zip(faces[1:], sides_f[1:]):
                total = total + w * (g - f)
            acc[c, i] = f + (0.5 * step_size) * total
        return carry

    lax.fori_loop(1, na - 1, plane, 0)
    for c in range(ncomp):
        spread_shares(c)

    def hop(c, j, k):
        there = lax.rem(seat + k, group_n)
        device = (there // 2, (half * depth + zpos) * 2 + lax.rem(there, 2))
        return remote(sorted_.at[c, j * group_n + there], arrival(c, j),
                      hop_send.at[(c * depth + j) * group_n + k],
                      hop_recv.at[(c * depth + j) * group_n + k], device)

    def arrival(c, j):
        return got.at[c, j * group_n + seat]

    def each_hop(c, j, act):
        def body(k, carry):
            act(hop(c, j, k))
            return carry
        lax.fori_loop(1, group_n, body, 0)

    def hop_mine(c, j):
        return pltpu.make_async_copy(sorted_.at[c, j * group_n + seat], arrival(c, j),
                                     hop_own.at[c * depth + j])

    for c in metas:
        c.wait()
    sorter = [(rmeta[j, :, 0:both].astype(jnp.int32)
               == lax.broadcasted_iota(jnp.int32, (group_n * cap, both), 0)
               ).astype(f32).astype(bf16) for j in range(depth)]

    def forward(c):
        for j in range(depth):
            packs[c][j].wait_recv()

            @pl.when(jnp.logical_not(gate))
            def _():
                shared_in(c, j).wait_recv()

            h, l = split(packed[c, j])
            sorted_[c, j * group_n:(j + 1) * group_n] = (
                dot(sorter[j], h) + dot(sorter[j], l)).reshape(group_n, cap, nr)
            each_hop(c, j, lambda x: x.start())
            hop_mine(c, j).start()

    def landed(c):
        for j in range(depth):
            each_hop(c, j, lambda x: x.wait())
            hop_mine(c, j).wait()

    def add(c, where, h, l):
        for m in range(2):
            rows = slice(m * (na // 2) * nt, (m + 1) * (na // 2) * nt)
            total = dot(where[rows], h) + dot(where[rows], l)
            acc[c, m * (na // 2):(m + 1) * (na // 2)] += total.reshape(na // 2, nt, nr)

    def stored(c):
        return pltpu.make_async_copy(acc.at[c], base.at[c], out_sem.at[c])

    forward(0)
    forward(1)

    wait_ahalo()

    @pl.when(ax == 0)
    def _():
        velx[:, 0] = jnp.zeros((ncomp, nt, nr), f32)
        viscx[0] = jnp.zeros((nt, nr), f32)

    @pl.when(ax == n_ax - 1)
    def _():
        velx[:, na + 1] = jnp.zeros((ncomp, nt, nr), f32)
        viscx[na + 1] = jnp.zeros((nt, nr), f32)

    lax.fori_loop(0, 2, lambda i, carry: plane(i * (na - 1), carry), 0)

    for c in own:
        c.wait()
    each(tiles_to, range(n_ax), lambda c: c.wait())
    each(cells_to, range(n_ax), lambda c: c.wait())
    h, l = split(tiles[...].reshape(-1, ncomp * nr))
    thi[...] = h
    tlo[...] = l
    near_at[...] = landing_of(wide_row(tcell[...].reshape(-1, LANES), cap), 0, na * nt)
    for c in range(ncomp):
        add(c, near_at, thi[:, c * nr:(c + 1) * nr], tlo[:, c * nr:(c + 1) * nr])
        stored(c).start()

    for c in range(2, ncomp):
        forward(c)
    each(cells_to, range(n_ax, 2 * n_ax), lambda c: c.wait())
    landing[...] = landing_of(wide_row(fcell[...].reshape(-1, LANES), cap), 0, na * nt)
    said = jnp.maximum(tcell[...].reshape(-1, LANES), fcell[...].reshape(-1, LANES))
    said = jnp.where(last[0:n // 2], said, 0.0)
    flag[...] = jnp.broadcast_to(jnp.max(jnp.max(said, axis=0, keepdims=True), axis=1,
                                         keepdims=True), (1, LANES))
    for c in range(ncomp):
        landed(c)
        stored(c).wait()
        shares[c].wait_send()
        for j in range(depth):
            packs[c][j].wait_send()

        @pl.when(gate)
        def _():
            for j in range(depth):
                for d in range(1, depth):
                    spread(c, j, d).wait_send()


def settle(cap, base, got, gcell, out, hi, lo, crow):
    step = pl.program_id(0)
    ncomp, blk, nt, nr = out.shape

    @pl.when(step == 0)
    def _():
        crow[...] = wide_row(gcell[...].reshape(-1, LANES), cap)
        h, l = split(got[...])
        hi[...] = h
        lo[...] = l

    landing = landing_of(crow[...], step * (blk * nt), blk * nt)
    for c in range(ncomp):
        cs = slice(c * nr, (c + 1) * nr)
        deposit = dot(landing, hi[:, cs]) + dot(landing, lo[:, cs])
        out[c] = base[c, pl.ds(step * blk, blk)] + deposit.reshape(blk, nt, nr)


def settle_packed(base, got, landing, out, total, sem):
    ncomp, na, nt, nr = base.shape
    parts = 4
    blk = na // parts
    stores = []
    for c in range(ncomp):
        hi, lo = split(got[c])
        for m in range(parts):
            rows = slice(m * blk * nt, (m + 1) * blk * nt)
            deposit = dot(landing[rows], hi) + dot(landing[rows], lo)
            planes = slice(m * blk, (m + 1) * blk)
            total[c, planes] = base[c, planes] + deposit.reshape(blk, nt, nr)
            planes = pl.ds(m * blk, blk)
            stores.append(pltpu.make_async_copy(total.at[c, planes], out.at[c, planes],
                                                sem.at[c * parts + m]))
            stores[-1].start()
    for c in stores:
        c.wait()


def direct(n_ax, n_az, cap, *inputs):
    velocity, _, force = inputs[:3]
    n = n_ax * n_az
    ncomp, pan, nr = force.shape
    na, nt = velocity.shape[1:3]
    slots = n * cap
    late = n // 2
    soon = n - late
    f32, bf16 = jnp.float32, jnp.bfloat16
    any_ = pl.BlockSpec(memory_space=pl.ANY)
    hbm = pl.BlockSpec(memory_space=pltpu.HBM)
    vmem = pl.BlockSpec(memory_space=pltpu.VMEM)
    dma = pltpu.SemaphoreType.DMA
    i32 = jnp.int32
    base, got, gcell = pl.pallas_call(
        functools.partial(exchange, n_ax, n_az, cap),
        out_shape=(jax.ShapeDtypeStruct(velocity.shape, f32),
                   jax.ShapeDtypeStruct((late, cap, ncomp * nr), f32),
                   jax.ShapeDtypeStruct((late, 1, LANES), f32)),
        in_specs=[hbm] * 7,
        out_specs=(any_, any_, any_),
        scratch_shapes=[
            pltpu.VMEM((1, pan), i32), pltpu.VMEM((1, pan), i32),
            pltpu.VMEM((1, pan), f32), pltpu.VMEM((4, pan), i32),
            pltpu.VMEM((ncomp, na + 2, nt, nr), f32),
            pltpu.VMEM((na + 2, nt, nr), f32),
            pltpu.VMEM((ncomp, pan + 2 * HALO, nr), f32),
            pltpu.VMEM((ncomp, pan + 2 * HALO, nr), bf16),
            pltpu.VMEM((ncomp, pan + 2 * HALO, nr), bf16),
            pltpu.VMEM((n, cap, ncomp * nr), f32),
            pltpu.VMEM((n, 1, LANES), f32),
            pltpu.VMEM((2, ncomp + 1, na, nr), f32),
            pltpu.VMEM((2, ncomp + 1, na, nr), f32),
            pltpu.VMEM((ncomp, na, nt, nr), f32),
            pltpu.VMEM((soon, cap, ncomp * nr), f32),
            pltpu.VMEM((soon, 1, LANES), f32),
            pltpu.VMEM((soon * cap, ncomp * nr), bf16),
            pltpu.VMEM((soon * cap, ncomp * nr), bf16),
            dma((7,)), dma((8,)), dma((8,)), dma((n,)), dma((n,)), dma((n,)), dma((n,)),
            dma((2,)), dma((na,)),
        ],
        compiler_params=pltpu.CompilerParams(collective_id=1, has_side_effects=True,
                                             vmem_limit_bytes=40 << 20),
        name="exchange",
    )(*inputs)
    blk = max(1, 128 // nt)
    window = pl.BlockSpec((ncomp, blk, nt, nr), lambda s: (0, s, 0, 0))
    return pl.pallas_call(
        functools.partial(settle, cap),
        out_shape=jax.ShapeDtypeStruct(velocity.shape, f32),
        grid=(na // blk,),
        in_specs=[vmem,
                  pl.BlockSpec((late * cap, ncomp * nr), lambda s: (0, 0)),
                  pl.BlockSpec((late, 1, LANES), lambda s: (0, 0, 0))],
        out_specs=window,
        scratch_shapes=[pltpu.VMEM((late * cap, ncomp * nr), bf16),
                        pltpu.VMEM((late * cap, ncomp * nr), bf16),
                        pltpu.VMEM((1, late * cap), f32)],
        compiler_params=pltpu.CompilerParams(vmem_limit_bytes=24 << 20),
        name="settle",
    )(base, got.reshape(late * cap, ncomp * nr), gcell)


def on_device(n_ax, n_az, velocity, viscosity, force, area, adjacency, crossing, cell):
    n, depth, group_n = n_ax * n_az, n_az // 4, 2 * n_ax
    ncomp, pan, nr = force.shape
    na, nt = velocity.shape[1:3]
    most = max(2, 2 * pan // n)
    cap = -(-most // 8) * 8
    bound = min(pan, group_n * most)
    keep = -(-5 * bound // 128) * 16
    extra = -(-bound // 128) * 16
    meta_lanes = -(-(keep + extra) // LANES) * LANES
    half = n // 2
    f32, bf16, i32 = jnp.float32, jnp.bfloat16, jnp.int32
    any_ = pl.BlockSpec(memory_space=pl.ANY)
    hbm = pl.BlockSpec(memory_space=pltpu.HBM)
    vmem = pl.BlockSpec(memory_space=pltpu.VMEM)
    dma = pltpu.SemaphoreType.DMA
    inputs = (velocity, viscosity, force, crossing.reshape(1, pan), cell.reshape(1, pan),
              area.reshape(1, pan), adjacency.T)
    inputs = [pltpu.with_memory_space_constraint(x, pltpu.HBM) for x in inputs]
    base, got, landing, flag = pl.pallas_call(
        functools.partial(exchange_packed, n_ax, n_az, cap, keep, extra),
        out_shape=(jax.ShapeDtypeStruct(velocity.shape, f32),
                   jax.ShapeDtypeStruct((ncomp, half, cap, nr), f32),
                   jax.ShapeDtypeStruct((na * nt, half * cap), bf16),
                   jax.ShapeDtypeStruct((1, LANES), f32)),
        in_specs=[hbm] * 7,
        out_specs=(any_, any_, vmem, vmem),
        scratch_shapes=[
            pltpu.VMEM((1, pan), i32), pltpu.VMEM((1, pan), i32),
            pltpu.VMEM((1, pan), f32), pltpu.VMEM((4, pan), i32),
            pltpu.VMEM((ncomp, na + 2, nt, nr), f32),
            pltpu.VMEM((na + 2, nt, nr), f32),
            pltpu.VMEM((ncomp, pan + 2 * HALO, nr), f32),
            pltpu.VMEM((ncomp, pan + 2 * HALO, nr), bf16),
            pltpu.VMEM((ncomp, pan + 2 * HALO, nr), bf16),
            pltpu.VMEM((half, cap, ncomp * nr), f32),
            pltpu.VMEM((n, 1, LANES), f32),
            pltpu.VMEM((2, ncomp + 1, na, nr), f32),
            pltpu.VMEM((2, ncomp + 1, na, nr), f32),
            pltpu.VMEM((ncomp, na, nt, nr), f32),
            pltpu.VMEM((half, cap, ncomp * nr), f32),
            pltpu.VMEM((half, 1, LANES), f32),
            pltpu.VMEM((half, 1, LANES), f32),
            pltpu.VMEM((half * cap, ncomp * nr), bf16),
            pltpu.VMEM((half * cap, ncomp * nr), bf16),
            pltpu.VMEM((ncomp, depth, keep, nr), f32),
            pltpu.VMEM((ncomp, extra, nr), f32),
            pltpu.VMEM((ncomp, depth, keep + extra, nr), f32),
            pltpu.VMEM((depth, 1, meta_lanes), f32),
            pltpu.VMEM((depth, 1, meta_lanes), f32),
            pltpu.VMEM((ncomp, half, cap, nr), f32),
            pltpu.VMEM((na * nt, half * cap), bf16),
            pltpu.VMEM((2, nt, nr), f32),
            dma((7,)), dma((12,)), dma((12,)), dma((half,)), dma((half,)), dma((n,)), dma((n,)),
            dma((2,)), dma((na,)),
            dma((ncomp, depth)), dma((ncomp, depth)), dma((depth,)), dma((depth,)),
            dma((ncomp * half,)), dma((ncomp * half,)), dma((ncomp * depth,)),
            dma((ncomp,)), dma((ncomp, depth)), dma((ncomp, depth, depth)),
        ],
        compiler_params=pltpu.CompilerParams(collective_id=0, has_side_effects=True,
                                             vmem_limit_bytes=44 << 20),
        name="exchange_packed",
    )(*inputs)
    def finish(base, got, landing, *inputs):
        return pl.pallas_call(
            settle_packed,
            out_shape=jax.ShapeDtypeStruct(velocity.shape, f32),
            in_specs=[vmem, vmem, vmem],
            out_specs=hbm,
            scratch_shapes=[pltpu.VMEM((ncomp, na, nt, nr), f32), dma((4 * ncomp,))],
            compiler_params=pltpu.CompilerParams(vmem_limit_bytes=52 << 20),
            name="settle_packed",
        )(base, got.reshape(ncomp, half * cap, nr), landing)

    def again(base, got, landing, *inputs):
        return direct(n_ax, n_az, cap, *inputs)

    return lax.cond(flag[0, 0] > 0.5, again, finish, base, got, landing, *inputs)


def solution(mesh):
    n_ax, n_az = mesh.shape["ax"], mesh.shape["az"]
    in_specs = (
        P(None, "ax", "az", None),
        P("ax", "az", None),
        P(None, ("ax", "az"), None),
        P(("ax", "az")),
        P(("ax", "az"), None),
        P(("ax", "az"), None),
        P(("ax", "az")),
    )
    return jax.shard_map(
        functools.partial(on_device, n_ax, n_az), mesh=mesh, in_specs=in_specs,
        out_specs=P(None, "ax", "az", None), check_vma=False)
```
